512 devices in a mesh: seq: 64 (over y_lo, z, core), head: 8 (over x, y_hi).
Axes of the slice: x: 4, y: 8 (y_hi: 2, y_lo: 4; y = y_hi * 4 + y_lo), z: 8, core: 2. Of those that a mesh axis runs over, the one named last changes fastest.
Arguments:
- query_rows: bfloat16 [20480, 3072], P('seq', 'head'), may hold values from -6 to 6
- key_rows: bfloat16 [20480, 3072], P('seq', 'head'), may hold values from -6 to 6
- value_rows: bfloat16 [20480, 3072], P('seq', 'head'), may hold values from -6 to 6
- pattern: int32 [64, 6], P('seq'), may hold values 0 or 1
- owners: int32 [4], replicated, may hold values from 0 to 63, as said below
- out_weight: bfloat16 [3072, 3072], P('head'), may hold values from -0.15625 to 0.15625
Outputs:
- mixed: bfloat16 [20480, 3072], P('seq', 'head')
The draws below stay inside these ranges and needn't reach their ends.
Inputs may be any that keep to these rules, and one draw needn't show every extreme that they name: `owners`: distinct block indices; blocks 0 and 64 - 1 are always among them.
All inputs are finite; a program needn't handle non-finite values. No bound on the sum of `pattern` on one device may be relied on, other than what follows from the above.
Results may differ from the reference program's by a relative error of at most 0.02.
Values may be sent and summed in bfloat16 or wider, within the bound.
A program may use at most 64 MiB of HBM per device.

```python
import jax
import jax.numpy as jnp
from jax import lax

D = 3072
HEADS = 24
HD = 128
TOK_DEV = 320
REACH = 3
OWNERS = 4
REFS = 1024
REF_DEV = 256
TOKENS = 20480
N_SEQ = 64
N_HEAD = 8


def shared_pair(key):
    first = jax.random.fold_in(key, 11)
    second = jax.random.fold_in(key, 23)
    width = HEADS * HD
    queries = jnp.clip(jax.random.normal(first, (TOKENS, width), jnp.float32), -6.0, 6.0)
    keys_all = jnp.clip(jax.random.normal(second, (TOKENS, width), jnp.float32), -6.0, 6.0)
    return (queries, keys_all)


def draw_query_rows(key, part):
    return shared_pair(key)[0].astype(jnp.bfloat16)


def draw_key_rows(key, part):
    return shared_pair(key)[1].astype(jnp.bfloat16)


def draw_owners(key, part):
    inner = jax.random.permutation(jax.random.fold_in(key, 5), N_SEQ - 2) + 1
    picked = jnp.concatenate([jnp.array([0, N_SEQ - 1], dtype=jnp.int32), inner[:OWNERS - 2].astype(jnp.int32)])
    return jax.random.permutation(jax.random.fold_in(key, 7), picked).astype(jnp.int32)


def place_ends(result, rng, smallest, top_value):
    longest = result.shape.index(max(result.shape))
    spots = []
    for shift in (0, 1):
        where = [jax.random.randint(jax.random.fold_in(rng, axis), (), 0, length) for axis, length in enumerate(result.shape)]
        where[longest] = (where[longest] + shift) % result.shape[longest]
        spots.append(tuple(where))
    return result.at[spots[0]].set(smallest).at[spots[1]].set(top_value)


def with_spikes(result, key, source, target, parts, factor):
    def block_of(position):
        return (jnp.arange(result.shape[position]) // (result.shape[position] // parts)).reshape((-1,) + (1,) * (result.ndim - 1 - position))

    first = jax.random.permutation(key, parts)[block_of(target)]
    second = (block_of(target) + parts // 2) % parts
    return jnp.where((block_of(source) == first) | (block_of(source) == second), factor * result, result)


def levels(rng, extent, cuts, low, top_value):
    def one(axis_at, shards_of):
        draws = jax.random.uniform(jax.random.fold_in(jax.random.fold_in(rng, 6), axis_at), (shards_of,), jnp.float32, low / len(cuts), top_value / len(cuts))
        return jnp.repeat(jnp.exp(draws), extent[axis_at] // shards_of).reshape((-1,) + (1,) * (len(extent) - axis_at - 1))

    gain = one(*cuts[0])
    for cut in cuts[1:]:
        gain = gain * one(*cut)
    return gain


def centred(key, dims, scale, most, pieces=(), kind=jnp.bfloat16):
    result = scale * jax.random.normal(key, dims, jnp.float32)
    if pieces:
        result = result * levels(key, dims, pieces, -0.22, 0.18)
    return jnp.clip(result, -most, most).astype(kind)


def gaussian_with(key, shape, scale, limit, pieces, heavy, kind=jnp.bfloat16):
    result = scale * jax.random.normal(key, shape, jnp.float32)
    if pieces:
        result = result * levels(key, shape, pieces, -0.22, 0.18)
    return jnp.clip(with_spikes(result, jax.random.fold_in(key, 3), *heavy), -limit, limit).astype(kind)


def setup_inputs(seed: int = 0) -> dict:
    key_of = jax.random.split(jax.random.key(seed), 7)
    return {
        "query_rows": draw_query_rows(jax.random.fold_in(key_of[6], 71), 0),
        "key_rows": draw_key_rows(jax.random.fold_in(key_of[6], 71), 0),
        "value_rows": centred(key_of[2], (TOKENS, HEADS * HD), 1.0, 6.0, ((0, 64), (1, 8))),
        "pattern": place_ends((jax.random.randint(key_of[3], (N_SEQ, 2 * REACH), 0, 3) < 1).astype(jnp.int32), jax.random.fold_in(key_of[3], 1), 0, 1),
        "owners": draw_owners(jax.random.fold_in(key_of[6], 71), 0),
        "out_weight": gaussian_with(key_of[5], (HEADS * HD, D), (HEADS * HD) ** -0.5, 0.15625, ((0, 8),), (0, 1, 8, 2.0)),
    }


def column_of(offset):
    return offset + REACH if offset < 0 else offset + REACH - 1


def reference(query_rows, key_rows, value_rows, pattern, owners, out_weight):
    scale = HD ** -0.5
    ref_keys = jnp.concatenate([lax.dynamic_slice_in_dim(key_rows, (owners[member] * TOK_DEV).astype(jnp.int32), REF_DEV, 0) for member in range(OWNERS)], axis=0)
    ref_values = jnp.concatenate([lax.dynamic_slice_in_dim(value_rows, (owners[member] * TOK_DEV).astype(jnp.int32), REF_DEV, 0) for member in range(OWNERS)], axis=0)

    def one_block(block):
        block = block.astype(jnp.int32)
        queries = lax.dynamic_slice_in_dim(query_rows, block * TOK_DEV, TOK_DEV, 0)
        key_list = []
        value_list = []
        mask_list = []
        for offset in range(-REACH, REACH + 1):
            source = ((block + offset) % N_SEQ).astype(jnp.int32)
            key_list.append(lax.dynamic_slice_in_dim(key_rows, source * TOK_DEV, TOK_DEV, 0))
            value_list.append(lax.dynamic_slice_in_dim(value_rows, source * TOK_DEV, TOK_DEV, 0))
            if offset == 0:
                active = jnp.ones((), dtype=bool)
            else:
                active = pattern[block, column_of(offset)] != 0
            mask_list.append(jnp.broadcast_to(active, (TOK_DEV,)))
        key_list.append(ref_keys)
        value_list.append(ref_values)
        mask_list.append(jnp.ones((REFS,), dtype=bool))
        all_keys = jnp.concatenate(key_list, axis=0).astype(jnp.float32).reshape(-1, HEADS, HD)
        all_values = jnp.concatenate(value_list, axis=0).astype(jnp.float32).reshape(-1, HEADS, HD)
        key_mask = jnp.concatenate(mask_list, axis=0)
        query_three = queries.astype(jnp.float32).reshape(TOK_DEV, HEADS, HD)
        scores = jnp.einsum('qhd,khd->hqk', query_three, all_keys) * scale
        scores = jnp.where(key_mask[None, None, :], scores, -jnp.inf)
        peaks = jnp.max(scores, axis=-1, keepdims=True)
        weights = jnp.exp(scores - peaks)
        totals = jnp.sum(weights, axis=-1)
        rounded = weights.astype(jnp.bfloat16).astype(jnp.float32)
        summed = jnp.einsum('hqk,khd->hqd', rounded, all_values)
        attended = summed / totals[:, :, None]
        return jnp.transpose(attended, (1, 0, 2)).reshape(TOK_DEV, HEADS * HD).astype(jnp.bfloat16)

    attended = lax.map(one_block, jnp.arange(N_SEQ, dtype=jnp.int32))
    attended = attended.reshape(TOKENS, HEADS * HD)
    group_width = HEADS * HD // N_HEAD
    mixed = jnp.zeros((TOKENS, D), jnp.float32)
    for group in range(N_HEAD):
        partial_value = jnp.dot(attended[:, group * group_width:(group + 1) * group_width], out_weight[group * group_width:(group + 1) * group_width], preferred_element_type=jnp.float32)
        mixed = mixed + partial_value.astype(jnp.bfloat16).astype(jnp.float32)
    return mixed.astype(jnp.bfloat16)
```

```python
import functools

import jax
import jax.numpy as jnp
from jax import lax
from jax.experimental import pallas as pl
from jax.experimental.pallas import tpu as pltpu
from jax.sharding import PartitionSpec as P

MESH = pl.DeviceIdType.MESH
HD = 128
LH = 3
TOK = 320
REF = 256
REACH = 3
NZ = 8
NY = 4
NX = 4
HK = 2 * LH
CH = 2
OWN = 4 * REF
HALO = OWN + TOK
KEYS = HALO + 2 * REACH * TOK
PAD = -(-KEYS // 256) * 256
NEG = -1e30
VMEM = pl.BlockSpec(memory_space=pltpu.VMEM)
SMEM = pl.BlockSpec(memory_space=pltpu.SMEM)
BF = jnp.bfloat16


def gather_kernel(
    owners_ref, k_ref, v_ref, kv, mine, stat, msend, mrecv, zp_s, zp_r, zs_s, zs_r,
    yp_s, yp_r, ys_s, ys_r, hs_sem, hr_sem, rs_sem, rr_sem,
):
    s = lax.axis_index("seq")
    n = 2 * NZ * NY
    core = lax.rem(s, 2)
    z = lax.rem(s // 2, NZ)
    y = s // (2 * NZ)
    step = 1 - 2 * core
    pz = jnp.where(core == 0, z, NZ - 1 - z)
    py = jnp.where(core == 0, y, NY - 1 - y)
    right = lax.rem(s + 2, n)
    left = lax.rem(s - 2 + n, n)
    partner = s + step
    extra = lax.rem(s - step + n, n)
    znext = lax.rem(s + 2 * step + n, n)
    zprev = lax.rem(s - 2 * step + n, n)
    ynext = lax.rem(s + 2 * NZ * step + n, n)
    yprev = lax.rem(s - 2 * NZ * step + n, n)

    barrier = pltpu.get_barrier_semaphore()
    for peer in (partner, right, left, extra, ynext, yprev):
        pl.semaphore_signal(barrier, inc=1, device_id={"seq": peer}, device_id_type=MESH)

    for h in range(LH):
        cols = slice(h * HD, (h + 1) * HD)
        kv[2 * h, OWN:HALO, :] = k_ref[:, cols]
        kv[2 * h + 1, OWN:HALO, :] = v_ref[:, cols]
    if PAD > KEYS:
        kv[:, KEYS:PAD, :] = jnp.zeros((HK, PAD - KEYS, HD), BF)

    low = jnp.int32(n)
    high = jnp.int32(-1)
    for i in range(4):
        o = owners_ref[i]
        low = jnp.minimum(low, jnp.where(o == 0, n, o))
        high = jnp.maximum(high, jnp.where(o == n - 1, -1, o))
    wanted = jnp.where(core == 0, low, high)
    given = jnp.where(core == 0, high, low)
    keep = jnp.where(wanted == s, 1.0, 0.0).astype(BF)
    give = jnp.where(given == s, 1.0, 0.0).astype(BF)
    fixed = jnp.where((pz == 0) & (py == 0), 1.0, 0.0).astype(BF)
    rows = REF // CH
    for hk in range(HK):
        for c in range(CH):
            block = kv[hk, OWN + c * rows : OWN + (c + 1) * rows, :]
            mine[hk * CH + c] = block * keep
            msend[hk * CH + c] = block * give
            stat[hk * CH + c] = block * fixed

    @pl.when(pz == 0)
    def _():
        zp_r[...] = jnp.zeros_like(zp_r)

    @pl.when(pz == NZ - 1)
    def _():
        zs_r[...] = jnp.zeros_like(zs_r)

    @pl.when(py == 0)
    def _():
        yp_r[...] = jnp.zeros_like(yp_r)

    @pl.when(py == NY - 1)
    def _():
        ys_r[...] = jnp.zeros_like(ys_r)

    pl.semaphore_wait(barrier, 6)
    chunks = HK * CH

    def ref_copy(kind, src, dst, k, peer):
        return pltpu.make_async_remote_copy(
            src_ref=src, dst_ref=dst, send_sem=rs_sem.at[kind, k], recv_sem=rr_sem.at[kind, k],
            device_id={"seq": peer}, device_id_type=MESH,
        )

    def m_copy(k):
        return ref_copy(0, msend.at[k], mrecv.at[k], k, partner)

    def zp_copy(k):
        return ref_copy(1, zp_s.at[k], zp_r.at[k], k, znext)

    def zs_copy(k):
        return ref_copy(2, zs_s.at[k], zs_r.at[k], k, zprev)

    def yp_copy(k):
        return ref_copy(3, yp_s.at[k], yp_r.at[k], k, ynext)

    def ys_copy(k):
        return ref_copy(4, ys_s.at[k], ys_r.at[k], k, yprev)

    def ref_rows(k, slot):
        return kv.at[k // CH, pl.ds(pl.multiple_of(slot * REF + lax.rem(k, CH) * rows, rows), rows)]

    def fx_copy(k):
        place = ref_rows(k, core)
        return ref_copy(5, place, place, k, partner)

    def fs_copy(k):
        place = ref_rows(k, 2 + core)
        return ref_copy(6, place, place, k, partner)

    def fx_wait(k):
        place = ref_rows(k, 1 - core)
        ref_copy(5, place, place, k, partner).wait_recv()

    def fs_wait(k):
        place = ref_rows(k, 3 - core)
        ref_copy(6, place, place, k, partner).wait_recv()

    def halo_rows(hk, col):
        return kv.at[hk, pl.ds(pl.multiple_of(HALO + col * TOK, 16), TOK)]

    def halo_copy(kind, src, hk, col, peer):
        return pltpu.make_async_remote_copy(
            src_ref=src, dst_ref=halo_rows(hk, col), send_sem=hs_sem.at[kind, hk],
            recv_sem=hr_sem.at[col, hk], device_id={"seq": peer}, device_id_type=MESH,
        )

    def own_rows(hk):
        return kv.at[hk, OWN:HALO]

    def halo_sends(hk):
        return (
            halo_copy(0, own_rows(hk), hk, 1, right),
            halo_copy(1, own_rows(hk), hk, 4, left),
            halo_copy(2, own_rows(hk), hk, 2 + core, partner),
        )

    def forward_behind(hk):
        return halo_copy(3, halo_rows(hk, 1), hk, 2 * core, partner)

    def forward_ahead(hk):
        return halo_copy(4, halo_rows(hk, 4), hk, 3 + 2 * core, partner)

    def forward_far(hk):
        return halo_copy(5, halo_rows(hk, 4 - 3 * core), hk, 5 - 5 * core, extra)

    def halo_wait(hk, col):
        halo_copy(0, own_rows(hk), hk, col, right).wait_recv()

    def start_m(k, carry):
        m_copy(k).start()
        return carry

    lax.fori_loop(0, chunks, start_m, 0)

    def when_in(k, bound, body):
        @pl.when((k >= 0) & (k < bound))
        def _():
            body(k)

    def zs_step(k):
        @pl.when(pz < NZ - 1)
        def _():
            zs_copy(k).wait_recv()

        @pl.when(pz > 0)
        def _():
            zs_s[k] = zs_r[k] + mine[k]
            zs_copy(k).start()

    def z_total(k):
        mine[k] = mine[k] + zp_r[k, 0] + zs_r[k]
        stat[k] = stat[k] + zp_r[k, 1]

    def yp_step(k):
        @pl.when(py > 0)
        def _():
            yp_copy(k).wait_recv()

        @pl.when(py < NY - 1)
        def _():
            yp_s[k, 0] = yp_r[k, 0] + mine[k]
            yp_s[k, 1] = yp_r[k, 1] + stat[k]
            yp_copy(k).start()

    def ys_step(k):
        @pl.when(py < NY - 1)
        def _():
            ys_copy(k).wait_recv()

        @pl.when(py > 0)
        def _():
            ys_s[k] = ys_r[k] + mine[k]
            ys_copy(k).start()

    def last_step(k):
        ref_rows(k, core)[...] = mine[k] + yp_r[k, 0] + ys_r[k]
        ref_rows(k, 2 + core)[...] = stat[k] + yp_r[k, 1]
        fx_copy(k).start()
        fs_copy(k).start()

    def halo_start(hk):
        for copy in halo_sends(hk):
            copy.start()

    def halo_forward(hk):
        halo_wait(hk, 1)
        halo_wait(hk, 4)
        forward_behind(hk).start()
        forward_ahead(hk).start()
        forward_far(hk).start()

    lag = NZ - 1

    def tick(t, carry):
        when_in(t - pz, chunks, zp_step_guarded)
        when_in(t - (NZ - 1 - pz), chunks, zs_step_guarded)
        when_in(t - lag, chunks, z_total)
        when_in(t - lag - py, chunks, yp_step)
        when_in(t - lag - (NY - 1 - py), chunks, ys_step)
        when_in(t - lag - (NY - 1), chunks, last_step)
        when_in(jnp.where(lax.rem(t, 2) == 0, t // 2, -1), HK, halo_start)
        when_in(jnp.where(lax.rem(t, 2) == 0, t // 2 - 2, -1), HK, halo_forward)
        return carry

    def merged(k):
        m_copy(k).wait_recv()
        mine[k] = mine[k] + mrecv[k]

    primary_first = pz <= NZ - 1 - pz

    def zp_step_guarded(k):
        @pl.when(primary_first)
        def _():
            merged(k)

        @pl.when(pz > 0)
        def _():
            zp_copy(k).wait_recv()

        @pl.when(pz < NZ - 1)
        def _():
            zp_s[k, 0] = zp_r[k, 0] + mine[k]
            zp_s[k, 1] = zp_r[k, 1] + stat[k]
            zp_copy(k).start()

    def zs_step_guarded(k):
        @pl.when(jnp.logical_not(primary_first))
        def _():
            merged(k)

        zs_step(k)

    lax.fori_loop(0, chunks + lag + NY - 1, tick, 0)

    def finish_ref(k, carry):
        fx_wait(k)
        fs_wait(k)
        m_copy(k).wait_send()
        fx_copy(k).wait_send()
        fs_copy(k).wait_send()

        @pl.when(pz < NZ - 1)
        def _():
            zp_copy(k).wait_send()

        @pl.when(pz > 0)
        def _():
            zs_copy(k).wait_send()

        @pl.when(py < NY - 1)
        def _():
            yp_copy(k).wait_send()

        @pl.when(py > 0)
        def _():
            ys_copy(k).wait_send()

        return carry

    lax.fori_loop(0, chunks, finish_ref, 0)

    def finish(hk, carry):
        for col in (0, 2, 3, 5):
            halo_wait(hk, col)
        for copy in halo_sends(hk):
            copy.wait_send()
        forward_behind(hk).wait_send()
        forward_ahead(hk).wait_send()
        forward_far(hk).wait_send()
        return carry

    lax.fori_loop(0, HK, finish, 0)


def gather(owners, k, v):
    chunks = HK * CH
    rows = REF // CH
    dma = pltpu.SemaphoreType.DMA
    one = pltpu.VMEM((chunks, rows, HD), BF)
    two = pltpu.VMEM((chunks, 2, rows, HD), BF)
    return pl.pallas_call(
        gather_kernel,
        out_shape=jax.ShapeDtypeStruct((HK, PAD, HD), BF),
        in_specs=[SMEM, VMEM, VMEM],
        out_specs=VMEM,
        scratch_shapes=[
            one, one, one, one, two, two, one, one, two, two, one, one,
            dma((6, HK)), dma((6, HK)), dma((7, chunks)), dma((7, chunks)),
        ],
        compiler_params=pltpu.CompilerParams(
            collective_id=0, has_side_effects=True, vmem_limit_bytes=40 << 20
        ),
        name="gather_keys",
    )(owners, k, v)


def attend_kernel(pattern_ref, q_ref, kv, w_ref, out, scores, att):
    position = lax.broadcasted_iota(jnp.int32, (1, PAD), 1)
    bias = jnp.where(position >= KEYS, NEG, 0.0)
    for col in range(2 * REACH):
        low = HALO + col * TOK
        closed = jnp.where(pattern_ref[0, col] != 0, 0.0, NEG)
        bias = bias + jnp.where((position >= low) & (position < low + TOK), closed, 0.0)
    scale = HD ** -0.5
    for h in range(LH):
        q = q_ref[:, h * HD : (h + 1) * HD]
        peak = jnp.full((TOK, HD), NEG, jnp.float32)
        for t in range(PAD // 256):
            keys = kv[2 * h, t * 256 : (t + 1) * 256, :]
            sc = lax.dot_general(
                q, keys, (((1,), (1,)), ((), ())), preferred_element_type=jnp.float32
            )
            sc = sc * scale + bias[:, t * 256 : (t + 1) * 256]
            scores[:, t * 256 : (t + 1) * 256] = sc
            peak = jnp.maximum(peak, jnp.maximum(sc[:, :128], sc[:, 128:]))
        top = jnp.max(peak, axis=1, keepdims=True)
        total = jnp.zeros((TOK, HD), jnp.float32)
        acc = jnp.zeros((TOK, HD), jnp.float32)
        for t in range(PAD // 256):
            w = jnp.exp(scores[:, t * 256 : (t + 1) * 256] - top)
            total = total + (w[:, :128] + w[:, 128:])
            acc = acc + jnp.dot(
                w.astype(BF), kv[2 * h + 1, t * 256 : (t + 1) * 256, :],
                preferred_element_type=jnp.float32,
            )
        total = jnp.sum(total, axis=1, keepdims=True)
        att[:, h * HD : (h + 1) * HD] = (acc / total).astype(BF)
    width = LH * HD
    for b in range(2 * NX):
        out[b] = jnp.dot(
            att[...], w_ref[:, b * width : (b + 1) * width], preferred_element_type=jnp.float32
        ).astype(BF)


def attend(pattern, q, kv, w):
    return pl.pallas_call(
        attend_kernel,
        out_shape=jax.ShapeDtypeStruct((2 * NX, TOK, LH * HD), BF),
        in_specs=[SMEM, VMEM, VMEM, VMEM],
        out_specs=VMEM,
        scratch_shapes=[pltpu.VMEM((TOK, PAD), jnp.float32), pltpu.VMEM((TOK, LH * HD), BF)],
        compiler_params=pltpu.CompilerParams(vmem_limit_bytes=48 << 20),
        name="attend",
    )(pattern, q, kv, w)


def mix_kernel(p, out, r1p, r1m, t2p, t2m, r2p, r2m, ty, ry, s_sem, r_sem, y_sem):
    h = lax.axis_index("head")
    x = h // 2
    y = lax.rem(h, 2)
    xn = lax.rem(x + 1, NX)
    xp = lax.rem(x + NX - 1, NX)
    xo = lax.rem(x + 2, NX)
    nxt = xn * 2 + y
    prv = xp * 2 + y
    pair = x * 2 + 1 - y
    barrier = pltpu.get_barrier_semaphore()
    for peer in (nxt, prv, pair):
        pl.semaphore_signal(barrier, inc=1, device_id={"head": peer}, device_id_type=MESH)
    pl.semaphore_wait(barrier, 3)
    half = TOK // 2
    top, bottom = slice(0, half), slice(half, TOK)

    def copy(kind, i, src, dst, peer):
        return pltpu.make_async_remote_copy(
            src_ref=src, dst_ref=dst, send_sem=s_sem.at[kind, i], recv_sem=r_sem.at[kind, i],
            device_id={"head": peer}, device_id_type=MESH,
        )

    def cross(i):
        return pltpu.make_async_remote_copy(
            src_ref=ty, dst_ref=ry, send_sem=y_sem.at[0], recv_sem=y_sem.at[1],
            device_id={"head": pair}, device_id_type=MESH,
        )

    sides = (1 - y, y)
    stage1 = []
    direct = []
    for i, side in enumerate(sides):
        far = xo * 2 + side
        stage1.append((
            copy(0, i, p.at[far, top], r1p.at[i], nxt),
            copy(1, i, p.at[far, bottom], r1m.at[i], prv),
        ))
        direct.append((
            copy(2, i, p.at[xn * 2 + side, bottom], r2p.at[i, bottom], nxt),
            copy(3, i, p.at[xp * 2 + side, top], r2m.at[i, top], prv),
        ))
    for i in range(2):
        for c in stage1[i]:
            c.start()
        for c in direct[i]:
            c.start()
    stage2 = []
    for i, side in enumerate(sides):
        stage1[i][0].wait_recv()
        t2p[i] = p[xn * 2 + side, top] + r1p[i]
        a = copy(4, i, t2p.at[i], r2p.at[i, top], nxt)
        a.start()
        stage1[i][1].wait_recv()
        t2m[i] = p[xp * 2 + side, bottom] + r1m[i]
        b = copy(5, i, t2m.at[i], r2m.at[i, bottom], prv)
        b.start()
        stage2.append((a, b))
    for i, side in enumerate(sides):
        for c in direct[i] + stage2[i]:
            c.wait_recv()
        total = (
            p[x * 2 + side].astype(jnp.float32)
            + r2p[i].astype(jnp.float32)
            + r2m[i].astype(jnp.float32)
        )
        if i == 0:
            ty[...] = total.astype(BF)
            cross(0).start()
        else:
            cross(0).wait_recv()
            out[...] = (total + ry[...].astype(jnp.float32)).astype(BF)
    for i in range(2):
        for c in stage1[i] + direct[i] + stage2[i]:
            c.wait_send()
    cross(0).wait_send()


def mix(p):
    dma = pltpu.SemaphoreType.DMA
    width = LH * HD
    halfs = pltpu.VMEM((2, TOK // 2, width), BF)
    fulls = pltpu.VMEM((2, TOK, width), BF)
    one = pltpu.VMEM((TOK, width), BF)
    return pl.pallas_call(
        mix_kernel,
        out_shape=jax.ShapeDtypeStruct((TOK, width), BF),
        in_specs=[VMEM],
        out_specs=VMEM,
        scratch_shapes=[
            halfs, halfs, halfs, halfs, fulls, fulls, one, one, dma((6, 2)), dma((6, 2)), dma((2,)),
        ],
        compiler_params=pltpu.CompilerParams(
            collective_id=1, has_side_effects=True, vmem_limit_bytes=32 << 20
        ),
        name="mix_heads",
    )(p)


def body(query_rows, key_rows, value_rows, pattern, owners, out_weight):
    kv = gather(owners, key_rows, value_rows)
    return mix(attend(pattern, query_rows, kv, out_weight))


def solution(mesh):
    return jax.shard_map(
        body,
        mesh=mesh,
        in_specs=(
            P("seq", "head"),
            P("seq", "head"),
            P("seq", "head"),
            P("seq", None),
            P(),
            P("head", None),
        ),
        out_specs=P("seq", "head"),
        check_vma=False,
    )
```

```python
import functools

import jax
import jax.numpy as jnp
from jax import lax
from jax.experimental import pallas as pl
from jax.experimental.pallas import tpu as pltpu
from jax.sharding import PartitionSpec as P

MESH = pl.DeviceIdType.MESH
HD = 128
LH = 3
TOK = 320
REF = 256
REACH = 3
NZ = 8
NY = 4
NX = 4
HK = 2 * LH
PIECE = REF // NZ
OWN = 4 * REF
HALO = OWN + TOK
KEYS = HALO + 2 * REACH * TOK
PAD = -(-KEYS // 256) * 256
NEG = -1e30
VMEM = pl.BlockSpec(memory_space=pltpu.VMEM)
SMEM = pl.BlockSpec(memory_space=pltpu.SMEM)
BF = jnp.bfloat16


def gather_kernel(
    owners_ref, k_ref, v_ref, kv, mine, msend, mrecv, ps, pr, ss, sr, ysend, yr,
    hs_sem, hr_sem, m_sem, p_sem, s_sem, x_sem, y_sem, ys_sem, a_sem, b_sem, f_sem,
):
    s = lax.axis_index("seq")
    n = 2 * NZ * NY
    core = lax.rem(s, 2)
    z = lax.rem(s // 2, NZ)
    y = s // (2 * NZ)
    step = 1 - 2 * core
    pz = jnp.where(core == 0, z, NZ - 1 - z)
    py = jnp.where(core == 0, y, NY - 1 - y)
    right = lax.rem(s + 2, n)
    left = lax.rem(s - 2 + n, n)
    partner = s + step
    extra = lax.rem(s - step + n, n)

    def at(yy, zz):
        zz = lax.rem(zz + NZ, NZ)
        yy = lax.rem(yy + NY, NY)
        zz = jnp.where(core == 0, zz, NZ - 1 - zz)
        yy = jnp.where(core == 0, yy, NY - 1 - yy)
        return (yy * NZ + zz) * 2 + core

    ahead = at(py, pz + 1)
    behind = at(py, pz - 1)

    barrier = pltpu.get_barrier_semaphore()
    peers = [partner, right, left, extra]
    peers += [at(py, pz + d) for d in range(1, NZ)]
    peers += [at(py + d, pz) for d in range(1, NY)]
    for peer in peers:
        pl.semaphore_signal(barrier, inc=1, device_id={"seq": peer}, device_id_type=MESH)

    for h in range(LH):
        cols = slice(h * HD, (h + 1) * HD)
        kv[2 * h, OWN:HALO, :] = k_ref[:, cols]
        kv[2 * h + 1, OWN:HALO, :] = v_ref[:, cols]
    if PAD > KEYS:
        kv[:, KEYS:PAD, :] = jnp.zeros((HK, PAD - KEYS, HD), BF)

    low = jnp.int32(n)
    high = jnp.int32(-1)
    for i in range(4):
        o = owners_ref[i]
        low = jnp.minimum(low, jnp.where(o == 0, n, o))
        high = jnp.maximum(high, jnp.where(o == n - 1, -1, o))
    wanted = jnp.where(core == 0, low, high)
    given = jnp.where(core == 0, high, low)
    keep = jnp.where(wanted == s, 1.0, 0.0).astype(BF)
    give = jnp.where(given == s, 1.0, 0.0).astype(BF)
    for hk in range(HK):
        block = kv[hk, OWN : OWN + REF, :]
        mine[hk] = block * keep
        msend[hk] = block * give

    pl.semaphore_wait(barrier, len(peers))

    def remote(src, dst, send, recv, peer):
        return pltpu.make_async_remote_copy(
            src_ref=src, dst_ref=dst, send_sem=send, recv_sem=recv,
            device_id={"seq": peer}, device_id_type=MESH,
        )

    def planes(ref, g):
        return ref.at[2 * g : 2 * g + 2]

    def swap(g):
        return remote(planes(msend, g), planes(mrecv, g), m_sem.at[0, g], m_sem.at[1, g], partner)

    def p_copy(j, g):
        return remote(ps.at[j, g], pr.at[j, g], p_sem.at[0, j, g], p_sem.at[1, j, g], ahead)

    def s_copy(j, g):
        return remote(ss.at[j, g], sr.at[j, g], s_sem.at[0, j, g], s_sem.at[1, j, g], behind)

    base = core * 2 * REF

    def piece(g, q, first, count):
        start = base + lax.rem(q + NZ, NZ) * 2 * PIECE + first
        return kv.at[2 * g : 2 * g + 2, pl.ds(pl.multiple_of(start, PIECE), count)]

    def mine_rows(g, q):
        start = lax.rem(q + NZ, NZ) * PIECE
        return mine[2 * g : 2 * g + 2, pl.ds(pl.multiple_of(start, PIECE), PIECE), :]

    def fixed_copy(q, g):
        return remote(
            kv.at[2 * g : 2 * g + 2, OWN + q * PIECE : OWN + (q + 1) * PIECE],
            piece(g, q, PIECE, PIECE), x_sem.at[0, q, g], x_sem.at[1, 0, g], at(0, q),
        )

    def y_copy(d, g):
        return remote(planes(ysend, g), yr.at[d - 1, g], y_sem.at[0, d, g], y_sem.at[1, d, g], at(py + d, pz))

    def y_fixed(d, g):
        part = piece(g, pz, PIECE, PIECE)
        return remote(part, part, ys_sem.at[0, d, g], ys_sem.at[1, 0, g], at(py + d, pz))

    def around(j, g):
        part = piece(g, pz - j, 0, 2 * PIECE)
        return remote(part, part, a_sem.at[0, j, g], a_sem.at[1, j, g], ahead)

    def around_arrived(j, g):
        part = piece(g, pz - j - 1, 0, 2 * PIECE)
        remote(part, part, a_sem.at[0, j, g], a_sem.at[1, j, g], ahead).wait_recv()

    def back(j, g):
        part = piece(g, pz + j, 0, 2 * PIECE)
        return remote(part, part, b_sem.at[0, j, g], b_sem.at[1, j, g], behind)

    def back_arrived(j, g):
        part = piece(g, pz + j + 1, 0, 2 * PIECE)
        remote(part, part, b_sem.at[0, j, g], b_sem.at[1, j, g], behind).wait_recv()

    def share(g):
        part = kv.at[2 * g : 2 * g + 2, pl.ds(pl.multiple_of(base, PIECE), 2 * REF)]
        return remote(part, part, f_sem.at[0, g], f_sem.at[1, g], partner)

    def shared(g):
        part = kv.at[2 * g : 2 * g + 2, pl.ds(pl.multiple_of(2 * REF - base, PIECE), 2 * REF)]
        remote(part, part, f_sem.at[0, g], f_sem.at[1, g], partner).wait_recv()

    def halo_rows(g, col):
        return kv.at[2 * g : 2 * g + 2, pl.ds(pl.multiple_of(HALO + col * TOK, 16), TOK)]

    def halo_copy(kind, src, g, col, peer):
        return remote(src, halo_rows(g, col), hs_sem.at[kind, g], hr_sem.at[col, g], peer)

    def own_rows(g):
        return kv.at[2 * g : 2 * g + 2, OWN:HALO]

    def halo_sends(g):
        return (
            halo_copy(0, own_rows(g), g, 1, right),
            halo_copy(1, own_rows(g), g, 4, left),
            halo_copy(2, own_rows(g), g, 2 + core, partner),
        )

    def forwards(g):
        return (
            halo_copy(3, halo_rows(g, 1), g, 2 * core, partner),
            halo_copy(4, halo_rows(g, 4), g, 3 + 2 * core, partner),
            halo_copy(5, halo_rows(g, 4 - 3 * core), g, 5 - 5 * core, extra),
        )

    def halo_wait(g, col):
        halo_copy(0, own_rows(g), g, col, right).wait_recv()

    def halo_start(g):
        for copy in halo_sends(g):
            copy.start()

    def halo_forward(g):
        halo_wait(g, 1)
        halo_wait(g, 4)
        for copy in forwards(g):
            copy.start()

    source = (pz == 0) & (py == 0)
    heads = range(LH)
    for g in heads:
        swap(g).start()

    @pl.when(source)
    def _():
        for g in heads:
            for q in range(1, NZ):
                fixed_copy(q, g).start()
            part = kv[2 * g : 2 * g + 2, OWN : OWN + PIECE, :]
            piece(g, 0, PIECE, PIECE)[...] = part

    halo_start(0)
    far, near = NZ // 2, NZ // 2 - 1
    for j in range(far):
        for g in heads:
            if j == 0:
                swap(g).wait_recv()
                mine[2 * g : 2 * g + 2] = mine[2 * g : 2 * g + 2] + mrecv[2 * g : 2 * g + 2]
                ps[0, g] = mine_rows(g, pz + far)
                p_copy(0, g).start()
                if near > 0:
                    ss[0, g] = mine_rows(g, pz - near)
                    s_copy(0, g).start()
            else:
                p_copy(j - 1, g).wait_recv()
                ps[j, g] = mine_rows(g, pz + far - j) + pr[j - 1, g]
                p_copy(j, g).start()
                if j < near:
                    s_copy(j - 1, g).wait_recv()
                    ss[j, g] = mine_rows(g, pz - near + j) + sr[j - 1, g]
                    s_copy(j, g).start()
        if j == 1:
            halo_start(1)
        if j == 2:
            halo_start(2)
    for g in heads:
        total = mine_rows(g, pz)
        if near > 0:
            s_copy(near - 1, g).wait_recv()
            total = total + sr[near - 1, g]
        p_copy(far - 1, g).wait_recv()
        ysend[2 * g : 2 * g + 2] = total + pr[far - 1, g]
        for d in range(1, NY):
            y_copy(d, g).start()

        @pl.when(py == 0)
        def _():
            @pl.when(pz > 0)
            def _():
                part = piece(g, pz, PIECE, PIECE)
                remote(part, part, x_sem.at[0, 0, g], x_sem.at[1, 0, g], ahead).wait_recv()

            for d in range(1, NY):
                y_fixed(d, g).start()

    halo_forward(0)
    for g in heads:
        total = ysend[2 * g : 2 * g + 2]
        for d in range(1, NY):
            y_copy(d, g).wait_recv()
            total = total + yr[d - 1, g]
        piece(g, pz, 0, PIECE)[...] = total

        @pl.when(py > 0)
        def _():
            part = piece(g, pz, PIECE, PIECE)
            remote(part, part, ys_sem.at[0, 0, g], ys_sem.at[1, 0, g], ahead).wait_recv()

        around(0, g).start()
        if near > 0:
            back(0, g).start()
    for j in range(1, far):
        for g in heads:
            around_arrived(j - 1, g)
            around(j, g).start()
            if j < near:
                back_arrived(j - 1, g)
                back(j, g).start()
        if j < 3:
            halo_forward(j)
    if far < 3:
        for g in range(max(far, 1), 3):
            halo_forward(g)
    for g in heads:
        around_arrived(far - 1, g)
        if near > 0:
            back_arrived(near - 1, g)
        share(g).start()
    for g in heads:
        shared(g)
        for col in (0, 2, 3, 5):
            halo_wait(g, col)

    for g in heads:
        swap(g).wait_send()
        share(g).wait_send()
        for j in range(far):
            p_copy(j, g).wait_send()
            around(j, g).wait_send()
        for j in range(near):
            s_copy(j, g).wait_send()
            back(j, g).wait_send()
        for d in range(1, NY):
            y_copy(d, g).wait_send()
        for copy in halo_sends(g) + forwards(g):
            copy.wait_send()

        @pl.when(py == 0)
        def _():
            for d in range(1, NY):
                y_fixed(d, g).wait_send()

        @pl.when(source)
        def _():
            for q in range(1, NZ):
                fixed_copy(q, g).wait_send()


def gather(owners, k, v):
    dma = pltpu.SemaphoreType.DMA
    whole = pltpu.VMEM((HK, REF, HD), BF)
    hop = pltpu.VMEM((NZ // 2, LH, 2, PIECE, HD), BF)
    return pl.pallas_call(
        gather_kernel,
        out_shape=jax.ShapeDtypeStruct((HK, PAD, HD), BF),
        in_specs=[SMEM, VMEM, VMEM],
        out_specs=VMEM,
        scratch_shapes=[
            whole, whole, whole, hop, hop, hop, hop,
            pltpu.VMEM((HK, PIECE, HD), BF), pltpu.VMEM((NY - 1, LH, 2, PIECE, HD), BF),
            dma((6, LH)), dma((6, LH)), dma((2, LH)), dma((2, NZ // 2, LH)), dma((2, NZ // 2, LH)),
            dma((2, NZ, LH)), dma((2, NY, LH)), dma((2, NY, LH)),
            dma((2, NZ // 2, LH)), dma((2, NZ // 2, LH)), dma((2, LH)),
        ],
        compiler_params=pltpu.CompilerParams(
            collective_id=0, has_side_effects=True, vmem_limit_bytes=40 << 20
        ),
        name="gather_keys",
    )(owners, k, v)


def attend_kernel(pattern_ref, q_ref, kv, w_ref, out, scores, att):
    position = lax.broadcasted_iota(jnp.int32, (1, PAD), 1)
    bias = jnp.where(position >= KEYS, NEG, 0.0)
    for col in range(2 * REACH):
        low = HALO + col * TOK
        closed = jnp.where(pattern_ref[0, col] != 0, 0.0, NEG)
        bias = bias + jnp.where((position >= low) & (position < low + TOK), closed, 0.0)
    scale = HD ** -0.5
    for h in range(LH):
        q = q_ref[:, h * HD : (h + 1) * HD]
        peak = jnp.full((TOK, HD), NEG, jnp.float32)
        for t in range(PAD // 256):
            keys = kv[2 * h, t * 256 : (t + 1) * 256, :]
            sc = lax.dot_general(
                q, keys, (((1,), (1,)), ((), ())), preferred_element_type=jnp.float32
            )
            sc = sc * scale + bias[:, t * 256 : (t + 1) * 256]
            scores[:, t * 256 : (t + 1) * 256] = sc
            peak = jnp.maximum(peak, jnp.maximum(sc[:, :128], sc[:, 128:]))
        top = jnp.max(peak, axis=1, keepdims=True)
        total = jnp.zeros((TOK, HD), jnp.float32)
        acc = jnp.zeros((TOK, HD), jnp.float32)
        for t in range(PAD // 256):
            w = jnp.exp(scores[:, t * 256 : (t + 1) * 256] - top)
            total = total + (w[:, :128] + w[:, 128:])
            acc = acc + jnp.dot(
                w.astype(BF), kv[2 * h + 1, t * 256 : (t + 1) * 256, :],
                preferred_element_type=jnp.float32,
            )
        total = jnp.sum(total, axis=1, keepdims=True)
        att[:, h * HD : (h + 1) * HD] = (acc / total).astype(BF)
    width = LH * HD
    for b in range(2 * NX):
        out[b] = jnp.dot(
            att[...], w_ref[:, b * width : (b + 1) * width], preferred_element_type=jnp.float32
        ).astype(BF)


def attend(pattern, q, kv, w):
    return pl.pallas_call(
        attend_kernel,
        out_shape=jax.ShapeDtypeStruct((2 * NX, TOK, LH * HD), BF),
        in_specs=[SMEM, VMEM, VMEM, VMEM],
        out_specs=VMEM,
        scratch_shapes=[pltpu.VMEM((TOK, PAD), jnp.float32), pltpu.VMEM((TOK, LH * HD), BF)],
        compiler_params=pltpu.CompilerParams(vmem_limit_bytes=48 << 20),
        name="attend",
    )(pattern, q, kv, w)


def mix_kernel(p, out, r1p, r1m, t2p, t2m, r2p, r2m, ty, ry, s_sem, r_sem, y_sem):
    h = lax.axis_index("head")
    x = h // 2
    y = lax.rem(h, 2)
    xn = lax.rem(x + 1, NX)
    xp = lax.rem(x + NX - 1, NX)
    xo = lax.rem(x + 2, NX)
    nxt = xn * 2 + y
    prv = xp * 2 + y
    pair = x * 2 + 1 - y
    barrier = pltpu.get_barrier_semaphore()
    for peer in (nxt, prv, pair):
        pl.semaphore_signal(barrier, inc=1, device_id={"head": peer}, device_id_type=MESH)
    pl.semaphore_wait(barrier, 3)
    half = TOK // 2
    top, bottom = slice(0, half), slice(half, TOK)

    def copy(kind, i, src, dst, peer):
        return pltpu.make_async_remote_copy(
            src_ref=src, dst_ref=dst, send_sem=s_sem.at[kind, i], recv_sem=r_sem.at[kind, i],
            device_id={"head": peer}, device_id_type=MESH,
        )

    def cross(i):
        return pltpu.make_async_remote_copy(
            src_ref=ty, dst_ref=ry, send_sem=y_sem.at[0], recv_sem=y_sem.at[1],
            device_id={"head": pair}, device_id_type=MESH,
        )

    sides = (1 - y, y)
    stage1 = []
    direct = []
    for i, side in enumerate(sides):
        far = xo * 2 + side
        stage1.append((
            copy(0, i, p.at[far, top], r1p.at[i], nxt),
            copy(1, i, p.at[far, bottom], r1m.at[i], prv),
        ))
        direct.append((
            copy(2, i, p.at[xn * 2 + side, bottom], r2p.at[i, bottom], nxt),
            copy(3, i, p.at[xp * 2 + side, top], r2m.at[i, top], prv),
        ))
    for i in range(2):
        for c in stage1[i]:
            c.start()
        for c in direct[i]:
            c.start()
    stage2 = []
    for i, side in enumerate(sides):
        stage1[i][0].wait_recv()
        t2p[i] = p[xn * 2 + side, top] + r1p[i]
        a = copy(4, i, t2p.at[i], r2p.at[i, top], nxt)
        a.start()
        stage1[i][1].wait_recv()
        t2m[i] = p[xp * 2 + side, bottom] + r1m[i]
        b = copy(5, i, t2m.at[i], r2m.at[i, bottom], prv)
        b.start()
        stage2.append((a, b))
    for i, side in enumerate(sides):
        for c in direct[i] + stage2[i]:
            c.wait_recv()
        total = (
            p[x * 2 + side].astype(jnp.float32)
            + r2p[i].astype(jnp.float32)
            + r2m[i].astype(jnp.float32)
        )
        if i == 0:
            ty[...] = total.astype(BF)
            cross(0).start()
        else:
            cross(0).wait_recv()
            out[...] = (total + ry[...].astype(jnp.float32)).astype(BF)
    for i in range(2):
        for c in stage1[i] + direct[i] + stage2[i]:
            c.wait_send()
    cross(0).wait_send()


def mix(p):
    dma = pltpu.SemaphoreType.DMA
    width = LH * HD
    halfs = pltpu.VMEM((2, TOK // 2, width), BF)
    fulls = pltpu.VMEM((2, TOK, width), BF)
    one = pltpu.VMEM((TOK, width), BF)
    return pl.pallas_call(
        mix_kernel,
        out_shape=jax.ShapeDtypeStruct((TOK, width), BF),
        in_specs=[VMEM],
        out_specs=VMEM,
        scratch_shapes=[
            halfs, halfs, halfs, halfs, fulls, fulls, one, one, dma((6, 2)), dma((6, 2)), dma((2,)),
        ],
        compiler_params=pltpu.CompilerParams(
            collective_id=1, has_side_effects=True, vmem_limit_bytes=32 << 20
        ),
        name="mix_heads",
    )(p)


def body(query_rows, key_rows, value_rows, pattern, owners, out_weight):
    kv = gather(owners, key_rows, value_rows)
    return mix(attend(pattern, query_rows, kv, out_weight))


def solution(mesh):
    return jax.shard_map(
        body,
        mesh=mesh,
        in_specs=(
            P("seq", "head"),
            P("seq", "head"),
            P("seq", "head"),
            P("seq", None),
            P(),
            P("head", None),
        ),
        out_specs=P("seq", "head"),
        check_vma=False,
    )
```

```python
import functools

import jax
import jax.numpy as jnp
from jax import lax
from jax.experimental import pallas as pl
from jax.experimental.pallas import tpu as pltpu
from jax.sharding import PartitionSpec as P

MESH = pl.DeviceIdType.MESH
HD = 128
LH = 3
TOK = 320
REF = 256
REACH = 3
NZ = 8
NY = 4
NX = 4
HK = 2 * LH
PIECE = REF // NZ
OWN = 4 * REF
HALO = OWN + TOK
KEYS = HALO + 2 * REACH * TOK
PAD = -(-KEYS // 256) * 256
NEG = -1e30
TILE = 256
PARTS = 2
VMEM = pl.BlockSpec(memory_space=pltpu.VMEM)
SMEM = pl.BlockSpec(memory_space=pltpu.SMEM)
BF = jnp.bfloat16


def layer_kernel(
    owners_ref, pattern_ref, q_hbm, k_hbm, v_hbm, w_hbm, out,
    kv, qb, wb, mine, msend, mrecv, ps, pr, ss, sr, ysend, yr,
    scores, att, acc1, top1, total1, p, r1p, r1m, t2p, t2m, r2p, r2m, ty, ry,
    hs_sem, hr_sem, m_sem, p_sem, s_sem, x_sem, y_sem, ys_sem, a_sem, b_sem, f_sem,
    in_sem, w_sem, q_sem, mix_s, mix_r, c_sem,
):
    s = lax.axis_index("seq")
    head = lax.axis_index("head")
    x = head // 2
    side = lax.rem(head, 2)
    xn = lax.rem(x + 1, NX)
    xp = lax.rem(x + NX - 1, NX)
    xo = lax.rem(x + 2, NX)
    nxt = xn * 2 + side
    prv = xp * 2 + side
    pair = x * 2 + 1 - side
    width = LH * HD
    n = 2 * NZ * NY
    core = lax.rem(s, 2)
    z = lax.rem(s // 2, NZ)
    y = s // (2 * NZ)
    step = 1 - 2 * core
    pz = jnp.where(core == 0, z, NZ - 1 - z)
    py = jnp.where(core == 0, y, NY - 1 - y)
    right = lax.rem(s + 2, n)
    left = lax.rem(s - 2 + n, n)
    partner = s + step
    extra = lax.rem(s - step + n, n)

    def at(yy, zz):
        zz = lax.rem(zz + NZ, NZ)
        yy = lax.rem(yy + NY, NY)
        zz = jnp.where(core == 0, zz, NZ - 1 - zz)
        yy = jnp.where(core == 0, yy, NY - 1 - yy)
        return (yy * NZ + zz) * 2 + core

    ahead = at(py, pz + 1)
    behind = at(py, pz - 1)

    loads = []
    for h in range(LH):
        for i, ref in enumerate((k_hbm, v_hbm)):
            loads.append(pltpu.make_async_copy(
                ref.at[:, h * HD : (h + 1) * HD], kv.at[2 * h + i, OWN:HALO], in_sem.at[2 * h + i]
            ))
            loads[-1].start()

    barrier = pltpu.get_barrier_semaphore()
    peers = [partner, right, left, extra]
    peers += [at(py, pz + d) for d in range(1, NZ)]
    peers += [at(py + d, pz) for d in range(1, NY)]
    for peer in peers:
        pl.semaphore_signal(barrier, inc=1, device_id={"seq": peer}, device_id_type=MESH)
    for peer in (nxt, prv, pair):
        pl.semaphore_signal(barrier, inc=1, device_id={"head": peer}, device_id_type=MESH)

    query_load = pltpu.make_async_copy(q_hbm, qb, q_sem)
    weight_loads = [
        pltpu.make_async_copy(w_hbm.at[:, b * width : (b + 1) * width], wb.at[b], w_sem.at[b])
        for b in range(2 * NX)
    ]
    if PAD > KEYS:
        kv[:, KEYS:PAD, :] = jnp.zeros((HK, PAD - KEYS, HD), BF)

    low = jnp.int32(n)
    high = jnp.int32(-1)
    for i in range(4):
        o = owners_ref[i]
        low = jnp.minimum(low, jnp.where(o == 0, n, o))
        high = jnp.maximum(high, jnp.where(o == n - 1, -1, o))
    wanted = jnp.where(core == 0, low, high)
    given = jnp.where(core == 0, high, low)
    keep = jnp.where(wanted == s, 1.0, 0.0).astype(BF)
    give = jnp.where(given == s, 1.0, 0.0).astype(BF)
    for hk in range(HK):
        loads[hk].wait()
        block = kv[hk, OWN : OWN + REF, :]
        mine[hk] = block * keep
        msend[hk] = block * give

    pl.semaphore_wait(barrier, len(peers) + 3)

    def remote(src, dst, send, recv, peer):
        return pltpu.make_async_remote_copy(
            src_ref=src, dst_ref=dst, send_sem=send, recv_sem=recv,
            device_id={"seq": peer}, device_id_type=MESH,
        )

    def planes(ref, g):
        return ref.at[2 * g : 2 * g + 2]

    def swap(g):
        return remote(planes(msend, g), planes(mrecv, g), m_sem.at[0, g], m_sem.at[1, g], partner)

    def p_copy(j, g):
        return remote(ps.at[j, g], pr.at[j, g], p_sem.at[0, j, g], p_sem.at[1, j, g], ahead)

    def s_copy(j, g):
        return remote(ss.at[j, g], sr.at[j, g], s_sem.at[0, j, g], s_sem.at[1, j, g], behind)

    base = core * 2 * REF

    def piece(g, q, first, count):
        start = base + lax.rem(q + NZ, NZ) * 2 * PIECE + first
        return kv.at[2 * g : 2 * g + 2, pl.ds(pl.multiple_of(start, PIECE), count)]

    def mine_rows(g, q):
        start = lax.rem(q + NZ, NZ) * PIECE
        return mine[2 * g : 2 * g + 2, pl.ds(pl.multiple_of(start, PIECE), PIECE), :]

    def fixed_copy(q, g):
        return remote(
            kv.at[2 * g : 2 * g + 2, OWN + q * PIECE : OWN + (q + 1) * PIECE],
            piece(g, q, PIECE, PIECE), x_sem.at[0, q, g], x_sem.at[1, 0, g], at(0, q),
        )

    def y_copy(d, g):
        return remote(planes(ysend, g), yr.at[d - 1, g], y_sem.at[0, d, g], y_sem.at[1, d, g], at(py + d, pz))

    def y_fixed(d, g):
        part = piece(g, pz, PIECE, PIECE)
        return remote(part, part, ys_sem.at[0, d, g], ys_sem.at[1, 0, g], at(py + d, pz))

    def around(j, g):
        part = piece(g, pz - j, 0, 2 * PIECE)
        return remote(part, part, a_sem.at[0, j, g], a_sem.at[1, j, g], ahead)

    def around_arrived(j, g):
        part = piece(g, pz - j - 1, 0, 2 * PIECE)
        remote(part, part, a_sem.at[0, j, g], a_sem.at[1, j, g], ahead).wait_recv()

    def back(j, g):
        part = piece(g, pz + j, 0, 2 * PIECE)
        return remote(part, part, b_sem.at[0, j, g], b_sem.at[1, j, g], behind)

    def back_arrived(j, g):
        part = piece(g, pz + j + 1, 0, 2 * PIECE)
        remote(part, part, b_sem.at[0, j, g], b_sem.at[1, j, g], behind).wait_recv()

    def share(g):
        part = kv.at[2 * g : 2 * g + 2, pl.ds(pl.multiple_of(base, PIECE), 2 * REF)]
        return remote(part, part, f_sem.at[0, g], f_sem.at[1, g], partner)

    def shared(g):
        part = kv.at[2 * g : 2 * g + 2, pl.ds(pl.multiple_of(2 * REF - base, PIECE), 2 * REF)]
        remote(part, part, f_sem.at[0, g], f_sem.at[1, g], partner).wait_recv()

    def halo_rows(g, col):
        return kv.at[2 * g : 2 * g + 2, pl.ds(pl.multiple_of(HALO + col * TOK, 16), TOK)]

    def halo_copy(kind, src, g, col, peer):
        return remote(src, halo_rows(g, col), hs_sem.at[kind, g], hr_sem.at[col, g], peer)

    def own_rows(g):
        return kv.at[2 * g : 2 * g + 2, OWN:HALO]

    def halo_sends(g):
        return (
            halo_copy(0, own_rows(g), g, 1, right),
            halo_copy(1, own_rows(g), g, 4, left),
            halo_copy(2, own_rows(g), g, 2 + core, partner),
        )

    def forwards(g):
        return (
            halo_copy(3, halo_rows(g, 1), g, 2 * core, partner),
            halo_copy(4, halo_rows(g, 4), g, 3 + 2 * core, partner),
            halo_copy(5, halo_rows(g, 4 - 3 * core), g, 5 - 5 * core, extra),
        )

    def halo_wait(g, col):
        halo_copy(0, own_rows(g), g, col, right).wait_recv()

    def halo_start(g):
        for copy in halo_sends(g):
            copy.start()

    def halo_forward(g):
        halo_wait(g, 1)
        halo_wait(g, 4)
        for copy in forwards(g):
            copy.start()

    position = lax.broadcasted_iota(jnp.int32, (1, PAD - OWN), 1) + OWN
    bias = jnp.where(position >= KEYS, NEG, 0.0)
    for col in range(2 * REACH):
        edge = HALO + col * TOK
        closed = jnp.where(pattern_ref[0, col] != 0, 0.0, NEG)
        bias = bias + jnp.where((position >= edge) & (position < edge + TOK), closed, 0.0)
    scale = HD ** -0.5

    def segment(h, first, last):
        q = qb[:, h * HD : (h + 1) * HD]
        peak = jnp.full((TOK, HD), NEG, jnp.float32)
        tiles = range(first, last, TILE)
        for row in tiles:
            sc = lax.dot_general(
                q, kv[2 * h, row : row + TILE, :], (((1,), (1,)), ((), ())),
                preferred_element_type=jnp.float32,
            )
            sc = sc * scale
            if row >= OWN:
                sc = sc + bias[:, row - OWN : row - OWN + TILE]
            scores[:, row - first : row - first + TILE] = sc
            peak = jnp.maximum(peak, jnp.maximum(sc[:, :HD], sc[:, HD:]))
        top = jnp.max(peak, axis=1, keepdims=True)
        total = jnp.zeros((TOK, HD), jnp.float32)
        acc = jnp.zeros((TOK, HD), jnp.float32)
        for row in tiles:
            w = jnp.exp(scores[:, row - first : row - first + TILE] - top)
            total = total + (w[:, :HD] + w[:, HD:])
            acc = acc + jnp.dot(
                w.astype(BF), kv[2 * h + 1, row : row + TILE, :], preferred_element_type=jnp.float32
            )
        return top, jnp.sum(total, axis=1, keepdims=True), acc

    def near_part(h):
        for col in range(2 * REACH):
            if col not in (1, 4):
                halo_wait(h, col)
        top, total, acc = segment(h, OWN, PAD)
        top1[h] = top
        total1[h] = total
        acc1[h] = acc

    def far_part(h):
        top, total, acc = segment(h, 0, OWN)
        best = jnp.maximum(top, top1[h])
        new = jnp.exp(top - best)
        old = jnp.exp(top1[h] - best)
        whole = total * new + total1[h] * old
        att[:, h * HD : (h + 1) * HD] = ((acc * new + acc1[h] * old) / whole).astype(BF)

    source = (pz == 0) & (py == 0)
    heads = range(LH)
    for g in heads:
        swap(g).start()

    @pl.when(source)
    def _():
        for g in heads:
            for q in range(1, NZ):
                fixed_copy(q, g).start()
            part = kv[2 * g : 2 * g + 2, OWN : OWN + PIECE, :]
            piece(g, 0, PIECE, PIECE)[...] = part

    halo_start(0)
    query_load.start()
    for load in weight_loads:
        load.start()
    far, near = NZ // 2, NZ // 2 - 1
    for j in range(far):
        for g in heads:
            if j == 0:
                swap(g).wait_recv()
                mine[2 * g : 2 * g + 2] = mine[2 * g : 2 * g + 2] + mrecv[2 * g : 2 * g + 2]
                ps[0, g] = mine_rows(g, pz + far)
                p_copy(0, g).start()
                if near > 0:
                    ss[0, g] = mine_rows(g, pz - near)
                    s_copy(0, g).start()
            else:
                p_copy(j - 1, g).wait_recv()
                ps[j, g] = mine_rows(g, pz + far - j) + pr[j - 1, g]
                p_copy(j, g).start()
                if j < near:
                    s_copy(j - 1, g).wait_recv()
                    ss[j, g] = mine_rows(g, pz - near + j) + sr[j - 1, g]
                    s_copy(j, g).start()
        if j == 1:
            halo_start(1)
        if j == 2:
            halo_start(2)
            halo_forward(0)
        if j == 3:
            halo_forward(1)
    if far <= 2:
        halo_start(2)
        halo_forward(0)
    if far <= 3:
        halo_forward(1)
    for g in heads:
        total = mine_rows(g, pz)
        if near > 0:
            s_copy(near - 1, g).wait_recv()
            total = total + sr[near - 1, g]
        p_copy(far - 1, g).wait_recv()
        ysend[2 * g : 2 * g + 2] = total + pr[far - 1, g]
        for d in range(1, NY):
            y_copy(d, g).start()

        @pl.when(py == 0)
        def _():
            @pl.when(pz > 0)
            def _():
                part = piece(g, pz, PIECE, PIECE)
                remote(part, part, x_sem.at[0, 0, g], x_sem.at[1, 0, g], ahead).wait_recv()

            for d in range(1, NY):
                y_fixed(d, g).start()

    halo_forward(2)
    for g in heads:
        total = ysend[2 * g : 2 * g + 2]
        for d in range(1, NY):
            y_copy(d, g).wait_recv()
            total = total + yr[d - 1, g]
        piece(g, pz, 0, PIECE)[...] = total

        @pl.when(py > 0)
        def _():
            part = piece(g, pz, PIECE, PIECE)
            remote(part, part, ys_sem.at[0, 0, g], ys_sem.at[1, 0, g], ahead).wait_recv()

        around(0, g).start()
        if near > 0:
            back(0, g).start()
    query_load.wait()
    for j in range(1, far):
        for g in heads:
            around_arrived(j - 1, g)
            around(j, g).start()
            if j < near:
                back_arrived(j - 1, g)
                back(j, g).start()
        near_part(j - 1)
    for h in range(far - 1, LH):
        near_part(h)
    for g in heads:
        around_arrived(far - 1, g)
        if near > 0:
            back_arrived(near - 1, g)
        share(g).start()
    for g in heads:
        shared(g)
        far_part(g)

    for load in weight_loads:
        load.wait()

    def project(b):
        p[b] = jnp.dot(att[...], wb[b], preferred_element_type=jnp.float32).astype(BF)

    def head_copy(kind, i, src, dst, peer):
        return pltpu.make_async_remote_copy(
            src_ref=src, dst_ref=dst, send_sem=mix_s.at[kind, i], recv_sem=mix_r.at[kind, i],
            device_id={"head": peer}, device_id_type=MESH,
        )

    def cross(c):
        return pltpu.make_async_remote_copy(
            src_ref=ty.at[c], dst_ref=ry.at[c], send_sem=c_sem.at[0, c], recv_sem=c_sem.at[1, c],
            device_id={"head": pair}, device_id_type=MESH,
        )

    part = TOK // PARTS
    half = part // 2
    items = [(which, c) for which in (1 - side, side) for c in range(PARTS)]
    rows = [(slice(c * part, c * part + half), slice(c * part + half, (c + 1) * part)) for c in range(PARTS)]
    first, direct, second = [], [], []
    for i, (which, c) in enumerate(items):
        upper, lower = rows[c]
        first.append((
            head_copy(0, i, p.at[xo * 2 + which, upper], r1p.at[i], nxt),
            head_copy(1, i, p.at[xo * 2 + which, lower], r1m.at[i], prv),
        ))
        direct.append((
            head_copy(2, i, p.at[xn * 2 + which, lower], r2p.at[i, half:], nxt),
            head_copy(3, i, p.at[xp * 2 + which, upper], r2m.at[i, :half], prv),
        ))
        second.append((
            head_copy(4, i, t2p.at[i], r2p.at[i, :half], nxt),
            head_copy(5, i, t2m.at[i], r2m.at[i, half:], prv),
        ))

    def pass_on(i):
        which, c = items[i]
        upper, lower = rows[c]
        first[i][0].wait_recv()
        t2p[i] = p[xn * 2 + which, upper] + r1p[i]
        second[i][0].start()
        first[i][1].wait_recv()
        t2m[i] = p[xp * 2 + which, lower] + r1m[i]
        second[i][1].start()

    def collect(i):
        which, c = items[i]
        for copy in direct[i] + second[i]:
            copy.wait_recv()
        return (
            p[x * 2 + which, c * part : (c + 1) * part].astype(jnp.float32)
            + r2p[i].astype(jnp.float32)
            + r2m[i].astype(jnp.float32)
        )

    for phase in range(2):
        which = items[phase * PARTS][0]
        mineq = range(phase * PARTS, (phase + 1) * PARTS)
        project(xo * 2 + which)
        for i in mineq:
            for copy in first[i]:
                copy.start()
        project(xn * 2 + which)
        project(xp * 2 + which)
        for i in mineq:
            for copy in direct[i]:
                copy.start()
            pass_on(i)
        project(x * 2 + which)
    for c in range(PARTS):
        ty[c] = collect(c).astype(BF)
        cross(c).start()
    for c in range(PARTS):
        total = collect(PARTS + c)
        cross(c).wait_recv()
        out[c * part : (c + 1) * part, :] = (total + ry[c].astype(jnp.float32)).astype(BF)

    for i in range(2 * PARTS):
        for copy in first[i] + direct[i] + second[i]:
            copy.wait_send()
    for c in range(PARTS):
        cross(c).wait_send()

    for g in heads:
        swap(g).wait_send()
        share(g).wait_send()
        for j in range(far):
            p_copy(j, g).wait_send()
            around(j, g).wait_send()
        for j in range(near):
            s_copy(j, g).wait_send()
            back(j, g).wait_send()
        for d in range(1, NY):
            y_copy(d, g).wait_send()
        for copy in halo_sends(g) + forwards(g):
            copy.wait_send()

        @pl.when(py == 0)
        def _():
            for d in range(1, NY):
                y_fixed(d, g).wait_send()

        @pl.when(source)
        def _():
            for q in range(1, NZ):
                fixed_copy(q, g).wait_send()


def layer(owners, pattern, q, k, v, w):
    dma = pltpu.SemaphoreType.DMA
    width = LH * HD
    whole = pltpu.VMEM((HK, REF, HD), BF)
    hop = pltpu.VMEM((NZ // 2, LH, 2, PIECE, HD), BF)
    part = TOK // PARTS
    halves = pltpu.VMEM((2 * PARTS, part // 2, width), BF)
    fulls = pltpu.VMEM((2 * PARTS, part, width), BF)
    pairs = pltpu.VMEM((PARTS, part, width), BF)
    column = pltpu.VMEM((LH, TOK, 1), jnp.float32)
    hbm = pl.BlockSpec(memory_space=pl.ANY)
    return pl.pallas_call(
        layer_kernel,
        out_shape=jax.ShapeDtypeStruct((TOK, width), BF),
        in_specs=[SMEM, SMEM, hbm, hbm, hbm, hbm],
        out_specs=VMEM,
        scratch_shapes=[
            pltpu.VMEM((HK, PAD, HD), BF), pltpu.VMEM((TOK, width), BF),
            pltpu.VMEM((2 * NX, width, width), BF),
            whole, whole, whole, hop, hop, hop, hop,
            pltpu.VMEM((HK, PIECE, HD), BF), pltpu.VMEM((NY - 1, LH, 2, PIECE, HD), BF),
            pltpu.VMEM((TOK, PAD - OWN), jnp.float32), pltpu.VMEM((TOK, width), BF),
            pltpu.VMEM((LH, TOK, HD), jnp.float32), column, column,
            pltpu.VMEM((2 * NX, TOK, width), BF),
            halves, halves, halves, halves, fulls, fulls, pairs, pairs,
            dma((6, LH)), dma((6, LH)), dma((2, LH)), dma((2, NZ // 2, LH)), dma((2, NZ // 2, LH)),
            dma((2, NZ, LH)), dma((2, NY, LH)), dma((2, NY, LH)),
            dma((2, NZ // 2, LH)), dma((2, NZ // 2, LH)), dma((2, LH)),
            dma((HK,)), dma((2 * NX,)), dma, dma((6, 2 * PARTS)), dma((6, 2 * PARTS)), dma((2, PARTS)),
        ],
        compiler_params=pltpu.CompilerParams(
            collective_id=0, has_side_effects=True, vmem_limit_bytes=56 << 20
        ),
        name="layer",
    )(owners, pattern, q, k, v, w)


def body(query_rows, key_rows, value_rows, pattern, owners, out_weight):
    return layer(owners, pattern, query_rows, key_rows, value_rows, out_weight)


def solution(mesh):
    return jax.shard_map(
        body,
        mesh=mesh,
        in_specs=(
            P("seq", "head"),
            P("seq", "head"),
            P("seq", "head"),
            P("seq", None),
            P(),
            P("head", None),
        ),
        out_specs=P("seq", "head"),
        check_vma=False,
    )
```

```python
import functools

import jax
import jax.numpy as jnp
from jax import lax
from jax.experimental import pallas as pl
from jax.experimental.pallas import tpu as pltpu
from jax.sharding import PartitionSpec as P

MESH = pl.DeviceIdType.MESH
HD = 128
LH = 3
TOK = 320
REF = 256
REACH = 3
NZ = 8
NY = 4
NX = 4
HK = 2 * LH
PIECE = REF // NZ
OWN = 4 * REF
HALO = OWN + TOK
KEYS = HALO + 2 * REACH * TOK
PAD = -(-KEYS // 256) * 256
NEG = -1e30
TILE = 256
PARTS = 2
PACE = (
    (("own", 2), ("spread",)),
    (("own", 3),),
    (("own", 4), ("here",), ("fixed", 0)),
    (("own", 5), ("fixed", 1), ("on", 0)),
    (("fixed", 2), ("on", 1), ("on", 2)),
    (("fixed", 3), ("on", 3)),
    (("on", 4), ("near", 0)),
    (("on", 5), ("near", 1)),
    (("near", 2),),
    (),
)
VMEM = pl.BlockSpec(memory_space=pltpu.VMEM)
SMEM = pl.BlockSpec(memory_space=pltpu.SMEM)
BF = jnp.bfloat16


def layer_kernel(
    owners_ref, pattern_ref, q_hbm, k_hbm, v_hbm, w_hbm, out,
    kv, qb, wb, mine, msend, mrecv, ps, pr, ss, sr, ysend, yr,
    scores, att, acc1, top1, total1, p, r1p, r1m, t2p, t2m, r2p, r2m, ty, ry,
    hs_sem, hr_sem, m_sem, p_sem, s_sem, x_sem, y_sem, ys_sem, a_sem, b_sem, fa_sem, fb_sem, f_sem,
    in_sem, w_sem, q_sem, mix_s, mix_r, c_sem,
):
    s = lax.axis_index("seq")
    head = lax.axis_index("head")
    x = head // 2
    side = lax.rem(head, 2)
    xn = lax.rem(x + 1, NX)
    xp = lax.rem(x + NX - 1, NX)
    xo = lax.rem(x + 2, NX)
    nxt = xn * 2 + side
    prv = xp * 2 + side
    pair = x * 2 + 1 - side
    width = LH * HD
    n = 2 * NZ * NY
    core = lax.rem(s, 2)
    z = lax.rem(s // 2, NZ)
    y = s // (2 * NZ)
    step = 1 - 2 * core
    pz = jnp.where(core == 0, z, NZ - 1 - z)
    py = jnp.where(core == 0, y, NY - 1 - y)
    right = lax.rem(s + 2, n)
    left = lax.rem(s - 2 + n, n)
    partner = s + step
    extra = lax.rem(s - step + n, n)

    def at(yy, zz):
        zz = lax.rem(zz + NZ, NZ)
        yy = lax.rem(yy + NY, NY)
        zz = jnp.where(core == 0, zz, NZ - 1 - zz)
        yy = jnp.where(core == 0, yy, NY - 1 - yy)
        return (yy * NZ + zz) * 2 + core

    far, near = NZ // 2, NZ // 2 - 1
    ahead = at(py, pz + 1)
    behind = at(py, pz - 1)

    loads = []
    for h in range(LH):
        for i, ref in enumerate((k_hbm, v_hbm)):
            loads.append(pltpu.make_async_copy(
                ref.at[:, h * HD : (h + 1) * HD], kv.at[2 * h + i, OWN:HALO], in_sem.at[2 * h + i]
            ))
            loads[-1].start()

    barrier = pltpu.get_barrier_semaphore()
    peers = [partner, right, left, extra]
    peers += [at(py, pz + d) for d in range(1, NZ)]
    peers += [at(py + d, pz) for d in range(1, NY)]
    for peer in peers:
        pl.semaphore_signal(barrier, inc=1, device_id={"seq": peer}, device_id_type=MESH)
    for peer in (nxt, prv, pair):
        pl.semaphore_signal(barrier, inc=1, device_id={"head": peer}, device_id_type=MESH)

    query_load = pltpu.make_async_copy(q_hbm, qb, q_sem)
    weight_loads = [
        pltpu.make_async_copy(w_hbm.at[:, b * width : (b + 1) * width], wb.at[b], w_sem.at[b])
        for b in range(2 * NX)
    ]
    if PAD > KEYS:
        kv[:, KEYS:PAD, :] = jnp.zeros((HK, PAD - KEYS, HD), BF)

    low = jnp.int32(n)
    high = jnp.int32(-1)
    for i in range(4):
        o = owners_ref[i]
        low = jnp.minimum(low, jnp.where(o == 0, n, o))
        high = jnp.maximum(high, jnp.where(o == n - 1, -1, o))
    wanted = jnp.where(core == 0, low, high)
    given = jnp.where(core == 0, high, low)
    keep = jnp.where(wanted == s, 1.0, 0.0).astype(BF)
    give = jnp.where(given == s, 1.0, 0.0).astype(BF)
    for hk in range(HK):
        loads[hk].wait()
        block = kv[hk, OWN : OWN + REF, :]
        mine[hk] = block * keep
        msend[hk] = block * give

    pl.semaphore_wait(barrier, len(peers) + 3)

    def remote(src, dst, send, recv, peer):
        return pltpu.make_async_remote_copy(
            src_ref=src, dst_ref=dst, send_sem=send, recv_sem=recv,
            device_id={"seq": peer}, device_id_type=MESH,
        )

    def planes(ref, g):
        return ref.at[2 * g : 2 * g + 2]

    def swap(g):
        return remote(planes(msend, g), planes(mrecv, g), m_sem.at[0, g], m_sem.at[1, g], partner)

    def p_copy(j, g):
        return remote(ps.at[j, g], pr.at[j, g], p_sem.at[0, j, g], p_sem.at[1, j, g], ahead)

    def s_copy(j, g):
        return remote(ss.at[j, g], sr.at[j, g], s_sem.at[0, j, g], s_sem.at[1, j, g], behind)

    base = core * 2 * REF

    def piece(g, q, first, count):
        start = base + lax.rem(q + NZ, NZ) * 2 * PIECE + first
        return kv.at[2 * g : 2 * g + 2, pl.ds(pl.multiple_of(start, PIECE), count)]

    def mine_rows(g, q):
        start = lax.rem(q + NZ, NZ) * PIECE
        return mine[2 * g : 2 * g + 2, pl.ds(pl.multiple_of(start, PIECE), PIECE), :]

    def fixed_rows(q):
        start = base + lax.rem(q + NZ, NZ) * 2 * PIECE + PIECE
        return kv.at[:, pl.ds(pl.multiple_of(start, PIECE), PIECE)]

    def fixed_copy(q):
        return remote(
            kv.at[:, OWN + q * PIECE : OWN + (q + 1) * PIECE], fixed_rows(q),
            x_sem.at[0, q], x_sem.at[1, 0], at(0, q),
        )

    def y_copy(d, g):
        return remote(planes(ysend, g), yr.at[d - 1, g], y_sem.at[0, d, g], y_sem.at[1, d, g], at(py + d, pz))

    def y_fixed(d):
        return remote(fixed_rows(pz), fixed_rows(pz), ys_sem.at[0, d], ys_sem.at[1, 0], at(py + d, pz))

    def around(j, g):
        part = piece(g, pz - j, 0, PIECE)
        return remote(part, part, a_sem.at[0, j, g], a_sem.at[1, j, g], ahead)

    def around_arrived(j, g):
        part = piece(g, pz - j - 1, 0, PIECE)
        remote(part, part, a_sem.at[0, j, g], a_sem.at[1, j, g], ahead).wait_recv()

    def back(j, g):
        part = piece(g, pz + j, 0, PIECE)
        return remote(part, part, b_sem.at[0, j, g], b_sem.at[1, j, g], behind)

    def back_arrived(j, g):
        part = piece(g, pz + j + 1, 0, PIECE)
        remote(part, part, b_sem.at[0, j, g], b_sem.at[1, j, g], behind).wait_recv()

    def fixed_around(j):
        part = fixed_rows(pz - j)
        return remote(part, part, fa_sem.at[0, j], fa_sem.at[1, j], ahead)

    def fixed_back(j):
        part = fixed_rows(pz + j)
        return remote(part, part, fb_sem.at[0, j], fb_sem.at[1, j], behind)

    def fixed_start(j):
        if j > 0:
            part = fixed_rows(pz - j)
            remote(part, part, fa_sem.at[0, j - 1], fa_sem.at[1, j - 1], ahead).wait_recv()
        fixed_around(j).start()
        if j < near:
            if j > 0:
                part = fixed_rows(pz + j)
                remote(part, part, fb_sem.at[0, j - 1], fb_sem.at[1, j - 1], behind).wait_recv()
            fixed_back(j).start()

    def fixed_finish():
        part = fixed_rows(pz - far)
        remote(part, part, fa_sem.at[0, far - 1], fa_sem.at[1, far - 1], ahead).wait_recv()
        if near > 0:
            part = fixed_rows(pz + near)
            remote(part, part, fb_sem.at[0, near - 1], fb_sem.at[1, near - 1], behind).wait_recv()

    def fixed_spread():
        @pl.when(py == 0)
        def _():
            @pl.when(pz > 0)
            def _():
                part = fixed_rows(pz)
                remote(part, part, x_sem.at[0, 0], x_sem.at[1, 0], ahead).wait_recv()

            for d in range(1, NY):
                y_fixed(d).start()

    def fixed_here():
        @pl.when(py > 0)
        def _():
            part = fixed_rows(pz)
            remote(part, part, ys_sem.at[0, 0], ys_sem.at[1, 0], ahead).wait_recv()

    def share(g):
        part = kv.at[2 * g : 2 * g + 2, pl.ds(pl.multiple_of(base, PIECE), 2 * REF)]
        return remote(part, part, f_sem.at[0, g], f_sem.at[1, g], partner)

    def shared(g):
        part = kv.at[2 * g : 2 * g + 2, pl.ds(pl.multiple_of(2 * REF - base, PIECE), 2 * REF)]
        remote(part, part, f_sem.at[0, g], f_sem.at[1, g], partner).wait_recv()

    def halo_rows(hk, col):
        return kv.at[hk, pl.ds(pl.multiple_of(HALO + col * TOK, 16), TOK)]

    def halo_copy(kind, src, hk, col, peer):
        return remote(src, halo_rows(hk, col), hs_sem.at[kind, hk], hr_sem.at[col, hk], peer)

    def own_rows(hk):
        return kv.at[hk, OWN:HALO]

    def halo_sends(hk):
        return (
            halo_copy(0, own_rows(hk), hk, 1, right),
            halo_copy(1, own_rows(hk), hk, 4, left),
            halo_copy(2, own_rows(hk), hk, 2 + core, partner),
        )

    def forwards(hk):
        return (
            halo_copy(5, halo_rows(hk, 4 - 3 * core), hk, 5 - 5 * core, extra),
            halo_copy(3, halo_rows(hk, 1), hk, 2 * core, partner),
            halo_copy(4, halo_rows(hk, 4), hk, 3 + 2 * core, partner),
        )

    def halo_wait(hk, col):
        halo_copy(0, own_rows(hk), hk, col, right).wait_recv()

    def halo_start(hk):
        for copy in halo_sends(hk):
            copy.start()

    def halo_forward(hk):
        halo_wait(hk, 1)
        halo_wait(hk, 4)
        for copy in forwards(hk):
            copy.start()

    position = lax.broadcasted_iota(jnp.int32, (1, PAD - OWN), 1) + OWN
    bias = jnp.where(position >= KEYS, NEG, 0.0)
    for col in range(2 * REACH):
        edge = HALO + col * TOK
        closed = jnp.where(pattern_ref[0, col] != 0, 0.0, NEG)
        bias = bias + jnp.where((position >= edge) & (position < edge + TOK), closed, 0.0)
    scale = HD ** -0.5

    def segment(h, first, last):
        q = qb[:, h * HD : (h + 1) * HD]
        peak = jnp.full((TOK, HD), NEG, jnp.float32)
        tiles = range(first, last, TILE)
        for row in tiles:
            sc = lax.dot_general(
                q, kv[2 * h, row : row + TILE, :], (((1,), (1,)), ((), ())),
                preferred_element_type=jnp.float32,
            )
            sc = sc * scale
            if row >= OWN:
                sc = sc + bias[:, row - OWN : row - OWN + TILE]
            scores[:, row - first : row - first + TILE] = sc
            peak = jnp.maximum(peak, jnp.maximum(sc[:, :HD], sc[:, HD:]))
        top = jnp.max(peak, axis=1, keepdims=True)
        total = jnp.zeros((TOK, HD), jnp.float32)
        acc = jnp.zeros((TOK, HD), jnp.float32)
        for row in tiles:
            w = jnp.exp(scores[:, row - first : row - first + TILE] - top)
            total = total + (w[:, :HD] + w[:, HD:])
            acc = acc + jnp.dot(
                w.astype(BF), kv[2 * h + 1, row : row + TILE, :], preferred_element_type=jnp.float32
            )
        return top, jnp.sum(total, axis=1, keepdims=True), acc

    def near_part(h):
        for col in range(2 * REACH):
            if col not in (1, 4):
                halo_wait(2 * h, col)
                halo_wait(2 * h + 1, col)
        top, total, acc = segment(h, OWN, PAD)
        top1[h] = top
        total1[h] = total
        acc1[h] = acc

    def far_part(h):
        top, total, acc = segment(h, 0, OWN)
        best = jnp.maximum(top, top1[h])
        new = jnp.exp(top - best)
        old = jnp.exp(top1[h] - best)
        whole = total * new + total1[h] * old
        att[:, h * HD : (h + 1) * HD] = ((acc * new + acc1[h] * old) / whole).astype(BF)

    source = (pz == 0) & (py == 0)
    heads = range(LH)
    step_actions = {
        "own": halo_start, "on": halo_forward, "near": near_part, "spread": fixed_spread,
        "here": fixed_here, "fixed": fixed_start,
    }
    for g in heads:
        swap(g).start()

    @pl.when(source)
    def _():
        for q in range(1, NZ):
            fixed_copy(q).start()
        fixed_rows(0)[...] = kv[:, OWN : OWN + PIECE, :]

    halo_start(0)
    halo_start(1)
    query_load.start()
    for load in weight_loads:
        load.start()
    for j in range(far):
        for g in heads:
            if j == 0:
                swap(g).wait_recv()
                mine[2 * g : 2 * g + 2] = mine[2 * g : 2 * g + 2] + mrecv[2 * g : 2 * g + 2]
                ps[0, g] = mine_rows(g, pz + far)
                p_copy(0, g).start()
                if near > 0:
                    ss[0, g] = mine_rows(g, pz - near)
                    s_copy(0, g).start()
            else:
                p_copy(j - 1, g).wait_recv()
                ps[j, g] = mine_rows(g, pz + far - j) + pr[j - 1, g]
                p_copy(j, g).start()
                if j < near:
                    s_copy(j - 1, g).wait_recv()
                    ss[j, g] = mine_rows(g, pz - near + j) + sr[j - 1, g]
                    s_copy(j, g).start()
        for action in PACE[j]:
            step_actions[action[0]](*action[1:])
    for g in heads:
        total = mine_rows(g, pz)
        if near > 0:
            s_copy(near - 1, g).wait_recv()
            total = total + sr[near - 1, g]
        p_copy(far - 1, g).wait_recv()
        ysend[2 * g : 2 * g + 2] = total + pr[far - 1, g]
        for d in range(1, NY):
            y_copy(d, g).start()
    for action in PACE[far]:
        step_actions[action[0]](*action[1:])
    for g in heads:
        total = ysend[2 * g : 2 * g + 2]
        for d in range(1, NY):
            y_copy(d, g).wait_recv()
            total = total + yr[d - 1, g]
        piece(g, pz, 0, PIECE)[...] = total
        around(0, g).start()
        if near > 0:
            back(0, g).start()
    query_load.wait()
    for action in PACE[far + 1]:
        step_actions[action[0]](*action[1:])
    for j in range(1, far):
        for g in heads:
            around_arrived(j - 1, g)
            around(j, g).start()
            if j < near:
                back_arrived(j - 1, g)
                back(j, g).start()
        for action in PACE[far + 1 + j]:
            step_actions[action[0]](*action[1:])
    fixed_finish()
    for g in heads:
        around_arrived(far - 1, g)
        if near > 0:
            back_arrived(near - 1, g)
        share(g).start()
    for action in PACE[2 * far + 1]:
        step_actions[action[0]](*action[1:])
    for g in heads:
        shared(g)
        far_part(g)
    for load in weight_loads:
        load.wait()

    def project(b):
        p[b] = jnp.dot(att[...], wb[b], preferred_element_type=jnp.float32).astype(BF)

    def head_copy(kind, i, src, dst, peer):
        return pltpu.make_async_remote_copy(
            src_ref=src, dst_ref=dst, send_sem=mix_s.at[kind, i], recv_sem=mix_r.at[kind, i],
            device_id={"head": peer}, device_id_type=MESH,
        )

    def cross(c):
        return pltpu.make_async_remote_copy(
            src_ref=ty.at[c], dst_ref=ry.at[c], send_sem=c_sem.at[0, c], recv_sem=c_sem.at[1, c],
            device_id={"head": pair}, device_id_type=MESH,
        )

    part = TOK // PARTS
    half = part // 2
    items = [(which, c) for which in (1 - side, side) for c in range(PARTS)]
    rows = [(slice(c * part, c * part + half), slice(c * part + half, (c + 1) * part)) for c in range(PARTS)]
    first, direct, second = [], [], []
    for i, (which, c) in enumerate(items):
        upper, lower = rows[c]
        first.append((
            head_copy(0, i, p.at[xo * 2 + which, upper], r1p.at[i], nxt),
            head_copy(1, i, p.at[xo * 2 + which, lower], r1m.at[i], prv),
        ))
        direct.append((
            head_copy(2, i, p.at[xn * 2 + which, lower], r2p.at[i, half:], nxt),
            head_copy(3, i, p.at[xp * 2 + which, upper], r2m.at[i, :half], prv),
        ))
        second.append((
            head_copy(4, i, t2p.at[i], r2p.at[i, :half], nxt),
            head_copy(5, i, t2m.at[i], r2m.at[i, half:], prv),
        ))

    def pass_on(i):
        which, c = items[i]
        upper, lower = rows[c]
        first[i][0].wait_recv()
        t2p[i] = p[xn * 2 + which, upper] + r1p[i]
        second[i][0].start()
        first[i][1].wait_recv()
        t2m[i] = p[xp * 2 + which, lower] + r1m[i]
        second[i][1].start()

    def collect(i):
        which, c = items[i]
        for copy in direct[i] + second[i]:
            copy.wait_recv()
        return (
            p[x * 2 + which, c * part : (c + 1) * part].astype(jnp.float32)
            + r2p[i].astype(jnp.float32)
            + r2m[i].astype(jnp.float32)
        )

    for phase in range(2):
        which = items[phase * PARTS][0]
        mineq = range(phase * PARTS, (phase + 1) * PARTS)
        project(xo * 2 + which)
        for i in mineq:
            for copy in first[i]:
                copy.start()
        project(xn * 2 + which)
        project(xp * 2 + which)
        for i in mineq:
            for copy in direct[i]:
                copy.start()
            pass_on(i)
        project(x * 2 + which)
    for c in range(PARTS):
        ty[c] = collect(c).astype(BF)
        cross(c).start()
    for c in range(PARTS):
        total = collect(PARTS + c)
        cross(c).wait_recv()
        out[c * part : (c + 1) * part, :] = (total + ry[c].astype(jnp.float32)).astype(BF)

    for i in range(2 * PARTS):
        for copy in first[i] + direct[i] + second[i]:
            copy.wait_send()
    for c in range(PARTS):
        cross(c).wait_send()

    for g in heads:
        swap(g).wait_send()
        share(g).wait_send()
        for j in range(far):
            p_copy(j, g).wait_send()
            around(j, g).wait_send()
        for j in range(near):
            s_copy(j, g).wait_send()
            back(j, g).wait_send()
        for d in range(1, NY):
            y_copy(d, g).wait_send()
    for j in range(far):
        fixed_around(j).wait_send()
    for j in range(near):
        fixed_back(j).wait_send()
    for hk in range(HK):
        for copy in halo_sends(hk) + forwards(hk):
            copy.wait_send()

    @pl.when(py == 0)
    def _():
        for d in range(1, NY):
            y_fixed(d).wait_send()

    @pl.when(source)
    def _():
        for q in range(1, NZ):
            fixed_copy(q).wait_send()


def layer(owners, pattern, q, k, v, w):
    dma = pltpu.SemaphoreType.DMA
    width = LH * HD
    whole = pltpu.VMEM((HK, REF, HD), BF)
    hop = pltpu.VMEM((NZ // 2, LH, 2, PIECE, HD), BF)
    part = TOK // PARTS
    halves = pltpu.VMEM((2 * PARTS, part // 2, width), BF)
    fulls = pltpu.VMEM((2 * PARTS, part, width), BF)
    pairs = pltpu.VMEM((PARTS, part, width), BF)
    column = pltpu.VMEM((LH, TOK, 1), jnp.float32)
    hbm = pl.BlockSpec(memory_space=pl.ANY)
    return pl.pallas_call(
        layer_kernel,
        out_shape=jax.ShapeDtypeStruct((TOK, width), BF),
        in_specs=[SMEM, SMEM, hbm, hbm, hbm, hbm],
        out_specs=VMEM,
        scratch_shapes=[
            pltpu.VMEM((HK, PAD, HD), BF), pltpu.VMEM((TOK, width), BF),
            pltpu.VMEM((2 * NX, width, width), BF),
            whole, whole, whole, hop, hop, hop, hop,
            pltpu.VMEM((HK, PIECE, HD), BF), pltpu.VMEM((NY - 1, LH, 2, PIECE, HD), BF),
            pltpu.VMEM((TOK, PAD - OWN), jnp.float32), pltpu.VMEM((TOK, width), BF),
            pltpu.VMEM((LH, TOK, HD), jnp.float32), column, column,
            pltpu.VMEM((2 * NX, TOK, width), BF),
            halves, halves, halves, halves, fulls, fulls, pairs, pairs,
            dma((6, HK)), dma((6, HK)), dma((2, LH)), dma((2, NZ // 2, LH)), dma((2, NZ // 2, LH)),
            dma((2, NZ)), dma((2, NY, LH)), dma((2, NY)),
            dma((2, NZ // 2, LH)), dma((2, NZ // 2, LH)), dma((2, NZ // 2)), dma((2, NZ // 2)), dma((2, LH)),
            dma((HK,)), dma((2 * NX,)), dma, dma((6, 2 * PARTS)), dma((6, 2 * PARTS)), dma((2, PARTS)),
        ],
        compiler_params=pltpu.CompilerParams(
            collective_id=0, has_side_effects=True, vmem_limit_bytes=56 << 20
        ),
        name="layer",
    )(owners, pattern, q, k, v, w)


def body(query_rows, key_rows, value_rows, pattern, owners, out_weight):
    return layer(owners, pattern, query_rows, key_rows, value_rows, out_weight)


def solution(mesh):
    return jax.shard_map(
        body,
        mesh=mesh,
        in_specs=(
            P("seq", "head"),
            P("seq", "head"),
            P("seq", "head"),
            P("seq", None),
            P(),
            P("head", None),
        ),
        out_specs=P("seq", "head"),
        check_vma=False,
    )
```

```python
import functools

import jax
import jax.numpy as jnp
from jax import lax
from jax.experimental import pallas as pl
from jax.experimental.pallas import tpu as pltpu
from jax.sharding import PartitionSpec as P

MESH = pl.DeviceIdType.MESH
HD = 128
LH = 3
TOK = 320
REF = 256
REACH = 3
NZ = 8
NY = 4
NX = 4
HK = 2 * LH
PIECE = REF // NZ
OWN = 4 * REF
HALO = OWN + TOK
KEYS = HALO + 2 * REACH * TOK
PAD = -(-KEYS // 256) * 256
NEG = -1e30
TILE = 256
GROUPS = 1
PER = HK // GROUPS
PARTS = 2
PACE = (
    (("own", 2), ("spread",)),
    (("own", 3),),
    (("own", 4), ("here",), ("fixed", 0)),
    (("own", 5), ("fixed", 1), ("on", 0), ("on", 1)),
    (("fixed", 2), ("on", 2), ("on", 3), ("query",), ("near", 0)),
    (("fixed", 3), ("on", 4)),
    (("on", 5), ("near", 1)),
    (("near", 2),),
    (("fixed_part",),),
    (),
)
VMEM = pl.BlockSpec(memory_space=pltpu.VMEM)
SMEM = pl.BlockSpec(memory_space=pltpu.SMEM)
BF = jnp.bfloat16


def layer_kernel(
    owners_ref, pattern_ref, q_hbm, k_hbm, v_hbm, w_hbm, out,
    kv, qb, wb, mine, msend, mrecv, ps, pr, ss, sr, ysend, yr,
    scores, att, acc1, top1, total1, p, r1p, r1m, t2p, t2m, r2p, r2m, ty, ry,
    hs_sem, hr_sem, m_sem, p_sem, s_sem, x_sem, y_sem, ys_sem, a_sem, b_sem, fa_sem, fb_sem, f_sem,
    in_sem, w_sem, q_sem, mix_s, mix_r, c_sem,
):
    s = lax.axis_index("seq")
    head = lax.axis_index("head")
    x = head // 2
    side = lax.rem(head, 2)
    xn = lax.rem(x + 1, NX)
    xp = lax.rem(x + NX - 1, NX)
    xo = lax.rem(x + 2, NX)
    nxt = xn * 2 + side
    prv = xp * 2 + side
    pair = x * 2 + 1 - side
    width = LH * HD
    n = 2 * NZ * NY
    core = lax.rem(s, 2)
    z = lax.rem(s // 2, NZ)
    y = s // (2 * NZ)
    step = 1 - 2 * core
    pz = jnp.where(core == 0, z, NZ - 1 - z)
    py = jnp.where(core == 0, y, NY - 1 - y)
    right = lax.rem(s + 2, n)
    left = lax.rem(s - 2 + n, n)
    partner = s + step
    extra = lax.rem(s - step + n, n)

    def at(yy, zz):
        zz = lax.rem(zz + NZ, NZ)
        yy = lax.rem(yy + NY, NY)
        zz = jnp.where(core == 0, zz, NZ - 1 - zz)
        yy = jnp.where(core == 0, yy, NY - 1 - yy)
        return (yy * NZ + zz) * 2 + core

    far, near = NZ // 2, NZ // 2 - 1
    ahead = at(py, pz + 1)
    behind = at(py, pz - 1)

    loads = []
    for h in range(LH):
        for i, ref in enumerate((k_hbm, v_hbm)):
            loads.append(pltpu.make_async_copy(
                ref.at[:, h * HD : (h + 1) * HD], kv.at[2 * h + i, OWN:HALO], in_sem.at[2 * h + i]
            ))
            loads[-1].start()

    barrier = pltpu.get_barrier_semaphore()
    peers = [partner, right, left, extra]
    peers += [at(py, pz + d) for d in range(1, NZ)]
    peers += [at(py + d, pz) for d in range(1, NY)]
    for peer in peers:
        pl.semaphore_signal(barrier, inc=1, device_id={"seq": peer}, device_id_type=MESH)
    for peer in (nxt, prv, pair):
        pl.semaphore_signal(barrier, inc=1, device_id={"head": peer}, device_id_type=MESH)

    query_load = pltpu.make_async_copy(q_hbm, qb, q_sem)
    weight_loads = [
        pltpu.make_async_copy(w_hbm.at[:, b * width : (b + 1) * width], wb.at[b], w_sem.at[b])
        for b in range(2 * NX)
    ]
    if PAD > KEYS:
        kv[:, KEYS:PAD, :] = jnp.zeros((HK, PAD - KEYS, HD), BF)

    low = jnp.int32(n)
    high = jnp.int32(-1)
    for i in range(4):
        o = owners_ref[i]
        low = jnp.minimum(low, jnp.where(o == 0, n, o))
        high = jnp.maximum(high, jnp.where(o == n - 1, -1, o))
    wanted = jnp.where(core == 0, low, high)
    given = jnp.where(core == 0, high, low)
    keep = jnp.where(wanted == s, 1.0, 0.0).astype(BF)
    give = jnp.where(given == s, 1.0, 0.0).astype(BF)
    for hk in range(HK):
        loads[hk].wait()
        block = kv[hk, OWN : OWN + REF, :]
        mine[hk] = block * keep
        msend[hk] = block * give

    pl.semaphore_wait(barrier, len(peers) + 3)

    def remote(src, dst, send, recv, peer):
        return pltpu.make_async_remote_copy(
            src_ref=src, dst_ref=dst, send_sem=send, recv_sem=recv,
            device_id={"seq": peer}, device_id_type=MESH,
        )

    def planes(ref, g):
        return ref.at[PER * g : PER * g + PER]

    def swap(g):
        return remote(planes(msend, g), planes(mrecv, g), m_sem.at[0, g], m_sem.at[1, g], partner)

    def p_copy(j, g):
        return remote(ps.at[j, g], pr.at[j, g], p_sem.at[0, j, g], p_sem.at[1, j, g], ahead)

    def s_copy(j, g):
        return remote(ss.at[j, g], sr.at[j, g], s_sem.at[0, j, g], s_sem.at[1, j, g], behind)

    base = core * REF

    def piece(g, q):
        start = base + lax.rem(q + NZ, NZ) * PIECE
        return kv.at[PER * g : PER * g + PER, pl.ds(pl.multiple_of(start, PIECE), PIECE)]

    def mine_rows(g, q):
        start = lax.rem(q + NZ, NZ) * PIECE
        return mine[PER * g : PER * g + PER, pl.ds(pl.multiple_of(start, PIECE), PIECE), :]

    def fixed_rows(q):
        start = 2 * REF + base + lax.rem(q + NZ, NZ) * PIECE
        return kv.at[:, pl.ds(pl.multiple_of(start, PIECE), PIECE)]

    def fixed_copy(q):
        return remote(
            kv.at[:, OWN + q * PIECE : OWN + (q + 1) * PIECE], fixed_rows(q),
            x_sem.at[0, q], x_sem.at[1, 0], at(0, q),
        )

    def y_copy(d, g):
        return remote(planes(ysend, g), yr.at[d - 1, g], y_sem.at[0, d, g], y_sem.at[1, d, g], at(py + d, pz))

    def y_fixed(d):
        return remote(fixed_rows(pz), fixed_rows(pz), ys_sem.at[0, d], ys_sem.at[1, 0], at(py + d, pz))

    def around(j, g):
        part = piece(g, pz - j)
        return remote(part, part, a_sem.at[0, j, g], a_sem.at[1, j, g], ahead)

    def around_arrived(j, g):
        part = piece(g, pz - j - 1)
        remote(part, part, a_sem.at[0, j, g], a_sem.at[1, j, g], ahead).wait_recv()

    def back(j, g):
        part = piece(g, pz + j)
        return remote(part, part, b_sem.at[0, j, g], b_sem.at[1, j, g], behind)

    def back_arrived(j, g):
        part = piece(g, pz + j + 1)
        remote(part, part, b_sem.at[0, j, g], b_sem.at[1, j, g], behind).wait_recv()

    def fixed_around(j):
        part = fixed_rows(pz - j)
        return remote(part, part, fa_sem.at[0, j], fa_sem.at[1, j], ahead)

    def fixed_back(j):
        part = fixed_rows(pz + j)
        return remote(part, part, fb_sem.at[0, j], fb_sem.at[1, j], behind)

    def fixed_start(j):
        if j > 0:
            part = fixed_rows(pz - j)
            remote(part, part, fa_sem.at[0, j - 1], fa_sem.at[1, j - 1], ahead).wait_recv()
        fixed_around(j).start()
        share(1, -j).start()
        if j <= near and j > 0:
            part = fixed_rows(pz + j)
            remote(part, part, fb_sem.at[0, j - 1], fb_sem.at[1, j - 1], behind).wait_recv()
            share(1, j).start()
        if j < near:
            fixed_back(j).start()

    def fixed_finish():
        part = fixed_rows(pz - far)
        remote(part, part, fa_sem.at[0, far - 1], fa_sem.at[1, far - 1], ahead).wait_recv()
        share(1, -far).start()

    def fixed_spread():
        @pl.when(py == 0)
        def _():
            @pl.when(pz > 0)
            def _():
                part = fixed_rows(pz)
                remote(part, part, x_sem.at[0, 0], x_sem.at[1, 0], ahead).wait_recv()

            for d in range(1, NY):
                y_fixed(d).start()

    def fixed_here():
        @pl.when(py > 0)
        def _():
            part = fixed_rows(pz)
            remote(part, part, ys_sem.at[0, 0], ys_sem.at[1, 0], ahead).wait_recv()

    def share(kind, off):
        start = (2 * kind + core) * REF + lax.rem(pz + off + NZ, NZ) * PIECE
        part = kv.at[:, pl.ds(pl.multiple_of(start, PIECE), PIECE)]
        return remote(part, part, f_sem.at[0, kind, off + far], f_sem.at[1, kind, off + far], partner)

    def shared(kind):
        for off in range(-far, near + 1):
            start = (2 * kind + 1 - core) * REF + lax.rem(2 * NZ - 1 - pz + off, NZ) * PIECE
            part = kv.at[:, pl.ds(pl.multiple_of(start, PIECE), PIECE)]
            remote(
                part, part, f_sem.at[0, kind, off + far], f_sem.at[1, kind, off + far], partner
            ).wait_recv()

    def halo_rows(hk, col):
        return kv.at[hk, pl.ds(pl.multiple_of(HALO + col * TOK, 16), TOK)]

    def halo_copy(kind, src, hk, col, peer):
        return remote(src, halo_rows(hk, col), hs_sem.at[kind, hk], hr_sem.at[col, hk], peer)

    def own_rows(hk):
        return kv.at[hk, OWN:HALO]

    def halo_sends(hk):
        return (
            halo_copy(0, own_rows(hk), hk, 1, right),
            halo_copy(1, own_rows(hk), hk, 4, left),
            halo_copy(2, own_rows(hk), hk, 2 + core, partner),
        )

    def forwards(hk):
        return (
            halo_copy(5, halo_rows(hk, 4 - 3 * core), hk, 5 - 5 * core, extra),
            halo_copy(3, halo_rows(hk, 1), hk, 2 * core, partner),
            halo_copy(4, halo_rows(hk, 4), hk, 3 + 2 * core, partner),
        )

    def halo_wait(hk, col):
        halo_copy(0, own_rows(hk), hk, col, right).wait_recv()

    def halo_start(hk):
        for copy in halo_sends(hk):
            copy.start()

    def halo_forward(hk):
        halo_wait(hk, 1)
        halo_wait(hk, 4)
        for copy in forwards(hk):
            copy.start()

    position = lax.broadcasted_iota(jnp.int32, (1, PAD - OWN), 1) + OWN
    bias = jnp.where(position >= KEYS, NEG, 0.0)
    for col in range(2 * REACH):
        edge = HALO + col * TOK
        closed = jnp.where(pattern_ref[0, col] != 0, 0.0, NEG)
        bias = bias + jnp.where((position >= edge) & (position < edge + TOK), closed, 0.0)
    scale = HD ** -0.5

    def segment(h, first, last):
        q = qb[:, h * HD : (h + 1) * HD]
        peak = jnp.full((TOK, HD), NEG, jnp.float32)
        tiles = range(first, last, TILE)
        for row in tiles:
            sc = lax.dot_general(
                q, kv[2 * h, row : row + TILE, :], (((1,), (1,)), ((), ())),
                preferred_element_type=jnp.float32,
            )
            sc = sc * scale
            if row >= OWN:
                sc = sc + bias[:, row - OWN : row - OWN + TILE]
            scores[:, row - first : row - first + TILE] = sc
            peak = jnp.maximum(peak, jnp.maximum(sc[:, :HD], sc[:, HD:]))
        top = jnp.max(peak, axis=1, keepdims=True)
        total = jnp.zeros((TOK, HD), jnp.float32)
        acc = jnp.zeros((TOK, HD), jnp.float32)
        for row in tiles:
            w = jnp.exp(scores[:, row - first : row - first + TILE] - top)
            total = total + (w[:, :HD] + w[:, HD:])
            acc = acc + jnp.dot(
                w.astype(BF), kv[2 * h + 1, row : row + TILE, :], preferred_element_type=jnp.float32
            )
        return top, jnp.sum(total, axis=1, keepdims=True), acc

    def near_part(h):
        for col in range(2 * REACH):
            if col not in (1, 4):
                halo_wait(2 * h, col)
                halo_wait(2 * h + 1, col)
        top, total, acc = segment(h, OWN, PAD)
        top1[h] = top
        total1[h] = total
        acc1[h] = acc

    def joined(h, first, last):
        top, total, acc = segment(h, first, last)
        best = jnp.maximum(top, top1[h])
        new = jnp.exp(top - best)
        old = jnp.exp(top1[h] - best)
        return best, total * new + total1[h] * old, acc * new + acc1[h] * old

    def fixed_part():
        fixed_finish()
        shared(1)
        for h in range(LH):
            best, total, acc = joined(h, 2 * REF, OWN)
            top1[h] = best
            total1[h] = total
            acc1[h] = acc

    def last_part(h):
        best, total, acc = joined(h, 0, 2 * REF)
        att[:, h * HD : (h + 1) * HD] = (acc / total).astype(BF)

    source = (pz == 0) & (py == 0)
    heads = range(LH)
    groups = range(GROUPS)
    step_actions = {
        "own": halo_start, "on": halo_forward, "near": near_part, "spread": fixed_spread,
        "here": fixed_here, "fixed": fixed_start, "fixed_part": fixed_part, "query": query_load.wait,
    }
    for g in groups:
        swap(g).start()

    @pl.when(source)
    def _():
        for q in range(1, NZ):
            fixed_copy(q).start()
        fixed_rows(0)[...] = kv[:, OWN : OWN + PIECE, :]

    halo_start(0)
    halo_start(1)
    query_load.start()
    for load in weight_loads:
        load.start()
    for j in range(far):
        for g in groups:
            if j == 0:
                swap(g).wait_recv()
                mine[PER * g : PER * g + PER] = mine[PER * g : PER * g + PER] + mrecv[PER * g : PER * g + PER]
                ps[0, g] = mine_rows(g, pz + far)
                p_copy(0, g).start()
                if near > 0:
                    ss[0, g] = mine_rows(g, pz - near)
                    s_copy(0, g).start()
            else:
                p_copy(j - 1, g).wait_recv()
                ps[j, g] = mine_rows(g, pz + far - j) + pr[j - 1, g]
                p_copy(j, g).start()
                if j < near:
                    s_copy(j - 1, g).wait_recv()
                    ss[j, g] = mine_rows(g, pz - near + j) + sr[j - 1, g]
                    s_copy(j, g).start()
        for action in PACE[j]:
            step_actions[action[0]](*action[1:])
    for g in groups:
        total = mine_rows(g, pz)
        if near > 0:
            s_copy(near - 1, g).wait_recv()
            total = total + sr[near - 1, g]
        p_copy(far - 1, g).wait_recv()
        ysend[PER * g : PER * g + PER] = total + pr[far - 1, g]
        for d in range(1, NY):
            y_copy(d, g).start()
    for action in PACE[far]:
        step_actions[action[0]](*action[1:])
    for g in groups:
        total = ysend[PER * g : PER * g + PER]
        for d in range(1, NY):
            y_copy(d, g).wait_recv()
            total = total + yr[d - 1, g]
        piece(g, pz)[...] = total
        around(0, g).start()
        if near > 0:
            back(0, g).start()
        share(0, 0).start()
    for action in PACE[far + 1]:
        step_actions[action[0]](*action[1:])
    for j in range(1, far):
        for g in groups:
            around_arrived(j - 1, g)
            around(j, g).start()
            share(0, -j).start()
            if j <= near:
                back_arrived(j - 1, g)
                share(0, j).start()
            if j < near:
                back(j, g).start()
        for action in PACE[far + 1 + j]:
            step_actions[action[0]](*action[1:])
    for g in groups:
        around_arrived(far - 1, g)
        share(0, -far).start()
    for action in PACE[2 * far + 1]:
        step_actions[action[0]](*action[1:])
    shared(0)
    for h in heads:
        last_part(h)
    for load in weight_loads:
        load.wait()

    def project(b):
        p[b] = jnp.dot(att[...], wb[b], preferred_element_type=jnp.float32).astype(BF)

    def head_copy(kind, i, src, dst, peer):
        return pltpu.make_async_remote_copy(
            src_ref=src, dst_ref=dst, send_sem=mix_s.at[kind, i], recv_sem=mix_r.at[kind, i],
            device_id={"head": peer}, device_id_type=MESH,
        )

    def cross(c):
        return pltpu.make_async_remote_copy(
            src_ref=ty.at[c], dst_ref=ry.at[c], send_sem=c_sem.at[0, c], recv_sem=c_sem.at[1, c],
            device_id={"head": pair}, device_id_type=MESH,
        )

    part = TOK // PARTS
    half = part // 2
    items = [(which, c) for which in (1 - side, side) for c in range(PARTS)]
    rows = [(slice(c * part, c * part + half), slice(c * part + half, (c + 1) * part)) for c in range(PARTS)]
    first, direct, second = [], [], []
    for i, (which, c) in enumerate(items):
        upper, lower = rows[c]
        first.append((
            head_copy(0, i, p.at[xo * 2 + which, upper], r1p.at[i], nxt),
            head_copy(1, i, p.at[xo * 2 + which, lower], r1m.at[i], prv),
        ))
        direct.append((
            head_copy(2, i, p.at[xn * 2 + which, lower], r2p.at[i, half:], nxt),
            head_copy(3, i, p.at[xp * 2 + which, upper], r2m.at[i, :half], prv),
        ))
        second.append((
            head_copy(4, i, t2p.at[i], r2p.at[i, :half], nxt),
            head_copy(5, i, t2m.at[i], r2m.at[i, half:], prv),
        ))

    def pass_on(i):
        which, c = items[i]
        upper, lower = rows[c]
        first[i][0].wait_recv()
        t2p[i] = p[xn * 2 + which, upper] + r1p[i]
        second[i][0].start()
        first[i][1].wait_recv()
        t2m[i] = p[xp * 2 + which, lower] + r1m[i]
        second[i][1].start()

    def collect(i):
        which, c = items[i]
        for copy in direct[i] + second[i]:
            copy.wait_recv()
        return (
            p[x * 2 + which, c * part : (c + 1) * part].astype(jnp.float32)
            + r2p[i].astype(jnp.float32)
            + r2m[i].astype(jnp.float32)
        )

    def launch(phase):
        which = items[phase * PARTS][0]
        todo = range(phase * PARTS, (phase + 1) * PARTS)
        project(xo * 2 + which)
        for i in todo:
            for copy in first[i]:
                copy.start()
        project(xn * 2 + which)
        project(xp * 2 + which)
        for i in todo:
            for copy in direct[i]:
                copy.start()

    launch(0)
    for i in range(PARTS):
        pass_on(i)
    launch(1)
    project(x * 2 + 1 - side)
    for c in range(PARTS):
        ty[c] = collect(c).astype(BF)
        cross(c).start()
    project(x * 2 + side)
    for i in range(PARTS, 2 * PARTS):
        pass_on(i)
    for c in range(PARTS):
        total = collect(PARTS + c)
        cross(c).wait_recv()
        out[c * part : (c + 1) * part, :] = (total + ry[c].astype(jnp.float32)).astype(BF)

    for i in range(2 * PARTS):
        for copy in first[i] + direct[i] + second[i]:
            copy.wait_send()
    for c in range(PARTS):
        cross(c).wait_send()

    for kind in range(2):
        for off in range(-far, near + 1):
            share(kind, off).wait_send()
    for g in groups:
        swap(g).wait_send()
        for j in range(far):
            p_copy(j, g).wait_send()
            around(j, g).wait_send()
        for j in range(near):
            s_copy(j, g).wait_send()
            back(j, g).wait_send()
        for d in range(1, NY):
            y_copy(d, g).wait_send()
    for j in range(far):
        fixed_around(j).wait_send()
    for j in range(near):
        fixed_back(j).wait_send()
    for hk in range(HK):
        for copy in halo_sends(hk) + forwards(hk):
            copy.wait_send()

    @pl.when(py == 0)
    def _():
        for d in range(1, NY):
            y_fixed(d).wait_send()

    @pl.when(source)
    def _():
        for q in range(1, NZ):
            fixed_copy(q).wait_send()


def layer(owners, pattern, q, k, v, w):
    dma = pltpu.SemaphoreType.DMA
    width = LH * HD
    whole = pltpu.VMEM((HK, REF, HD), BF)
    hop = pltpu.VMEM((NZ // 2, GROUPS, PER, PIECE, HD), BF)
    part = TOK // PARTS
    halves = pltpu.VMEM((2 * PARTS, part // 2, width), BF)
    fulls = pltpu.VMEM((2 * PARTS, part, width), BF)
    pairs = pltpu.VMEM((PARTS, part, width), BF)
    column = pltpu.VMEM((LH, TOK, 1), jnp.float32)
    hbm = pl.BlockSpec(memory_space=pl.ANY)
    return pl.pallas_call(
        layer_kernel,
        out_shape=jax.ShapeDtypeStruct((TOK, width), BF),
        in_specs=[SMEM, SMEM, hbm, hbm, hbm, hbm],
        out_specs=VMEM,
        scratch_shapes=[
            pltpu.VMEM((HK, PAD, HD), BF), pltpu.VMEM((TOK, width), BF),
            pltpu.VMEM((2 * NX, width, width), BF),
            whole, whole, whole, hop, hop, hop, hop,
            pltpu.VMEM((HK, PIECE, HD), BF), pltpu.VMEM((NY - 1, GROUPS, PER, PIECE, HD), BF),
            pltpu.VMEM((TOK, PAD - OWN), jnp.float32), pltpu.VMEM((TOK, width), BF),
            pltpu.VMEM((LH, TOK, HD), jnp.float32), column, column,
            pltpu.VMEM((2 * NX, TOK, width), BF),
            halves, halves, halves, halves, fulls, fulls, pairs, pairs,
            dma((6, HK)), dma((6, HK)), dma((2, GROUPS)), dma((2, NZ // 2, GROUPS)), dma((2, NZ // 2, GROUPS)),
            dma((2, NZ)), dma((2, NY, GROUPS)), dma((2, NY)),
            dma((2, NZ // 2, GROUPS)), dma((2, NZ // 2, GROUPS)), dma((2, NZ // 2)), dma((2, NZ // 2)), dma((2, 2, NZ)),
            dma((HK,)), dma((2 * NX,)), dma, dma((6, 2 * PARTS)), dma((6, 2 * PARTS)), dma((2, PARTS)),
        ],
        compiler_params=pltpu.CompilerParams(
            collective_id=0, has_side_effects=True, vmem_limit_bytes=56 << 20
        ),
        name="layer",
    )(owners, pattern, q, k, v, w)


def body(query_rows, key_rows, value_rows, pattern, owners, out_weight):
    return layer(owners, pattern, query_rows, key_rows, value_rows, out_weight)


def solution(mesh):
    return jax.shard_map(
        body,
        mesh=mesh,
        in_specs=(
            P("seq", "head"),
            P("seq", "head"),
            P("seq", "head"),
            P("seq", None),
            P(),
            P("head", None),
        ),
        out_specs=P("seq", "head"),
        check_vma=False,
    )
```

```python
import functools

import jax
import jax.numpy as jnp
from jax import lax
from jax.experimental import pallas as pl
from jax.experimental.pallas import tpu as pltpu
from jax.sharding import PartitionSpec as P

MESH = pl.DeviceIdType.MESH
HD = 128
LH = 3
TOK = 320
REF = 256
REACH = 3
NZ = 8
NY = 4
NX = 4
HK = 2 * LH
PIECE = REF // NZ
OWN = 4 * REF
HALO = OWN + TOK
KEYS = HALO + 2 * REACH * TOK
PAD = -(-KEYS // 256) * 256
NEG = -1e30
TILE = 256
GROUPS = 1
PER = HK // GROUPS
PARTS = 2
PACE = (
    (("own", 2), ("own", 3), ("spread",)),
    (("own", 4), ("own", 5), ("on", 0), ("here",), ("fixed", 0)),
    (("on", 1), ("on", 2), ("fixed", 1), ("on", 3), ("query",), ("near", 0), ("fixed", 2)),
    (("on", 4), ("on", 5), ("fixed", 3), ("near", 1)),
    (("near", 2), ("fixed_part",)),
    (),
)
VMEM = pl.BlockSpec(memory_space=pltpu.VMEM)
SMEM = pl.BlockSpec(memory_space=pltpu.SMEM)
BF = jnp.bfloat16


def layer_kernel(
    owners_ref, pattern_ref, q_hbm, k_hbm, v_hbm, w_hbm, out,
    kv, qb, wb, mine, msend, mrecv, part_s, part_r, ysend, yr,
    scores, att, acc1, top1, total1, p, r1p, r1m, t2p, t2m, r2p, r2m, ty, ry,
    hs_sem, hr_sem, m_sem, p_sem, x_sem, y_sem, ys_sem, a_sem, fa_sem, fb_sem, f_sem,
    in_sem, w_sem, q_sem, mix_s, mix_r, c_sem,
):
    s = lax.axis_index("seq")
    head = lax.axis_index("head")
    x = head // 2
    side = lax.rem(head, 2)
    xn = lax.rem(x + 1, NX)
    xp = lax.rem(x + NX - 1, NX)
    xo = lax.rem(x + 2, NX)
    nxt = xn * 2 + side
    prv = xp * 2 + side
    pair = x * 2 + 1 - side
    width = LH * HD
    n = 2 * NZ * NY
    core = lax.rem(s, 2)
    z = lax.rem(s // 2, NZ)
    y = s // (2 * NZ)
    step = 1 - 2 * core
    pz = jnp.where(core == 0, z, NZ - 1 - z)
    py = jnp.where(core == 0, y, NY - 1 - y)
    right = lax.rem(s + 2, n)
    left = lax.rem(s - 2 + n, n)
    partner = s + step
    extra = lax.rem(s - step + n, n)

    def at(yy, zz):
        zz = lax.rem(zz + NZ, NZ)
        yy = lax.rem(yy + NY, NY)
        zz = jnp.where(core == 0, zz, NZ - 1 - zz)
        yy = jnp.where(core == 0, yy, NY - 1 - yy)
        return (yy * NZ + zz) * 2 + core

    far, near = NZ // 2, NZ // 2 - 1
    ahead = at(py, pz + 1)
    behind = at(py, pz - 1)
    ahead2 = at(py, pz + 2)
    behind2 = at(py, pz - 2)

    loads = []
    for h in range(LH):
        for i, ref in enumerate((k_hbm, v_hbm)):
            loads.append(pltpu.make_async_copy(
                ref.at[:, h * HD : (h + 1) * HD], kv.at[2 * h + i, OWN:HALO], in_sem.at[2 * h + i]
            ))
            loads[-1].start()

    barrier = pltpu.get_barrier_semaphore()
    peers = [partner, right, left, extra]
    peers += [at(py, pz + d) for d in range(1, NZ)]
    peers += [at(py + d, pz) for d in range(1, NY)]
    for peer in peers:
        pl.semaphore_signal(barrier, inc=1, device_id={"seq": peer}, device_id_type=MESH)
    for peer in (nxt, prv, pair):
        pl.semaphore_signal(barrier, inc=1, device_id={"head": peer}, device_id_type=MESH)

    query_load = pltpu.make_async_copy(q_hbm, qb, q_sem)
    weight_loads = [
        pltpu.make_async_copy(w_hbm.at[:, b * width : (b + 1) * width], wb.at[b], w_sem.at[b])
        for b in range(2 * NX)
    ]
    if PAD > KEYS:
        kv[:, KEYS:PAD, :] = jnp.zeros((HK, PAD - KEYS, HD), BF)

    low = jnp.int32(n)
    high = jnp.int32(-1)
    for i in range(4):
        o = owners_ref[i]
        low = jnp.minimum(low, jnp.where(o == 0, n, o))
        high = jnp.maximum(high, jnp.where(o == n - 1, -1, o))
    wanted = jnp.where(core == 0, low, high)
    given = jnp.where(core == 0, high, low)
    keep = jnp.where(wanted == s, 1.0, 0.0).astype(BF)
    give = jnp.where(given == s, 1.0, 0.0).astype(BF)
    for hk in range(HK):
        loads[hk].wait()
        block = kv[hk, OWN : OWN + REF, :]
        mine[hk] = block * keep
        msend[hk] = block * give

    pl.semaphore_wait(barrier, len(peers) + 3)

    def remote(src, dst, send, recv, peer):
        return pltpu.make_async_remote_copy(
            src_ref=src, dst_ref=dst, send_sem=send, recv_sem=recv,
            device_id={"seq": peer}, device_id_type=MESH,
        )

    def planes(ref, g):
        return ref.at[PER * g : PER * g + PER]

    def swap(g):
        return remote(planes(msend, g), planes(mrecv, g), m_sem.at[0, g], m_sem.at[1, g], partner)

    def mine_at(q):
        return mine.at[:, pl.ds(pl.multiple_of(lax.rem(q + NZ, NZ) * PIECE, PIECE), PIECE)]

    def rs_copy(i):
        src, dst, peer = (
            (mine_at(pz + 3), part_r.at[1], ahead2),
            (mine_at(pz - 3), part_r.at[2], behind2),
            (mine_at(pz + 4), part_r.at[0], ahead2),
            (mine_at(pz - 2), part_r.at[3], behind2),
            (part_s.at[0], part_r.at[4], ahead2),
            (part_s.at[1], part_r.at[5], ahead),
            (part_s.at[2], part_r.at[6], behind),
        )[i]
        return remote(src, dst, p_sem.at[0, i], p_sem.at[1, i], peer)

    base = core * REF

    def piece(g, q):
        start = base + lax.rem(q + NZ, NZ) * PIECE
        return kv.at[PER * g : PER * g + PER, pl.ds(pl.multiple_of(start, PIECE), PIECE)]

    def mine_rows(g, q):
        start = lax.rem(q + NZ, NZ) * PIECE
        return mine[PER * g : PER * g + PER, pl.ds(pl.multiple_of(start, PIECE), PIECE), :]

    def fixed_rows(q):
        start = 2 * REF + base + lax.rem(q + NZ, NZ) * PIECE
        return kv.at[:, pl.ds(pl.multiple_of(start, PIECE), PIECE)]

    def fixed_copy(q):
        return remote(
            kv.at[:, OWN + q * PIECE : OWN + (q + 1) * PIECE], fixed_rows(q),
            x_sem.at[0, q], x_sem.at[1, 0], at(0, q),
        )

    def y_copy(d, g):
        return remote(planes(ysend, g), yr.at[d - 1, g], y_sem.at[0, d, g], y_sem.at[1, d, g], at(py + d, pz))

    def y_fixed(d):
        return remote(fixed_rows(pz), fixed_rows(pz), ys_sem.at[0, d], ys_sem.at[1, 0], at(py + d, pz))

    routes = ((0, 1), (0, -1), (0, 2), (0, -2), (-1, 2), (1, -2), (-2, 2))

    def ag_copy(i):
        off, to = routes[i]
        part = piece(0, pz + off)
        peer = {1: ahead, -1: behind, 2: ahead2, -2: behind2}[to]
        return remote(part, part, a_sem.at[0, i], a_sem.at[1, i], peer)

    def ag_arrived(i):
        off, to = routes[i]
        part = piece(0, pz + off - to)
        remote(part, part, a_sem.at[0, i], a_sem.at[1, i], ahead).wait_recv()
        share(0, off - to).start()

    def fixed_around(j):
        part = fixed_rows(pz - j)
        return remote(part, part, fa_sem.at[0, j], fa_sem.at[1, j], ahead)

    def fixed_back(j):
        part = fixed_rows(pz + j)
        return remote(part, part, fb_sem.at[0, j], fb_sem.at[1, j], behind)

    def fixed_start(j):
        if j > 0:
            part = fixed_rows(pz - j)
            remote(part, part, fa_sem.at[0, j - 1], fa_sem.at[1, j - 1], ahead).wait_recv()
        fixed_around(j).start()
        share(1, -j).start()
        if j <= near and j > 0:
            part = fixed_rows(pz + j)
            remote(part, part, fb_sem.at[0, j - 1], fb_sem.at[1, j - 1], behind).wait_recv()
            share(1, j).start()
        if j < near:
            fixed_back(j).start()

    def fixed_finish():
        part = fixed_rows(pz - far)
        remote(part, part, fa_sem.at[0, far - 1], fa_sem.at[1, far - 1], ahead).wait_recv()
        share(1, -far).start()

    def fixed_spread():
        @pl.when(py == 0)
        def _():
            @pl.when(pz > 0)
            def _():
                part = fixed_rows(pz)
                remote(part, part, x_sem.at[0, 0], x_sem.at[1, 0], ahead).wait_recv()

            for d in range(1, NY):
                y_fixed(d).start()

    def fixed_here():
        @pl.when(py > 0)
        def _():
            part = fixed_rows(pz)
            remote(part, part, ys_sem.at[0, 0], ys_sem.at[1, 0], ahead).wait_recv()

    def share(kind, off):
        start = (2 * kind + core) * REF + lax.rem(pz + off + NZ, NZ) * PIECE
        part = kv.at[:, pl.ds(pl.multiple_of(start, PIECE), PIECE)]
        return remote(part, part, f_sem.at[0, kind, off + far], f_sem.at[1, kind, off + far], partner)

    def shared(kind):
        for off in range(-far, near + 1):
            start = (2 * kind + 1 - core) * REF + lax.rem(2 * NZ - 1 - pz + off, NZ) * PIECE
            part = kv.at[:, pl.ds(pl.multiple_of(start, PIECE), PIECE)]
            remote(
                part, part, f_sem.at[0, kind, off + far], f_sem.at[1, kind, off + far], partner
            ).wait_recv()

    def halo_rows(hk, col):
        return kv.at[hk, pl.ds(pl.multiple_of(HALO + col * TOK, 16), TOK)]

    def halo_copy(kind, src, hk, col, peer):
        return remote(src, halo_rows(hk, col), hs_sem.at[kind, hk], hr_sem.at[col, hk], peer)

    def own_rows(hk):
        return kv.at[hk, OWN:HALO]

    def halo_sends(hk):
        return (
            halo_copy(0, own_rows(hk), hk, 1, right),
            halo_copy(1, own_rows(hk), hk, 4, left),
            halo_copy(2, own_rows(hk), hk, 2 + core, partner),
        )

    def forwards(hk):
        return (
            halo_copy(5, halo_rows(hk, 4 - 3 * core), hk, 5 - 5 * core, extra),
            halo_copy(3, halo_rows(hk, 1), hk, 2 * core, partner),
            halo_copy(4, halo_rows(hk, 4), hk, 3 + 2 * core, partner),
        )

    def halo_wait(hk, col):
        halo_copy(0, own_rows(hk), hk, col, right).wait_recv()

    def halo_start(hk):
        for copy in halo_sends(hk):
            copy.start()

    def halo_forward(hk):
        halo_wait(hk, 1)
        halo_wait(hk, 4)
        for copy in forwards(hk):
            copy.start()

    position = lax.broadcasted_iota(jnp.int32, (1, PAD - OWN), 1) + OWN
    bias = jnp.where(position >= KEYS, NEG, 0.0)
    for col in range(2 * REACH):
        edge = HALO + col * TOK
        closed = jnp.where(pattern_ref[0, col] != 0, 0.0, NEG)
        bias = bias + jnp.where((position >= edge) & (position < edge + TOK), closed, 0.0)
    scale = HD ** -0.5

    def segment(h, first, last):
        q = qb[:, h * HD : (h + 1) * HD]
        peak = jnp.full((TOK, HD), NEG, jnp.float32)
        tiles = range(first, last, TILE)
        for row in tiles:
            sc = lax.dot_general(
                q, kv[2 * h, row : row + TILE, :], (((1,), (1,)), ((), ())),
                preferred_element_type=jnp.float32,
            )
            sc = sc * scale
            if row >= OWN:
                sc = sc + bias[:, row - OWN : row - OWN + TILE]
            scores[:, row - first : row - first + TILE] = sc
            peak = jnp.maximum(peak, jnp.maximum(sc[:, :HD], sc[:, HD:]))
        top = jnp.max(peak, axis=1, keepdims=True)
        total = jnp.zeros((TOK, HD), jnp.float32)
        acc = jnp.zeros((TOK, HD), jnp.float32)
        for row in tiles:
            w = jnp.exp(scores[:, row - first : row - first + TILE] - top)
            total = total + (w[:, :HD] + w[:, HD:])
            acc = acc + jnp.dot(
                w.astype(BF), kv[2 * h + 1, row : row + TILE, :], preferred_element_type=jnp.float32
            )
        return top, jnp.sum(total, axis=1, keepdims=True), acc

    def near_part(h):
        for col in range(2 * REACH):
            if col not in (1, 4):
                halo_wait(2 * h, col)
                halo_wait(2 * h + 1, col)
        top, total, acc = segment(h, OWN, PAD)
        top1[h] = top
        total1[h] = total
        acc1[h] = acc

    def joined(h, first, last):
        top, total, acc = segment(h, first, last)
        best = jnp.maximum(top, top1[h])
        new = jnp.exp(top - best)
        old = jnp.exp(top1[h] - best)
        return best, total * new + total1[h] * old, acc * new + acc1[h] * old

    def fixed_part():
        fixed_finish()
        shared(1)
        for h in range(LH):
            best, total, acc = joined(h, 2 * REF, OWN)
            top1[h] = best
            total1[h] = total
            acc1[h] = acc

    def last_part(h):
        best, total, acc = joined(h, 0, 2 * REF)
        att[:, h * HD : (h + 1) * HD] = (acc / total).astype(BF)

    source = (pz == 0) & (py == 0)
    heads = range(LH)
    groups = range(GROUPS)
    step_actions = {
        "own": halo_start, "on": halo_forward, "near": near_part, "spread": fixed_spread,
        "here": fixed_here, "fixed": fixed_start, "fixed_part": fixed_part, "query": query_load.wait,
    }

    def pace(i):
        for action in PACE[i]:
            step_actions[action[0]](*action[1:])

    for g in groups:
        swap(g).start()

    @pl.when(source)
    def _():
        for q in range(1, NZ):
            fixed_copy(q).start()
        fixed_rows(0)[...] = kv[:, OWN : OWN + PIECE, :]

    halo_start(0)
    halo_start(1)
    query_load.start()
    for load in weight_loads:
        load.start()
    swap(0).wait_recv()
    mine[...] = mine[...] + mrecv[...]
    for i in range(4):
        rs_copy(i).start()
    pace(0)
    for i, first, held in ((5, 0, 1), (6, 1, 2), (4, 2, 0)):
        rs_copy(first).wait_recv()
        part_s[i - 4] = mine_rows(0, (pz + 2, pz + 1, pz - 1)[i - 4]) + part_r[held]
        rs_copy(i).start()
    pace(1)
    total = mine_rows(0, pz)
    for i, held in ((3, 3), (5, 5), (6, 6), (4, 4)):
        rs_copy(i).wait_recv()
        total = total + part_r[held]
    ysend[...] = total
    for d in range(1, NY):
        y_copy(d, 0).start()
    pace(2)
    total = ysend[...]
    for d in range(1, NY):
        y_copy(d, 0).wait_recv()
        total = total + yr[d - 1, 0]
    piece(0, pz)[...] = total
    for i in range(4):
        ag_copy(i).start()
    share(0, 0).start()
    pace(3)
    for i, onward in ((0, 4), (1, 5), (2, 6), (3, None)):
        ag_arrived(i)
        if onward is not None:
            ag_copy(onward).start()
    pace(4)
    for i in (4, 5, 6):
        ag_arrived(i)
    pace(5)
    shared(0)
    for h in heads:
        last_part(h)
    for load in weight_loads:
        load.wait()

    def project(b):
        p[b] = jnp.dot(att[...], wb[b], preferred_element_type=jnp.float32).astype(BF)

    def head_copy(kind, i, src, dst, peer):
        return pltpu.make_async_remote_copy(
            src_ref=src, dst_ref=dst, send_sem=mix_s.at[kind, i], recv_sem=mix_r.at[kind, i],
            device_id={"head": peer}, device_id_type=MESH,
        )

    def cross(c):
        return pltpu.make_async_remote_copy(
            src_ref=ty.at[c], dst_ref=ry.at[c], send_sem=c_sem.at[0, c], recv_sem=c_sem.at[1, c],
            device_id={"head": pair}, device_id_type=MESH,
        )

    part = TOK // PARTS
    half = part // 2
    items = [(which, c) for which in (1 - side, side) for c in range(PARTS)]
    rows = [(slice(c * part, c * part + half), slice(c * part + half, (c + 1) * part)) for c in range(PARTS)]
    first, direct, second = [], [], []
    for i, (which, c) in enumerate(items):
        upper, lower = rows[c]
        first.append((
            head_copy(0, i, p.at[xo * 2 + which, upper], r1p.at[i], nxt),
            head_copy(1, i, p.at[xo * 2 + which, lower], r1m.at[i], prv),
        ))
        direct.append((
            head_copy(2, i, p.at[xn * 2 + which, lower], r2p.at[i, half:], nxt),
            head_copy(3, i, p.at[xp * 2 + which, upper], r2m.at[i, :half], prv),
        ))
        second.append((
            head_copy(4, i, t2p.at[i], r2p.at[i, :half], nxt),
            head_copy(5, i, t2m.at[i], r2m.at[i, half:], prv),
        ))

    def pass_on(i):
        which, c = items[i]
        upper, lower = rows[c]
        first[i][0].wait_recv()
        t2p[i] = p[xn * 2 + which, upper] + r1p[i]
        second[i][0].start()
        first[i][1].wait_recv()
        t2m[i] = p[xp * 2 + which, lower] + r1m[i]
        second[i][1].start()

    def collect(i):
        which, c = items[i]
        for copy in direct[i] + second[i]:
            copy.wait_recv()
        return (
            p[x * 2 + which, c * part : (c + 1) * part].astype(jnp.float32)
            + r2p[i].astype(jnp.float32)
            + r2m[i].astype(jnp.float32)
        )

    def launch(phase):
        which = items[phase * PARTS][0]
        todo = range(phase * PARTS, (phase + 1) * PARTS)
        project(xo * 2 + which)
        for i in todo:
            for copy in first[i]:
                copy.start()
        project(xn * 2 + which)
        project(xp * 2 + which)
        for i in todo:
            for copy in direct[i]:
                copy.start()

    launch(0)
    for i in range(PARTS):
        pass_on(i)
    launch(1)
    project(x * 2 + 1 - side)
    for c in range(PARTS):
        ty[c] = collect(c).astype(BF)
        cross(c).start()
    project(x * 2 + side)
    for i in range(PARTS, 2 * PARTS):
        pass_on(i)
    for c in range(PARTS):
        total = collect(PARTS + c)
        cross(c).wait_recv()
        out[c * part : (c + 1) * part, :] = (total + ry[c].astype(jnp.float32)).astype(BF)

    for i in range(2 * PARTS):
        for copy in first[i] + direct[i] + second[i]:
            copy.wait_send()
    for c in range(PARTS):
        cross(c).wait_send()

    for kind in range(2):
        for off in range(-far, near + 1):
            share(kind, off).wait_send()
    for g in groups:
        swap(g).wait_send()
        for i in range(7):
            rs_copy(i).wait_send()
            ag_copy(i).wait_send()
        for d in range(1, NY):
            y_copy(d, g).wait_send()
    for j in range(far):
        fixed_around(j).wait_send()
    for j in range(near):
        fixed_back(j).wait_send()
    for hk in range(HK):
        for copy in halo_sends(hk) + forwards(hk):
            copy.wait_send()

    @pl.when(py == 0)
    def _():
        for d in range(1, NY):
            y_fixed(d).wait_send()

    @pl.when(source)
    def _():
        for q in range(1, NZ):
            fixed_copy(q).wait_send()


def layer(owners, pattern, q, k, v, w):
    dma = pltpu.SemaphoreType.DMA
    width = LH * HD
    whole = pltpu.VMEM((HK, REF, HD), BF)
    part = TOK // PARTS
    halves = pltpu.VMEM((2 * PARTS, part // 2, width), BF)
    fulls = pltpu.VMEM((2 * PARTS, part, width), BF)
    pairs = pltpu.VMEM((PARTS, part, width), BF)
    column = pltpu.VMEM((LH, TOK, 1), jnp.float32)
    hbm = pl.BlockSpec(memory_space=pl.ANY)
    return pl.pallas_call(
        layer_kernel,
        out_shape=jax.ShapeDtypeStruct((TOK, width), BF),
        in_specs=[SMEM, SMEM, hbm, hbm, hbm, hbm],
        out_specs=VMEM,
        scratch_shapes=[
            pltpu.VMEM((HK, PAD, HD), BF), pltpu.VMEM((TOK, width), BF),
            pltpu.VMEM((2 * NX, width, width), BF),
            whole, whole, whole,
            pltpu.VMEM((3, HK, PIECE, HD), BF), pltpu.VMEM((7, HK, PIECE, HD), BF),
            pltpu.VMEM((HK, PIECE, HD), BF), pltpu.VMEM((NY - 1, GROUPS, PER, PIECE, HD), BF),
            pltpu.VMEM((TOK, PAD - OWN), jnp.float32), pltpu.VMEM((TOK, width), BF),
            pltpu.VMEM((LH, TOK, HD), jnp.float32), column, column,
            pltpu.VMEM((2 * NX, TOK, width), BF),
            halves, halves, halves, halves, fulls, fulls, pairs, pairs,
            dma((6, HK)), dma((6, HK)), dma((2, GROUPS)), dma((2, 7)),
            dma((2, NZ)), dma((2, NY, GROUPS)), dma((2, NY)),
            dma((2, 7)), dma((2, NZ // 2)), dma((2, NZ // 2)), dma((2, 2, NZ)),
            dma((HK,)), dma((2 * NX,)), dma, dma((6, 2 * PARTS)), dma((6, 2 * PARTS)), dma((2, PARTS)),
        ],
        compiler_params=pltpu.CompilerParams(
            collective_id=0, has_side_effects=True, vmem_limit_bytes=56 << 20
        ),
        name="layer",
    )(owners, pattern, q, k, v, w)


def body(query_rows, key_rows, value_rows, pattern, owners, out_weight):
    return layer(owners, pattern, query_rows, key_rows, value_rows, out_weight)


def solution(mesh):
    return jax.shard_map(
        body,
        mesh=mesh,
        in_specs=(
            P("seq", "head"),
            P("seq", "head"),
            P("seq", "head"),
            P("seq", None),
            P(),
            P("head", None),
        ),
        out_specs=P("seq", "head"),
        check_vma=False,
    )
```

```python
import math

import jax
import jax.numpy as jnp
from jax import lax
from jax.experimental import pallas as pl
from jax.experimental.pallas import tpu as pltpu
from jax.sharding import PartitionSpec as P

MESH = pl.DeviceIdType.MESH
HD = 128
LH = 3
TOK = 320
REF = 256
REACH = 3
NZ = 8
NY = 4
NX = 4
HK = 2 * LH
PIECE = REF // NZ
OWN = 4 * REF
HALO = OWN + TOK
KEYS = HALO + 2 * REACH * TOK
PAD = -(-KEYS // 256) * 256
NEG = -1e30
TILE = 256
GROUPS = 1
PER = HK // GROUPS
PARTS = 2
PACE = (
    (("own", 2), ("spread",)),
    (("own", 3),),
    (("own", 4), ("here",), ("fixed", 0)),
    (("own", 5), ("fixed", 1), ("on", 0), ("on", 1)),
    (("fixed", 2), ("on", 2), ("on", 3), ("query",), ("near", 0)),
    (("fixed", 3), ("on", 4)),
    (("on", 5), ("near", 1)),
    (("near", 2),),
    (("fixed_part",),),
    (),
)
VMEM = pl.BlockSpec(memory_space=pltpu.VMEM)
SMEM = pl.BlockSpec(memory_space=pltpu.SMEM)
BF = jnp.bfloat16


def layer_kernel(
    owners_ref, pattern_ref, q_hbm, k_hbm, v_hbm, w_hbm, out,
    kv, qb, q2, wb, mine, msend, mrecv, ps, pr, ss, sr, ysend, yr,
    scores, att, acc1, top1, total1, p, r1p, r1m, t2p, t2m, r2p, r2m, ty, ry,
    hs_sem, hr_sem, m_sem, p_sem, s_sem, x_sem, y_sem, ys_sem, a_sem, b_sem, fa_sem, fb_sem, f_sem,
    in_sem, w_sem, q_sem, mix_s, mix_r, c_sem,
):
    s = lax.axis_index("seq")
    head = lax.axis_index("head")
    x = head // 2
    side = lax.rem(head, 2)
    xn = lax.rem(x + 1, NX)
    xp = lax.rem(x + NX - 1, NX)
    xo = lax.rem(x + 2, NX)
    nxt = xn * 2 + side
    prv = xp * 2 + side
    pair = x * 2 + 1 - side
    width = LH * HD
    n = 2 * NZ * NY
    core = lax.rem(s, 2)
    z = lax.rem(s // 2, NZ)
    y = s // (2 * NZ)
    step = 1 - 2 * core
    pz = jnp.where(core == 0, z, NZ - 1 - z)
    py = jnp.where(core == 0, y, NY - 1 - y)
    right = lax.rem(s + 2, n)
    left = lax.rem(s - 2 + n, n)
    partner = s + step
    extra = lax.rem(s - step + n, n)

    def at(yy, zz):
        zz = lax.rem(zz + NZ, NZ)
        yy = lax.rem(yy + NY, NY)
        zz = jnp.where(core == 0, zz, NZ - 1 - zz)
        yy = jnp.where(core == 0, yy, NY - 1 - yy)
        return (yy * NZ + zz) * 2 + core

    far, near = NZ // 2, NZ // 2 - 1
    ahead = at(py, pz + 1)
    behind = at(py, pz - 1)

    loads = []
    for h in range(LH):
        for i, ref in enumerate((k_hbm, v_hbm)):
            loads.append(pltpu.make_async_copy(
                ref.at[:, h * HD : (h + 1) * HD], kv.at[2 * h + i, OWN:HALO], in_sem.at[2 * h + i]
            ))
            loads[-1].start()

    barrier = pltpu.get_barrier_semaphore()
    peers = [partner, right, left, extra]
    peers += [at(py, pz + d) for d in range(1, NZ)]
    peers += [at(py + d, pz) for d in range(1, NY)]
    for peer in peers:
        pl.semaphore_signal(barrier, inc=1, device_id={"seq": peer}, device_id_type=MESH)
    for peer in (nxt, prv, pair):
        pl.semaphore_signal(barrier, inc=1, device_id={"head": peer}, device_id_type=MESH)

    query_load = pltpu.make_async_copy(q_hbm, qb, q_sem)
    weight_loads = [
        pltpu.make_async_copy(w_hbm.at[:, b * width : (b + 1) * width], wb.at[b], w_sem.at[b])
        for b in range(2 * NX)
    ]
    if PAD > KEYS:
        kv[:, KEYS:PAD, :] = jnp.zeros((HK, PAD - KEYS, HD), BF)

    low = jnp.int32(n)
    high = jnp.int32(-1)
    for i in range(4):
        o = owners_ref[i]
        low = jnp.minimum(low, jnp.where(o == 0, n, o))
        high = jnp.maximum(high, jnp.where(o == n - 1, -1, o))
    wanted = jnp.where(core == 0, low, high)
    given = jnp.where(core == 0, high, low)
    keep = jnp.where(wanted == s, 1.0, 0.0).astype(BF)
    give = jnp.where(given == s, 1.0, 0.0).astype(BF)
    for hk in range(HK):
        loads[hk].wait()
        block = kv[hk, OWN : OWN + REF, :]
        mine[hk] = block * keep
        msend[hk] = block * give

    pl.semaphore_wait(barrier, len(peers) + 3)

    def remote(src, dst, send, recv, peer):
        return pltpu.make_async_remote_copy(
            src_ref=src, dst_ref=dst, send_sem=send, recv_sem=recv,
            device_id={"seq": peer}, device_id_type=MESH,
        )

    def planes(ref, g):
        return ref.at[PER * g : PER * g + PER]

    def swap(g):
        return remote(planes(msend, g), planes(mrecv, g), m_sem.at[0, g], m_sem.at[1, g], partner)

    def p_copy(j, g):
        return remote(ps.at[j, g], pr.at[j, g], p_sem.at[0, j, g], p_sem.at[1, j, g], ahead)

    def s_copy(j, g):
        return remote(ss.at[j, g], sr.at[j, g], s_sem.at[0, j, g], s_sem.at[1, j, g], behind)

    base = core * REF

    def piece(g, q):
        start = base + lax.rem(q + NZ, NZ) * PIECE
        return kv.at[PER * g : PER * g + PER, pl.ds(pl.multiple_of(start, PIECE), PIECE)]

    def mine_rows(g, q):
        start = lax.rem(q + NZ, NZ) * PIECE
        return mine[PER * g : PER * g + PER, pl.ds(pl.multiple_of(start, PIECE), PIECE), :]

    def fixed_rows(q):
        start = 2 * REF + base + lax.rem(q + NZ, NZ) * PIECE
        return kv.at[:, pl.ds(pl.multiple_of(start, PIECE), PIECE)]

    def fixed_copy(q):
        return remote(
            kv.at[:, OWN + q * PIECE : OWN + (q + 1) * PIECE], fixed_rows(q),
            x_sem.at[0, q], x_sem.at[1, 0], at(0, q),
        )

    def y_copy(d, g):
        return remote(planes(ysend, g), yr.at[d - 1, g], y_sem.at[0, d, g], y_sem.at[1, d, g], at(py + d, pz))

    def y_fixed(d):
        return remote(fixed_rows(pz), fixed_rows(pz), ys_sem.at[0, d], ys_sem.at[1, 0], at(py + d, pz))

    def around(j, g):
        part = piece(g, pz - j)
        return remote(part, part, a_sem.at[0, j, g], a_sem.at[1, j, g], ahead)

    def around_arrived(j, g):
        part = piece(g, pz - j - 1)
        remote(part, part, a_sem.at[0, j, g], a_sem.at[1, j, g], ahead).wait_recv()

    def back(j, g):
        part = piece(g, pz + j)
        return remote(part, part, b_sem.at[0, j, g], b_sem.at[1, j, g], behind)

    def back_arrived(j, g):
        part = piece(g, pz + j + 1)
        remote(part, part, b_sem.at[0, j, g], b_sem.at[1, j, g], behind).wait_recv()

    def fixed_around(j):
        part = fixed_rows(pz - j)
        return remote(part, part, fa_sem.at[0, j], fa_sem.at[1, j], ahead)

    def fixed_back(j):
        part = fixed_rows(pz + j)
        return remote(part, part, fb_sem.at[0, j], fb_sem.at[1, j], behind)

    def fixed_start(j):
        if j > 0:
            part = fixed_rows(pz - j)
            remote(part, part, fa_sem.at[0, j - 1], fa_sem.at[1, j - 1], ahead).wait_recv()
        fixed_around(j).start()
        share(1, -j).start()
        if j <= near and j > 0:
            part = fixed_rows(pz + j)
            remote(part, part, fb_sem.at[0, j - 1], fb_sem.at[1, j - 1], behind).wait_recv()
            share(1, j).start()
        if j < near:
            fixed_back(j).start()

    def fixed_finish():
        part = fixed_rows(pz - far)
        remote(part, part, fa_sem.at[0, far - 1], fa_sem.at[1, far - 1], ahead).wait_recv()
        share(1, -far).start()

    def fixed_spread():
        @pl.when(py == 0)
        def _():
            @pl.when(pz > 0)
            def _():
                part = fixed_rows(pz)
                remote(part, part, x_sem.at[0, 0], x_sem.at[1, 0], ahead).wait_recv()

            for d in range(1, NY):
                y_fixed(d).start()

    def fixed_here():
        @pl.when(py > 0)
        def _():
            part = fixed_rows(pz)
            remote(part, part, ys_sem.at[0, 0], ys_sem.at[1, 0], ahead).wait_recv()

    def share(kind, off):
        start = (2 * kind + core) * REF + lax.rem(pz + off + NZ, NZ) * PIECE
        part = kv.at[:, pl.ds(pl.multiple_of(start, PIECE), PIECE)]
        return remote(part, part, f_sem.at[0, kind, off + far], f_sem.at[1, kind, off + far], partner)

    def shared(kind):
        for off in range(-far, near + 1):
            start = (2 * kind + 1 - core) * REF + lax.rem(2 * NZ - 1 - pz + off, NZ) * PIECE
            part = kv.at[:, pl.ds(pl.multiple_of(start, PIECE), PIECE)]
            remote(
                part, part, f_sem.at[0, kind, off + far], f_sem.at[1, kind, off + far], partner
            ).wait_recv()

    def halo_rows(hk, col):
        return kv.at[hk, pl.ds(pl.multiple_of(HALO + col * TOK, 16), TOK)]

    def halo_copy(kind, src, hk, col, peer):
        return remote(src, halo_rows(hk, col), hs_sem.at[kind, hk], hr_sem.at[col, hk], peer)

    def own_rows(hk):
        return kv.at[hk, OWN:HALO]

    def halo_sends(hk):
        return (
            halo_copy(0, own_rows(hk), hk, 1, right),
            halo_copy(1, own_rows(hk), hk, 4, left),
            halo_copy(2, own_rows(hk), hk, 2 + core, partner),
        )

    def forwards(hk):
        return (
            halo_copy(5, halo_rows(hk, 4 - 3 * core), hk, 5 - 5 * core, extra),
            halo_copy(3, halo_rows(hk, 1), hk, 2 * core, partner),
            halo_copy(4, halo_rows(hk, 4), hk, 3 + 2 * core, partner),
        )

    def halo_wait(hk, col):
        halo_copy(0, own_rows(hk), hk, col, right).wait_recv()

    def halo_start(hk):
        for copy in halo_sends(hk):
            copy.start()

    def halo_forward(hk):
        halo_wait(hk, 1)
        halo_wait(hk, 4)
        for copy in forwards(hk):
            copy.start()

    position = lax.broadcasted_iota(jnp.int32, (1, PAD - OWN), 1) + OWN
    bias = jnp.where(position >= KEYS, NEG, 0.0)
    for col in range(2 * REACH):
        edge = HALO + col * TOK
        closed = jnp.where(pattern_ref[0, col] != 0, 0.0, NEG)
        bias = bias + jnp.where((position >= edge) & (position < edge + TOK), closed, 0.0)
    scale = HD ** -0.5 * math.log2(math.e)

    def segment(h, first, last):
        q = q2[h]
        peak = jnp.full((TOK, HD), NEG, jnp.float32)
        tiles = range(first, last, TILE)
        for row in tiles:
            keys = kv[2 * h, row : row + TILE, :]
            sc = lax.dot_general(
                q, jnp.concatenate([keys, keys], axis=1), (((1,), (1,)), ((), ())),
                preferred_element_type=jnp.float32,
            )
            if row + TILE > HALO:
                sc = sc + bias[:, row - OWN : row - OWN + TILE]
            scores[:, row - first : row - first + TILE] = sc
            peak = jnp.maximum(peak, jnp.maximum(sc[:, :HD], sc[:, HD:]))
        top = jnp.max(peak, axis=1, keepdims=True)
        total = jnp.zeros((TOK, HD), jnp.float32)
        acc = jnp.zeros((TOK, HD), jnp.float32)
        for row in tiles:
            w = jnp.exp2(scores[:, row - first : row - first + TILE] - top)
            total = total + (w[:, :HD] + w[:, HD:])
            acc = acc + jnp.dot(
                w.astype(BF), kv[2 * h + 1, row : row + TILE, :], preferred_element_type=jnp.float32
            )
        return top, jnp.sum(total, axis=1, keepdims=True), acc

    def scale_queries():
        query_load.wait()
        for h in range(LH):
            exact = qb[:, h * HD : (h + 1) * HD].astype(jnp.float32) * scale
            upper = exact.astype(BF)
            q2[h, :, :HD] = upper
            q2[h, :, HD:] = (exact - upper.astype(jnp.float32)).astype(BF)

    def near_part(h):
        for col in range(2 * REACH):
            if col not in (1, 4):
                halo_wait(2 * h, col)
                halo_wait(2 * h + 1, col)
        top, total, acc = segment(h, OWN, PAD)
        top1[h] = top
        total1[h] = total
        acc1[h] = acc

    def joined(h, first, last):
        top, total, acc = segment(h, first, last)
        best = jnp.maximum(top, top1[h])
        new = jnp.exp2(top - best)
        old = jnp.exp2(top1[h] - best)
        return best, total * new + total1[h] * old, acc * new + acc1[h] * old

    def fixed_part():
        fixed_finish()
        shared(1)
        for h in range(LH):
            best, total, acc = joined(h, 2 * REF, OWN)
            top1[h] = best
            total1[h] = total
            acc1[h] = acc

    def last_part(h):
        best, total, acc = joined(h, 0, 2 * REF)
        att[:, h * HD : (h + 1) * HD] = (acc / total).astype(BF)

    source = (pz == 0) & (py == 0)
    heads = range(LH)
    groups = range(GROUPS)
    step_actions = {
        "own": halo_start, "on": halo_forward, "near": near_part, "spread": fixed_spread,
        "here": fixed_here, "fixed": fixed_start, "fixed_part": fixed_part, "query": scale_queries,
    }
    for g in groups:
        swap(g).start()

    @pl.when(source)
    def _():
        for q in range(1, NZ):
            fixed_copy(q).start()
        fixed_rows(0)[...] = kv[:, OWN : OWN + PIECE, :]

    halo_start(0)
    halo_start(1)
    query_load.start()
    for load in weight_loads:
        load.start()
    for j in range(far):
        for g in groups:
            if j == 0:
                swap(g).wait_recv()
                mine[PER * g : PER * g + PER] = mine[PER * g : PER * g + PER] + mrecv[PER * g : PER * g + PER]
                ps[0, g] = mine_rows(g, pz + far)
                p_copy(0, g).start()
                if near > 0:
                    ss[0, g] = mine_rows(g, pz - near)
                    s_copy(0, g).start()
            else:
                p_copy(j - 1, g).wait_recv()
                ps[j, g] = mine_rows(g, pz + far - j) + pr[j - 1, g]
                p_copy(j, g).start()
                if j < near:
                    s_copy(j - 1, g).wait_recv()
                    ss[j, g] = mine_rows(g, pz - near + j) + sr[j - 1, g]
                    s_copy(j, g).start()
        for action in PACE[j]:
            step_actions[action[0]](*action[1:])
    for g in groups:
        total = mine_rows(g, pz)
        if near > 0:
            s_copy(near - 1, g).wait_recv()
            total = total + sr[near - 1, g]
        p_copy(far - 1, g).wait_recv()
        ysend[PER * g : PER * g + PER] = total + pr[far - 1, g]
        for d in range(1, NY):
            y_copy(d, g).start()
    for action in PACE[far]:
        step_actions[action[0]](*action[1:])
    for g in groups:
        total = ysend[PER * g : PER * g + PER]
        for d in range(1, NY):
            y_copy(d, g).wait_recv()
            total = total + yr[d - 1, g]
        piece(g, pz)[...] = total
        around(0, g).start()
        if near > 0:
            back(0, g).start()
        share(0, 0).start()
    for action in PACE[far + 1]:
        step_actions[action[0]](*action[1:])
    for j in range(1, far):
        for g in groups:
            around_arrived(j - 1, g)
            around(j, g).start()
            share(0, -j).start()
            if j <= near:
                back_arrived(j - 1, g)
                share(0, j).start()
            if j < near:
                back(j, g).start()
        for action in PACE[far + 1 + j]:
            step_actions[action[0]](*action[1:])
    for g in groups:
        around_arrived(far - 1, g)
        share(0, -far).start()
    for action in PACE[2 * far + 1]:
        step_actions[action[0]](*action[1:])
    shared(0)
    for h in heads:
        last_part(h)
    for load in weight_loads:
        load.wait()

    def project(b):
        p[b] = jnp.dot(att[...], wb[b], preferred_element_type=jnp.float32).astype(BF)

    def head_copy(kind, i, src, dst, peer):
        return pltpu.make_async_remote_copy(
            src_ref=src, dst_ref=dst, send_sem=mix_s.at[kind, i], recv_sem=mix_r.at[kind, i],
            device_id={"head": peer}, device_id_type=MESH,
        )

    def cross(c):
        return pltpu.make_async_remote_copy(
            src_ref=ty.at[c], dst_ref=ry.at[c], send_sem=c_sem.at[0, c], recv_sem=c_sem.at[1, c],
            device_id={"head": pair}, device_id_type=MESH,
        )

    part = TOK // PARTS
    half = part // 2
    items = [(which, c) for which in (1 - side, side) for c in range(PARTS)]
    rows = [(slice(c * part, c * part + half), slice(c * part + half, (c + 1) * part)) for c in range(PARTS)]
    first, direct, second = [], [], []
    for i, (which, c) in enumerate(items):
        upper, lower = rows[c]
        first.append((
            head_copy(0, i, p.at[xo * 2 + which, upper], r1p.at[i], nxt),
            head_copy(1, i, p.at[xo * 2 + which, lower], r1m.at[i], prv),
        ))
        direct.append((
            head_copy(2, i, p.at[xn * 2 + which, lower], r2p.at[i, half:], nxt),
            head_copy(3, i, p.at[xp * 2 + which, upper], r2m.at[i, :half], prv),
        ))
        second.append((
            head_copy(4, i, t2p.at[i], r2p.at[i, :half], nxt),
            head_copy(5, i, t2m.at[i], r2m.at[i, half:], prv),
        ))

    def pass_on(i):
        which, c = items[i]
        upper, lower = rows[c]
        first[i][0].wait_recv()
        t2p[i] = p[xn * 2 + which, upper] + r1p[i]
        second[i][0].start()
        first[i][1].wait_recv()
        t2m[i] = p[xp * 2 + which, lower] + r1m[i]
        second[i][1].start()

    def collect(i):
        which, c = items[i]
        for copy in direct[i] + second[i]:
            copy.wait_recv()
        return (
            p[x * 2 + which, c * part : (c + 1) * part].astype(jnp.float32)
            + r2p[i].astype(jnp.float32)
            + r2m[i].astype(jnp.float32)
        )

    def launch(phase):
        which = items[phase * PARTS][0]
        todo = range(phase * PARTS, (phase + 1) * PARTS)
        project(xo * 2 + which)
        for i in todo:
            for copy in first[i]:
                copy.start()
        project(xn * 2 + which)
        project(xp * 2 + which)
        for i in todo:
            for copy in direct[i]:
                copy.start()

    launch(0)
    for i in range(PARTS):
        pass_on(i)
    launch(1)
    project(x * 2 + 1 - side)
    for c in range(PARTS):
        ty[c] = collect(c).astype(BF)
        cross(c).start()
    project(x * 2 + side)
    for i in range(PARTS, 2 * PARTS):
        pass_on(i)
    for kind in range(2):
        for off in range(-far, near + 1):
            share(kind, off).wait_send()
    for g in groups:
        swap(g).wait_send()
        for j in range(far):
            p_copy(j, g).wait_send()
            around(j, g).wait_send()
        for j in range(near):
            s_copy(j, g).wait_send()
            back(j, g).wait_send()
        for d in range(1, NY):
            y_copy(d, g).wait_send()
    for j in range(far):
        fixed_around(j).wait_send()
    for j in range(near):
        fixed_back(j).wait_send()
    for hk in range(HK):
        for copy in halo_sends(hk) + forwards(hk):
            copy.wait_send()

    @pl.when(py == 0)
    def _():
        for d in range(1, NY):
            y_fixed(d).wait_send()

    @pl.when(source)
    def _():
        for q in range(1, NZ):
            fixed_copy(q).wait_send()
    for c in range(PARTS):
        total = collect(PARTS + c)
        cross(c).wait_recv()
        out[c * part : (c + 1) * part, :] = (total + ry[c].astype(jnp.float32)).astype(BF)

    for i in range(2 * PARTS):
        for copy in first[i] + direct[i] + second[i]:
            copy.wait_send()
    for c in range(PARTS):
        cross(c).wait_send()


def layer(owners, pattern, q, k, v, w):
    dma = pltpu.SemaphoreType.DMA
    width = LH * HD
    whole = pltpu.VMEM((HK, REF, HD), BF)
    hop = pltpu.VMEM((NZ // 2, GROUPS, PER, PIECE, HD), BF)
    part = TOK // PARTS
    halves = pltpu.VMEM((2 * PARTS, part // 2, width), BF)
    fulls = pltpu.VMEM((2 * PARTS, part, width), BF)
    pairs = pltpu.VMEM((PARTS, part, width), BF)
    column = pltpu.VMEM((LH, TOK, 1), jnp.float32)
    hbm = pl.BlockSpec(memory_space=pl.ANY)
    return pl.pallas_call(
        layer_kernel,
        out_shape=jax.ShapeDtypeStruct((TOK, width), BF),
        in_specs=[SMEM, SMEM, hbm, hbm, hbm, hbm],
        out_specs=VMEM,
        scratch_shapes=[
            pltpu.VMEM((HK, PAD, HD), BF), pltpu.VMEM((TOK, width), BF),
            pltpu.VMEM((LH, TOK, 2 * HD), BF),
            pltpu.VMEM((2 * NX, width, width), BF),
            whole, whole, whole, hop, hop, hop, hop,
            pltpu.VMEM((HK, PIECE, HD), BF), pltpu.VMEM((NY - 1, GROUPS, PER, PIECE, HD), BF),
            pltpu.VMEM((TOK, PAD - OWN), jnp.float32), pltpu.VMEM((TOK, width), BF),
            pltpu.VMEM((LH, TOK, HD), jnp.float32), column, column,
            pltpu.VMEM((2 * NX, TOK, width), BF),
            halves, halves, halves, halves, fulls, fulls, pairs, pairs,
            dma((6, HK)), dma((6, HK)), dma((2, GROUPS)), dma((2, NZ // 2, GROUPS)), dma((2, NZ // 2, GROUPS)),
            dma((2, NZ)), dma((2, NY, GROUPS)), dma((2, NY)),
            dma((2, NZ // 2, GROUPS)), dma((2, NZ // 2, GROUPS)), dma((2, NZ // 2)), dma((2, NZ // 2)), dma((2, 2, NZ)),
            dma((HK,)), dma((2 * NX,)), dma, dma((6, 2 * PARTS)), dma((6, 2 * PARTS)), dma((2, PARTS)),
        ],
        compiler_params=pltpu.CompilerParams(
            collective_id=0, has_side_effects=True, vmem_limit_bytes=56 << 20
        ),
        name="layer",
    )(owners, pattern, q, k, v, w)


def body(query_rows, key_rows, value_rows, pattern, owners, out_weight):
    return layer(owners, pattern, query_rows, key_rows, value_rows, out_weight)


def solution(mesh):
    return jax.shard_map(
        body,
        mesh=mesh,
        in_specs=(
            P("seq", "head"),
            P("seq", "head"),
            P("seq", "head"),
            P("seq", None),
            P(),
            P("head", None),
        ),
        out_specs=P("seq", "head"),
        check_vma=False,
    )
```

```python
import math

import jax
import jax.numpy as jnp
from jax import lax
from jax.experimental import pallas as pl
from jax.experimental.pallas import tpu as pltpu
from jax.sharding import PartitionSpec as P

MESH = pl.DeviceIdType.MESH
HD = 128
LH = 3
TOK = 320
REF = 256
REACH = 3
NZ = 8
NY = 4
NX = 4
HK = 2 * LH
PIECE = REF // NZ
OWN = 4 * REF
HALO = OWN + TOK
KEYS = HALO + 2 * REACH * TOK
PAD = -(-KEYS // 256) * 256
NEG = -1e30
TILE = 256
GROUPS = 1
PER = HK // GROUPS
PARTS = 2
PACE = (
    (("own", 2), ("spread",)),
    (("own", 3),),
    (("own", 4), ("here",), ("fixed", 0)),
    (("own", 5), ("fixed", 1), ("on", 0), ("on", 1)),
    (("fixed", 2), ("on", 2), ("on", 3), ("query",), ("near", 0)),
    (("fixed", 3), ("on", 4)),
    (("on", 5), ("near", 1)),
    (("near", 2),),
    (("fixed_part",),),
    (),
)
VMEM = pl.BlockSpec(memory_space=pltpu.VMEM)
SMEM = pl.BlockSpec(memory_space=pltpu.SMEM)
BF = jnp.bfloat16


def layer_kernel(
    owners_ref, pattern_ref, q_hbm, k_hbm, v_hbm, w_hbm, out,
    kv, qb, q2, wb, mine, msend, mrecv, ps, pr, ss, sr, ysend, yr,
    scores, att, acc1, top1, total1, p, r1p, r1m, t2p, t2m, r2p, r2m, ty, ry,
    hs_sem, hr_sem, m_sem, p_sem, s_sem, x_sem, y_sem, ys_sem, a_sem, b_sem, fa_sem, fb_sem, f_sem,
    in_sem, w_sem, q_sem, mix_s, mix_r, c_sem,
):
    s = lax.axis_index("seq")
    head = lax.axis_index("head")
    x = head // 2
    side = lax.rem(head, 2)
    xn = lax.rem(x + 1, NX)
    xp = lax.rem(x + NX - 1, NX)
    xo = lax.rem(x + 2, NX)
    nxt = xn * 2 + side
    prv = xp * 2 + side
    pair = x * 2 + 1 - side
    width = LH * HD
    n = 2 * NZ * NY
    core = lax.rem(s, 2)
    z = lax.rem(s // 2, NZ)
    y = s // (2 * NZ)
    step = 1 - 2 * core
    pz = jnp.where(core == 0, z, NZ - 1 - z)
    py = jnp.where(core == 0, y, NY - 1 - y)
    right = lax.rem(s + 2, n)
    left = lax.rem(s - 2 + n, n)
    partner = s + step
    extra = lax.rem(s - step + n, n)

    def at(yy, zz):
        zz = lax.rem(zz + NZ, NZ)
        yy = lax.rem(yy + NY, NY)
        zz = jnp.where(core == 0, zz, NZ - 1 - zz)
        yy = jnp.where(core == 0, yy, NY - 1 - yy)
        return (yy * NZ + zz) * 2 + core

    far, near = NZ // 2, NZ // 2 - 1
    ahead = at(py, pz + 1)
    behind = at(py, pz - 1)

    loads = []
    for h in range(LH):
        for i, ref in enumerate((k_hbm, v_hbm)):
            loads.append(pltpu.make_async_copy(
                ref.at[:, h * HD : (h + 1) * HD], kv.at[2 * h + i, OWN:HALO], in_sem.at[2 * h + i]
            ))
            loads[-1].start()

    barrier = pltpu.get_barrier_semaphore()
    peers = [partner, right, left, extra]
    peers += [at(py, pz + d) for d in range(1, NZ)]
    peers += [at(py + d, pz) for d in range(1, NY)]
    for peer in peers:
        pl.semaphore_signal(barrier, inc=1, device_id={"seq": peer}, device_id_type=MESH)
    for peer in (nxt, prv, pair):
        pl.semaphore_signal(barrier, inc=1, device_id={"head": peer}, device_id_type=MESH)

    query_load = pltpu.make_async_copy(q_hbm, qb, q_sem)
    weight_loads = [
        pltpu.make_async_copy(w_hbm.at[:, b * width : (b + 1) * width], wb.at[b], w_sem.at[b])
        for b in range(2 * NX)
    ]
    if PAD > KEYS:
        kv[:, KEYS:PAD, :] = jnp.zeros((HK, PAD - KEYS, HD), BF)

    low = jnp.int32(n)
    high = jnp.int32(-1)
    for i in range(4):
        o = owners_ref[i]
        low = jnp.minimum(low, jnp.where(o == 0, n, o))
        high = jnp.maximum(high, jnp.where(o == n - 1, -1, o))
    wanted = jnp.where(core == 0, low, high)
    given = jnp.where(core == 0, high, low)
    keep = jnp.where(wanted == s, 1.0, 0.0).astype(BF)
    give = jnp.where(given == s, 1.0, 0.0).astype(BF)
    for hk in range(HK):
        loads[hk].wait()
        block = kv[hk, OWN : OWN + REF, :]
        mine[hk] = block * keep
        msend[hk] = block * give

    pl.semaphore_wait(barrier, len(peers) + 3)

    def remote(src, dst, send, recv, peer):
        return pltpu.make_async_remote_copy(
            src_ref=src, dst_ref=dst, send_sem=send, recv_sem=recv,
            device_id={"seq": peer}, device_id_type=MESH,
        )

    def planes(ref, g):
        return ref.at[PER * g : PER * g + PER]

    def swap(g):
        return remote(planes(msend, g), planes(mrecv, g), m_sem.at[0, g], m_sem.at[1, g], partner)

    def p_copy(j, g):
        return remote(ps.at[j, g], pr.at[j, g], p_sem.at[0, j, g], p_sem.at[1, j, g], ahead)

    def s_copy(j, g):
        return remote(ss.at[j, g], sr.at[j, g], s_sem.at[0, j, g], s_sem.at[1, j, g], behind)

    base = core * REF

    def piece(g, q):
        start = base + lax.rem(q + NZ, NZ) * PIECE
        return kv.at[PER * g : PER * g + PER, pl.ds(pl.multiple_of(start, PIECE), PIECE)]

    def mine_rows(g, q):
        start = lax.rem(q + NZ, NZ) * PIECE
        return mine[PER * g : PER * g + PER, pl.ds(pl.multiple_of(start, PIECE), PIECE), :]

    def fixed_rows(q):
        start = 2 * REF + base + lax.rem(q + NZ, NZ) * PIECE
        return kv.at[:, pl.ds(pl.multiple_of(start, PIECE), PIECE)]

    def fixed_copy(q):
        return remote(
            kv.at[:, OWN + q * PIECE : OWN + (q + 1) * PIECE], fixed_rows(q),
            x_sem.at[0, q], x_sem.at[1, 0], at(0, q),
        )

    def y_copy(d, g):
        return remote(planes(ysend, g), yr.at[d - 1, g], y_sem.at[0, d, g], y_sem.at[1, d, g], at(py + d, pz))

    def y_fixed(d):
        return remote(fixed_rows(pz), fixed_rows(pz), ys_sem.at[0, d], ys_sem.at[1, 0], at(py + d, pz))

    def around(j, g):
        part = piece(g, pz - j)
        return remote(part, part, a_sem.at[0, j, g], a_sem.at[1, j, g], ahead)

    def around_arrived(j, g):
        part = piece(g, pz - j - 1)
        remote(part, part, a_sem.at[0, j, g], a_sem.at[1, j, g], ahead).wait_recv()

    def back(j, g):
        part = piece(g, pz + j)
        return remote(part, part, b_sem.at[0, j, g], b_sem.at[1, j, g], behind)

    def back_arrived(j, g):
        part = piece(g, pz + j + 1)
        remote(part, part, b_sem.at[0, j, g], b_sem.at[1, j, g], behind).wait_recv()

    def fixed_around(j):
        part = fixed_rows(pz - j)
        return remote(part, part, fa_sem.at[0, j], fa_sem.at[1, j], ahead)

    def fixed_back(j):
        part = fixed_rows(pz + j)
        return remote(part, part, fb_sem.at[0, j], fb_sem.at[1, j], behind)

    def fixed_start(j):
        if j > 0:
            part = fixed_rows(pz - j)
            remote(part, part, fa_sem.at[0, j - 1], fa_sem.at[1, j - 1], ahead).wait_recv()
        fixed_around(j).start()
        share(1, -j).start()
        if j <= near and j > 0:
            part = fixed_rows(pz + j)
            remote(part, part, fb_sem.at[0, j - 1], fb_sem.at[1, j - 1], behind).wait_recv()
            share(1, j).start()
        if j < near:
            fixed_back(j).start()

    def fixed_finish():
        part = fixed_rows(pz - far)
        remote(part, part, fa_sem.at[0, far - 1], fa_sem.at[1, far - 1], ahead).wait_recv()
        share(1, -far).start()

    def fixed_spread():
        @pl.when(py == 0)
        def _():
            @pl.when(pz > 0)
            def _():
                part = fixed_rows(pz)
                remote(part, part, x_sem.at[0, 0], x_sem.at[1, 0], ahead).wait_recv()

            for d in range(1, NY):
                y_fixed(d).start()

    def fixed_here():
        @pl.when(py > 0)
        def _():
            part = fixed_rows(pz)
            remote(part, part, ys_sem.at[0, 0], ys_sem.at[1, 0], ahead).wait_recv()

    def share(kind, off):
        start = (2 * kind + core) * REF + lax.rem(pz + off + NZ, NZ) * PIECE
        part = kv.at[:, pl.ds(pl.multiple_of(start, PIECE), PIECE)]
        return remote(part, part, f_sem.at[0, kind, off + far], f_sem.at[1, kind, off + far], partner)

    def shared(kind):
        for off in range(-far, near + 1):
            start = (2 * kind + 1 - core) * REF + lax.rem(2 * NZ - 1 - pz + off, NZ) * PIECE
            part = kv.at[:, pl.ds(pl.multiple_of(start, PIECE), PIECE)]
            remote(
                part, part, f_sem.at[0, kind, off + far], f_sem.at[1, kind, off + far], partner
            ).wait_recv()

    def halo_rows(hk, col):
        return kv.at[hk, pl.ds(pl.multiple_of(HALO + col * TOK, 16), TOK)]

    def halo_copy(kind, src, hk, col, peer):
        return remote(src, halo_rows(hk, col), hs_sem.at[kind, hk], hr_sem.at[col, hk], peer)

    def own_rows(hk):
        return kv.at[hk, OWN:HALO]

    def halo_sends(hk):
        return (
            halo_copy(0, own_rows(hk), hk, 1, right),
            halo_copy(1, own_rows(hk), hk, 4, left),
            halo_copy(2, own_rows(hk), hk, 2 + core, partner),
        )

    def forwards(hk):
        return (
            halo_copy(5, halo_rows(hk, 4 - 3 * core), hk, 5 - 5 * core, extra),
            halo_copy(3, halo_rows(hk, 1), hk, 2 * core, partner),
            halo_copy(4, halo_rows(hk, 4), hk, 3 + 2 * core, partner),
        )

    def halo_wait(hk, col):
        halo_copy(0, own_rows(hk), hk, col, right).wait_recv()

    def halo_start(hk):
        for copy in halo_sends(hk):
            copy.start()

    def halo_forward(hk):
        halo_wait(hk, 1)
        halo_wait(hk, 4)
        for copy in forwards(hk):
            copy.start()

    position = lax.broadcasted_iota(jnp.int32, (1, PAD - OWN), 1) + OWN
    bias = jnp.where(position >= KEYS, NEG, 0.0)
    for col in range(2 * REACH):
        edge = HALO + col * TOK
        closed = jnp.where(pattern_ref[0, col] != 0, 0.0, NEG)
        bias = bias + jnp.where((position >= edge) & (position < edge + TOK), closed, 0.0)
    scale = HD ** -0.5 * math.log2(math.e)

    def segment(h, first, last, low=0, high=TOK):
        q = q2[h, low:high]
        peak = jnp.full((high - low, HD), NEG, jnp.float32)
        tiles = range(first, last, TILE)
        for row in tiles:
            keys = kv[2 * h, row : row + TILE, :]
            sc = lax.dot_general(
                q, jnp.concatenate([keys, keys], axis=1), (((1,), (1,)), ((), ())),
                preferred_element_type=jnp.float32,
            )
            if row + TILE > HALO:
                sc = sc + bias[:, row - OWN : row - OWN + TILE]
            scores[low:high, row - first : row - first + TILE] = sc
            peak = jnp.maximum(peak, jnp.maximum(sc[:, :HD], sc[:, HD:]))
        top = jnp.max(peak, axis=1, keepdims=True)
        total = jnp.zeros((high - low, HD), jnp.float32)
        acc = jnp.zeros((high - low, HD), jnp.float32)
        for row in tiles:
            w = jnp.exp2(scores[low:high, row - first : row - first + TILE] - top)
            total = total + (w[:, :HD] + w[:, HD:])
            acc = acc + jnp.dot(
                w.astype(BF), kv[2 * h + 1, row : row + TILE, :], preferred_element_type=jnp.float32
            )
        return top, jnp.sum(total, axis=1, keepdims=True), acc

    def scale_queries():
        query_load.wait()
        for h in range(LH):
            exact = qb[:, h * HD : (h + 1) * HD].astype(jnp.float32) * scale
            upper = exact.astype(BF)
            q2[h, :, :HD] = upper
            q2[h, :, HD:] = (exact - upper.astype(jnp.float32)).astype(BF)

    def near_part(h):
        for col in range(2 * REACH):
            if col not in (1, 4):
                halo_wait(2 * h, col)
                halo_wait(2 * h + 1, col)
        top, total, acc = segment(h, OWN, PAD)
        top1[h] = top
        total1[h] = total
        acc1[h] = acc

    def joined(h, first, last, low=0, high=TOK):
        top, total, acc = segment(h, first, last, low, high)
        before = top1[h, low:high]
        best = jnp.maximum(top, before)
        new = jnp.exp2(top - best)
        old = jnp.exp2(before - best)
        return best, total * new + total1[h, low:high] * old, acc * new + acc1[h, low:high] * old

    def fixed_part():
        fixed_finish()
        shared(1)
        for h in range(LH):
            best, total, acc = joined(h, 2 * REF, OWN)
            top1[h] = best
            total1[h] = total
            acc1[h] = acc

    def last_part(low, high):
        for h in range(LH):
            best, total, acc = joined(h, 0, 2 * REF, low, high)
            att[low:high, h * HD : (h + 1) * HD] = (acc / total).astype(BF)

    source = (pz == 0) & (py == 0)
    heads = range(LH)
    groups = range(GROUPS)
    step_actions = {
        "own": halo_start, "on": halo_forward, "near": near_part, "spread": fixed_spread,
        "here": fixed_here, "fixed": fixed_start, "fixed_part": fixed_part, "query": scale_queries,
    }
    for g in groups:
        swap(g).start()

    @pl.when(source)
    def _():
        for q in range(1, NZ):
            fixed_copy(q).start()
        fixed_rows(0)[...] = kv[:, OWN : OWN + PIECE, :]

    halo_start(0)
    halo_start(1)
    query_load.start()
    for load in weight_loads:
        load.start()
    for j in range(far):
        for g in groups:
            if j == 0:
                swap(g).wait_recv()
                mine[PER * g : PER * g + PER] = mine[PER * g : PER * g + PER] + mrecv[PER * g : PER * g + PER]
                ps[0, g] = mine_rows(g, pz + far)
                p_copy(0, g).start()
                if near > 0:
                    ss[0, g] = mine_rows(g, pz - near)
                    s_copy(0, g).start()
            else:
                p_copy(j - 1, g).wait_recv()
                ps[j, g] = mine_rows(g, pz + far - j) + pr[j - 1, g]
                p_copy(j, g).start()
                if j < near:
                    s_copy(j - 1, g).wait_recv()
                    ss[j, g] = mine_rows(g, pz - near + j) + sr[j - 1, g]
                    s_copy(j, g).start()
        for action in PACE[j]:
            step_actions[action[0]](*action[1:])
    for g in groups:
        total = mine_rows(g, pz)
        if near > 0:
            s_copy(near - 1, g).wait_recv()
            total = total + sr[near - 1, g]
        p_copy(far - 1, g).wait_recv()
        ysend[PER * g : PER * g + PER] = total + pr[far - 1, g]
        for d in range(1, NY):
            y_copy(d, g).start()
    for action in PACE[far]:
        step_actions[action[0]](*action[1:])
    for g in groups:
        total = ysend[PER * g : PER * g + PER]
        for d in range(1, NY):
            y_copy(d, g).wait_recv()
            total = total + yr[d - 1, g]
        piece(g, pz)[...] = total
        around(0, g).start()
        if near > 0:
            back(0, g).start()
        share(0, 0).start()
    for action in PACE[far + 1]:
        step_actions[action[0]](*action[1:])
    for j in range(1, far):
        for g in groups:
            around_arrived(j - 1, g)
            around(j, g).start()
            share(0, -j).start()
            if j <= near:
                back_arrived(j - 1, g)
                share(0, j).start()
            if j < near:
                back(j, g).start()
        for action in PACE[far + 1 + j]:
            step_actions[action[0]](*action[1:])
    for g in groups:
        around_arrived(far - 1, g)
        share(0, -far).start()
    for action in PACE[2 * far + 1]:
        step_actions[action[0]](*action[1:])
    shared(0)
    for load in weight_loads:
        load.wait()

    def project(b, low=0, high=TOK):
        p[b, low:high] = jnp.dot(
            att[low:high], wb[b], preferred_element_type=jnp.float32
        ).astype(BF)

    def head_copy(kind, i, src, dst, peer):
        return pltpu.make_async_remote_copy(
            src_ref=src, dst_ref=dst, send_sem=mix_s.at[kind, i], recv_sem=mix_r.at[kind, i],
            device_id={"head": peer}, device_id_type=MESH,
        )

    def cross(c):
        return pltpu.make_async_remote_copy(
            src_ref=ty.at[c], dst_ref=ry.at[c], send_sem=c_sem.at[0, c], recv_sem=c_sem.at[1, c],
            device_id={"head": pair}, device_id_type=MESH,
        )

    part = TOK // PARTS
    half = part // 2
    items = [(which, c) for which in (1 - side, side) for c in range(PARTS)]
    rows = [(slice(c * part, c * part + half), slice(c * part + half, (c + 1) * part)) for c in range(PARTS)]
    first, direct, second = [], [], []
    for i, (which, c) in enumerate(items):
        upper, lower = rows[c]
        first.append((
            head_copy(0, i, p.at[xo * 2 + which, upper], r1p.at[i], nxt),
            head_copy(1, i, p.at[xo * 2 + which, lower], r1m.at[i], prv),
        ))
        direct.append((
            head_copy(2, i, p.at[xn * 2 + which, lower], r2p.at[i, half:], nxt),
            head_copy(3, i, p.at[xp * 2 + which, upper], r2m.at[i, :half], prv),
        ))
        second.append((
            head_copy(4, i, t2p.at[i], r2p.at[i, :half], nxt),
            head_copy(5, i, t2m.at[i], r2m.at[i, half:], prv),
        ))

    def pass_on(i):
        which, c = items[i]
        upper, lower = rows[c]
        first[i][0].wait_recv()
        t2p[i] = p[xn * 2 + which, upper] + r1p[i]
        second[i][0].start()
        first[i][1].wait_recv()
        t2m[i] = p[xp * 2 + which, lower] + r1m[i]
        second[i][1].start()

    def collect(i):
        which, c = items[i]
        for copy in direct[i] + second[i]:
            copy.wait_recv()
        return (
            p[x * 2 + which, c * part : (c + 1) * part].astype(jnp.float32)
            + r2p[i].astype(jnp.float32)
            + r2m[i].astype(jnp.float32)
        )

    def begin(copies):
        for copy in copies:
            copy.start()

    other = 1 - side
    for c in range(PARTS):
        span = (c * part, (c + 1) * part)
        last_part(*span)
        project(xo * 2 + other, *span)
        begin(first[c])
        if c > 0:
            pass_on(c - 1)
        project(xn * 2 + other, *span)
        project(xp * 2 + other, *span)
        begin(direct[c])
    project(xo * 2 + side)
    for i in range(PARTS, 2 * PARTS):
        begin(first[i])
    pass_on(PARTS - 1)
    project(xn * 2 + side)
    project(xp * 2 + side)
    for i in range(PARTS, 2 * PARTS):
        begin(direct[i])
    project(x * 2 + other)
    for c in range(PARTS):
        ty[c] = collect(c).astype(BF)
        cross(c).start()
    project(x * 2 + side)
    for i in range(PARTS, 2 * PARTS):
        pass_on(i)
    for kind in range(2):
        for off in range(-far, near + 1):
            share(kind, off).wait_send()
    for g in groups:
        swap(g).wait_send()
        for j in range(far):
            p_copy(j, g).wait_send()
            around(j, g).wait_send()
        for j in range(near):
            s_copy(j, g).wait_send()
            back(j, g).wait_send()
        for d in range(1, NY):
            y_copy(d, g).wait_send()
    for j in range(far):
        fixed_around(j).wait_send()
    for j in range(near):
        fixed_back(j).wait_send()
    for hk in range(HK):
        for copy in halo_sends(hk) + forwards(hk):
            copy.wait_send()

    @pl.when(py == 0)
    def _():
        for d in range(1, NY):
            y_fixed(d).wait_send()

    @pl.when(source)
    def _():
        for q in range(1, NZ):
            fixed_copy(q).wait_send()
    for c in range(PARTS):
        total = collect(PARTS + c)
        cross(c).wait_recv()
        out[c * part : (c + 1) * part, :] = (total + ry[c].astype(jnp.float32)).astype(BF)

    for i in range(2 * PARTS):
        for copy in first[i] + direct[i] + second[i]:
            copy.wait_send()
    for c in range(PARTS):
        cross(c).wait_send()


def layer(owners, pattern, q, k, v, w):
    dma = pltpu.SemaphoreType.DMA
    width = LH * HD
    whole = pltpu.VMEM((HK, REF, HD), BF)
    hop = pltpu.VMEM((NZ // 2, GROUPS, PER, PIECE, HD), BF)
    part = TOK // PARTS
    halves = pltpu.VMEM((2 * PARTS, part // 2, width), BF)
    fulls = pltpu.VMEM((2 * PARTS, part, width), BF)
    pairs = pltpu.VMEM((PARTS, part, width), BF)
    column = pltpu.VMEM((LH, TOK, 1), jnp.float32)
    hbm = pl.BlockSpec(memory_space=pl.ANY)
    return pl.pallas_call(
        layer_kernel,
        out_shape=jax.ShapeDtypeStruct((TOK, width), BF),
        in_specs=[SMEM, SMEM, hbm, hbm, hbm, hbm],
        out_specs=VMEM,
        scratch_shapes=[
            pltpu.VMEM((HK, PAD, HD), BF), pltpu.VMEM((TOK, width), BF),
            pltpu.VMEM((LH, TOK, 2 * HD), BF),
            pltpu.VMEM((2 * NX, width, width), BF),
            whole, whole, whole, hop, hop, hop, hop,
            pltpu.VMEM((HK, PIECE, HD), BF), pltpu.VMEM((NY - 1, GROUPS, PER, PIECE, HD), BF),
            pltpu.VMEM((TOK, PAD - OWN), jnp.float32), pltpu.VMEM((TOK, width), BF),
            pltpu.VMEM((LH, TOK, HD), jnp.float32), column, column,
            pltpu.VMEM((2 * NX, TOK, width), BF),
            halves, halves, halves, halves, fulls, fulls, pairs, pairs,
            dma((6, HK)), dma((6, HK)), dma((2, GROUPS)), dma((2, NZ // 2, GROUPS)), dma((2, NZ // 2, GROUPS)),
            dma((2, NZ)), dma((2, NY, GROUPS)), dma((2, NY)),
            dma((2, NZ // 2, GROUPS)), dma((2, NZ // 2, GROUPS)), dma((2, NZ // 2)), dma((2, NZ // 2)), dma((2, 2, NZ)),
            dma((HK,)), dma((2 * NX,)), dma, dma((6, 2 * PARTS)), dma((6, 2 * PARTS)), dma((2, PARTS)),
        ],
        compiler_params=pltpu.CompilerParams(
            collective_id=0, has_side_effects=True, vmem_limit_bytes=56 << 20
        ),
        name="layer",
    )(owners, pattern, q, k, v, w)


def body(query_rows, key_rows, value_rows, pattern, owners, out_weight):
    return layer(owners, pattern, query_rows, key_rows, value_rows, out_weight)


def solution(mesh):
    return jax.shard_map(
        body,
        mesh=mesh,
        in_specs=(
            P("seq", "head"),
            P("seq", "head"),
            P("seq", "head"),
            P("seq", None),
            P(),
            P("head", None),
        ),
        out_specs=P("seq", "head"),
        check_vma=False,
    )
```

```python
import math

import jax
import jax.numpy as jnp
from jax import lax
from jax.experimental import pallas as pl
from jax.experimental.pallas import tpu as pltpu
from jax.sharding import PartitionSpec as P

MESH = pl.DeviceIdType.MESH
HD = 128
LH = 3
TOK = 320
REF = 256
REACH = 3
NZ = 8
NY = 4
NX = 4
HK = 2 * LH
PIECE = REF // NZ
OWN = 4 * REF
HALO = OWN + TOK
KEYS = HALO + 2 * REACH * TOK
PAD = -(-KEYS // 256) * 256
NEG = -1e30
TILE = 256
GROUPS = 1
PER = HK // GROUPS
PARTS = 2
PACE = (
    (("own", 2), ("spread",)),
    (("own", 3),),
    (("own", 4), ("here",), ("fixed", 0)),
    (("own", 5), ("fixed", 1), ("on", 0), ("on", 1)),
    (("fixed", 2), ("on", 2), ("on", 3), ("query",), ("near", 0)),
    (("fixed", 3), ("on", 4)),
    (("on", 5), ("near", 1)),
    (("near", 2),),
    (("fixed_part",),),
    (),
)
VMEM = pl.BlockSpec(memory_space=pltpu.VMEM)
SMEM = pl.BlockSpec(memory_space=pltpu.SMEM)
BF = jnp.bfloat16


def layer_kernel(
    owners_ref, pattern_ref, q_hbm, k_hbm, v_hbm, w_hbm, out,
    kv, qb, q2, wb, mine, msend, mrecv, ps, pr, ss, sr, ysend, yr,
    scores, att, acc1, top1, total1, p, r1p, r1m, t2p, t2m, r2p, r2m, ty, ry,
    hs_sem, hr_sem, m_sem, p_sem, s_sem, x_sem, y_sem, ys_sem, a_sem, b_sem, fa_sem, fb_sem, f_sem,
    in_sem, w_sem, q_sem, mix_s, mix_r, c_sem,
):
    s = lax.axis_index("seq")
    head = lax.axis_index("head")
    x = head // 2
    side = lax.rem(head, 2)
    xn = lax.rem(x + 1, NX)
    xp = lax.rem(x + NX - 1, NX)
    xo = lax.rem(x + 2, NX)
    nxt = xn * 2 + side
    prv = xp * 2 + side
    pair = x * 2 + 1 - side
    width = LH * HD
    n = 2 * NZ * NY
    core = lax.rem(s, 2)
    z = lax.rem(s // 2, NZ)
    y = s // (2 * NZ)
    step = 1 - 2 * core
    pz = jnp.where(core == 0, z, NZ - 1 - z)
    py = jnp.where(core == 0, y, NY - 1 - y)
    right = lax.rem(s + 2, n)
    left = lax.rem(s - 2 + n, n)
    partner = s + step
    extra = lax.rem(s - step + n, n)

    def at(yy, zz):
        zz = lax.rem(zz + NZ, NZ)
        yy = lax.rem(yy + NY, NY)
        zz = jnp.where(core == 0, zz, NZ - 1 - zz)
        yy = jnp.where(core == 0, yy, NY - 1 - yy)
        return (yy * NZ + zz) * 2 + core

    far, near = NZ // 2, NZ // 2 - 1
    ahead = at(py, pz + 1)
    behind = at(py, pz - 1)

    loads = []
    for h in range(LH):
        for i, ref in enumerate((k_hbm, v_hbm)):
            loads.append(pltpu.make_async_copy(
                ref.at[:, h * HD : (h + 1) * HD], kv.at[2 * h + i, OWN:HALO], in_sem.at[2 * h + i]
            ))
            loads[-1].start()

    barrier = pltpu.get_barrier_semaphore()
    peers = [partner, right, left, extra]
    peers += [at(py, pz + d) for d in range(1, NZ)]
    peers += [at(py + d, pz) for d in range(1, NY)]
    for peer in peers:
        pl.semaphore_signal(barrier, inc=1, device_id={"seq": peer}, device_id_type=MESH)
    for peer in (nxt, prv, pair):
        pl.semaphore_signal(barrier, inc=1, device_id={"head": peer}, device_id_type=MESH)

    query_load = pltpu.make_async_copy(q_hbm, qb, q_sem)
    weight_loads = [
        pltpu.make_async_copy(w_hbm.at[:, b * width : (b + 1) * width], wb.at[b], w_sem.at[b])
        for b in range(2 * NX)
    ]
    if PAD > KEYS:
        kv[:, KEYS:PAD, :] = jnp.zeros((HK, PAD - KEYS, HD), BF)

    low = jnp.int32(n)
    high = jnp.int32(-1)
    for i in range(4):
        o = owners_ref[i]
        low = jnp.minimum(low, jnp.where(o == 0, n, o))
        high = jnp.maximum(high, jnp.where(o == n - 1, -1, o))
    wanted = jnp.where(core == 0, low, high)
    given = jnp.where(core == 0, high, low)
    keep = jnp.where(wanted == s, 1.0, 0.0).astype(BF)
    give = jnp.where(given == s, 1.0, 0.0).astype(BF)
    for hk in range(HK):
        loads[hk].wait()
        block = kv[hk, OWN : OWN + REF, :]
        mine[hk] = block * keep
        msend[hk] = block * give

    pl.semaphore_wait(barrier, len(peers) + 3)

    def remote(src, dst, send, recv, peer):
        return pltpu.make_async_remote_copy(
            src_ref=src, dst_ref=dst, send_sem=send, recv_sem=recv,
            device_id={"seq": peer}, device_id_type=MESH,
        )

    def planes(ref, g):
        return ref.at[PER * g : PER * g + PER]

    def swap(g):
        return remote(planes(msend, g), planes(mrecv, g), m_sem.at[0, g], m_sem.at[1, g], partner)

    def p_copy(j, g):
        return remote(ps.at[j, g], pr.at[j, g], p_sem.at[0, j, g], p_sem.at[1, j, g], ahead)

    def s_copy(j, g):
        return remote(ss.at[j, g], sr.at[j, g], s_sem.at[0, j, g], s_sem.at[1, j, g], behind)

    base = core * REF

    def piece(g, q):
        start = base + lax.rem(q + NZ, NZ) * PIECE
        return kv.at[PER * g : PER * g + PER, pl.ds(pl.multiple_of(start, PIECE), PIECE)]

    def mine_rows(g, q):
        start = lax.rem(q + NZ, NZ) * PIECE
        return mine[PER * g : PER * g + PER, pl.ds(pl.multiple_of(start, PIECE), PIECE), :]

    def fixed_rows(q):
        start = 2 * REF + base + lax.rem(q + NZ, NZ) * PIECE
        return kv.at[:, pl.ds(pl.multiple_of(start, PIECE), PIECE)]

    def fixed_copy(q):
        return remote(
            kv.at[:, OWN + q * PIECE : OWN + (q + 1) * PIECE], fixed_rows(q),
            x_sem.at[0, q], x_sem.at[1, 0], at(0, q),
        )

    def y_copy(d, g):
        return remote(planes(ysend, g), yr.at[d - 1, g], y_sem.at[0, d, g], y_sem.at[1, d, g], at(py + d, pz))

    def y_fixed(d):
        return remote(fixed_rows(pz), fixed_rows(pz), ys_sem.at[0, d], ys_sem.at[1, 0], at(py + d, pz))

    def around(j, g):
        part = piece(g, pz - j)
        return remote(part, part, a_sem.at[0, j, g], a_sem.at[1, j, g], ahead)

    def around_arrived(j, g):
        part = piece(g, pz - j - 1)
        remote(part, part, a_sem.at[0, j, g], a_sem.at[1, j, g], ahead).wait_recv()

    def back(j, g):
        part = piece(g, pz + j)
        return remote(part, part, b_sem.at[0, j, g], b_sem.at[1, j, g], behind)

    def back_arrived(j, g):
        part = piece(g, pz + j + 1)
        remote(part, part, b_sem.at[0, j, g], b_sem.at[1, j, g], behind).wait_recv()

    def fixed_around(j):
        part = fixed_rows(pz - j)
        return remote(part, part, fa_sem.at[0, j], fa_sem.at[1, j], ahead)

    def fixed_back(j):
        part = fixed_rows(pz + j)
        return remote(part, part, fb_sem.at[0, j], fb_sem.at[1, j], behind)

    def fixed_start(j):
        if j > 0:
            part = fixed_rows(pz - j)
            remote(part, part, fa_sem.at[0, j - 1], fa_sem.at[1, j - 1], ahead).wait_recv()
        fixed_around(j).start()
        share(1, -j).start()
        if j <= near and j > 0:
            part = fixed_rows(pz + j)
            remote(part, part, fb_sem.at[0, j - 1], fb_sem.at[1, j - 1], behind).wait_recv()
            share(1, j).start()
        if j < near:
            fixed_back(j).start()

    def fixed_finish():
        part = fixed_rows(pz - far)
        remote(part, part, fa_sem.at[0, far - 1], fa_sem.at[1, far - 1], ahead).wait_recv()
        share(1, -far).start()

    def fixed_spread():
        @pl.when(py == 0)
        def _():
            @pl.when(pz > 0)
            def _():
                part = fixed_rows(pz)
                remote(part, part, x_sem.at[0, 0], x_sem.at[1, 0], ahead).wait_recv()

            for d in range(1, NY):
                y_fixed(d).start()

    def fixed_here():
        @pl.when(py > 0)
        def _():
            part = fixed_rows(pz)
            remote(part, part, ys_sem.at[0, 0], ys_sem.at[1, 0], ahead).wait_recv()

    def share(kind, off):
        start = (2 * kind + core) * REF + lax.rem(pz + off + NZ, NZ) * PIECE
        part = kv.at[:, pl.ds(pl.multiple_of(start, PIECE), PIECE)]
        return remote(part, part, f_sem.at[0, kind, off + far], f_sem.at[1, kind, off + far], partner)

    def shared(kind):
        for off in range(-far, near + 1):
            start = (2 * kind + 1 - core) * REF + lax.rem(2 * NZ - 1 - pz + off, NZ) * PIECE
            part = kv.at[:, pl.ds(pl.multiple_of(start, PIECE), PIECE)]
            remote(
                part, part, f_sem.at[0, kind, off + far], f_sem.at[1, kind, off + far], partner
            ).wait_recv()

    def halo_rows(hk, col):
        return kv.at[hk, pl.ds(pl.multiple_of(HALO + col * TOK, 16), TOK)]

    def halo_copy(kind, src, hk, col, peer):
        return remote(src, halo_rows(hk, col), hs_sem.at[kind, hk], hr_sem.at[col, hk], peer)

    def own_rows(hk):
        return kv.at[hk, OWN:HALO]

    def halo_sends(hk):
        return (
            halo_copy(0, own_rows(hk), hk, 1, right),
            halo_copy(1, own_rows(hk), hk, 4, left),
            halo_copy(2, own_rows(hk), hk, 2 + core, partner),
        )

    def forwards(hk):
        return (
            halo_copy(5, halo_rows(hk, 4 - 3 * core), hk, 5 - 5 * core, extra),
            halo_copy(3, halo_rows(hk, 1), hk, 2 * core, partner),
            halo_copy(4, halo_rows(hk, 4), hk, 3 + 2 * core, partner),
        )

    def halo_wait(hk, col):
        halo_copy(0, own_rows(hk), hk, col, right).wait_recv()

    def halo_start(hk):
        for copy in halo_sends(hk):
            copy.start()

    def halo_forward(hk):
        halo_wait(hk, 1)
        halo_wait(hk, 4)
        for copy in forwards(hk):
            copy.start()

    position = lax.broadcasted_iota(jnp.int32, (1, PAD - OWN), 1) + OWN
    bias = jnp.where(position >= KEYS, NEG, 0.0)
    for col in range(2 * REACH):
        edge = HALO + col * TOK
        closed = jnp.where(pattern_ref[0, col] != 0, 0.0, NEG)
        bias = bias + jnp.where((position >= edge) & (position < edge + TOK), closed, 0.0)
    scale = HD ** -0.5 * math.log2(math.e)

    def segment(h, first, last, low=0, high=TOK):
        q = q2[h, low:high]
        peak = jnp.full((high - low, HD), NEG, jnp.float32)
        tiles = range(first, last, TILE)
        for row in tiles:
            keys = kv[2 * h, row : row + TILE, :]
            sc = lax.dot_general(
                q, jnp.concatenate([keys, keys], axis=1), (((1,), (1,)), ((), ())),
                preferred_element_type=jnp.float32,
            )
            if row + TILE > HALO:
                sc = sc + bias[:, row - OWN : row - OWN + TILE]
            scores[low:high, row - first : row - first + TILE] = sc
            peak = jnp.maximum(peak, jnp.maximum(sc[:, :HD], sc[:, HD:]))
        top = jnp.max(peak, axis=1, keepdims=True)
        total = jnp.zeros((high - low, HD), jnp.float32)
        acc = jnp.zeros((high - low, HD), jnp.float32)
        for row in tiles:
            w = jnp.exp2(scores[low:high, row - first : row - first + TILE] - top)
            total = total + (w[:, :HD] + w[:, HD:])
            acc = acc + jnp.dot(
                w.astype(BF), kv[2 * h + 1, row : row + TILE, :], preferred_element_type=jnp.float32
            )
        return top, jnp.sum(total, axis=1, keepdims=True), acc

    def scale_queries():
        query_load.wait()
        for h in range(LH):
            exact = qb[:, h * HD : (h + 1) * HD].astype(jnp.float32) * scale
            upper = exact.astype(BF)
            q2[h, :, :HD] = upper
            q2[h, :, HD:] = (exact - upper.astype(jnp.float32)).astype(BF)

    def near_part(h):
        for col in range(2 * REACH):
            if col not in (1, 4):
                halo_wait(2 * h, col)
                halo_wait(2 * h + 1, col)
        top, total, acc = segment(h, OWN, PAD)
        top1[h] = top
        total1[h] = total
        acc1[h] = acc

    def joined(h, first, last, low=0, high=TOK):
        top, total, acc = segment(h, first, last, low, high)
        before = top1[h, low:high]
        best = jnp.maximum(top, before)
        new = jnp.exp2(top - best)
        old = jnp.exp2(before - best)
        return best, total * new + total1[h, low:high] * old, acc * new + acc1[h, low:high] * old

    def fixed_part():
        fixed_finish()
        shared(1)
        for h in range(LH):
            best, total, acc = joined(h, 2 * REF, OWN)
            top1[h] = best
            total1[h] = total
            acc1[h] = acc

    def last_part(low, high):
        for h in range(LH):
            best, total, acc = joined(h, 0, 2 * REF, low, high)
            att[low:high, h * HD : (h + 1) * HD] = (acc / total).astype(BF)

    source = (pz == 0) & (py == 0)
    heads = range(LH)
    groups = range(GROUPS)
    step_actions = {
        "own": halo_start, "on": halo_forward, "near": near_part, "spread": fixed_spread,
        "here": fixed_here, "fixed": fixed_start, "fixed_part": fixed_part, "query": scale_queries,
    }
    for g in groups:
        swap(g).start()

    @pl.when(source)
    def _():
        for q in range(1, NZ):
            fixed_copy(q).start()
        fixed_rows(0)[...] = kv[:, OWN : OWN + PIECE, :]

    halo_start(0)
    halo_start(1)
    query_load.start()
    for load in weight_loads:
        load.start()
    for j in range(far):
        for g in groups:
            if j == 0:
                swap(g).wait_recv()
                mine[PER * g : PER * g + PER] = mine[PER * g : PER * g + PER] + mrecv[PER * g : PER * g + PER]
                ps[0, g] = mine_rows(g, pz + far)
                p_copy(0, g).start()
                if near > 0:
                    ss[0, g] = mine_rows(g, pz - near)
                    s_copy(0, g).start()
            else:
                p_copy(j - 1, g).wait_recv()
                ps[j, g] = mine_rows(g, pz + far - j) + pr[j - 1, g]
                p_copy(j, g).start()
                if j < near:
                    s_copy(j - 1, g).wait_recv()
                    ss[j, g] = mine_rows(g, pz - near + j) + sr[j - 1, g]
                    s_copy(j, g).start()
        for action in PACE[j]:
            step_actions[action[0]](*action[1:])
    for g in groups:
        total = mine_rows(g, pz)
        if near > 0:
            s_copy(near - 1, g).wait_recv()
            total = total + sr[near - 1, g]
        p_copy(far - 1, g).wait_recv()
        ysend[PER * g : PER * g + PER] = total + pr[far - 1, g]
        for d in range(1, NY):
            y_copy(d, g).start()
    for action in PACE[far]:
        step_actions[action[0]](*action[1:])
    for g in groups:
        total = ysend[PER * g : PER * g + PER]
        for d in range(1, NY):
            y_copy(d, g).wait_recv()
            total = total + yr[d - 1, g]
        piece(g, pz)[...] = total
        around(0, g).start()
        if near > 0:
            back(0, g).start()
        share(0, 0).start()
    for action in PACE[far + 1]:
        step_actions[action[0]](*action[1:])
    for j in range(1, far):
        for g in groups:
            around_arrived(j - 1, g)
            around(j, g).start()
            share(0, -j).start()
            if j <= near:
                back_arrived(j - 1, g)
                share(0, j).start()
            if j < near:
                back(j, g).start()
        for action in PACE[far + 1 + j]:
            step_actions[action[0]](*action[1:])
    for g in groups:
        around_arrived(far - 1, g)
        share(0, -far).start()
    for action in PACE[2 * far + 1]:
        step_actions[action[0]](*action[1:])
    shared(0)
    for load in weight_loads:
        load.wait()

    def project(b, low=0, high=TOK):
        p[b, low:high] = jnp.dot(
            att[low:high], wb[b], preferred_element_type=jnp.float32
        ).astype(BF)

    def head_copy(kind, i, src, dst, peer):
        return pltpu.make_async_remote_copy(
            src_ref=src, dst_ref=dst, send_sem=mix_s.at[kind, i], recv_sem=mix_r.at[kind, i],
            device_id={"head": peer}, device_id_type=MESH,
        )

    def cross(c):
        return pltpu.make_async_remote_copy(
            src_ref=ty.at[c], dst_ref=ry.at[c], send_sem=c_sem.at[0, c], recv_sem=c_sem.at[1, c],
            device_id={"head": pair}, device_id_type=MESH,
        )

    part = TOK // PARTS
    half = part // 2
    items = [(which, c) for which in (1 - side, side) for c in range(PARTS)]
    rows = [(slice(c * part, c * part + half), slice(c * part + half, (c + 1) * part)) for c in range(PARTS)]
    first, direct, second = [], [], []
    for i, (which, c) in enumerate(items):
        upper, lower = rows[c]
        first.append((
            head_copy(0, i, p.at[xo * 2 + which, upper], r1p.at[i], nxt),
            head_copy(1, i, p.at[xo * 2 + which, lower], r1m.at[i], prv),
        ))
        direct.append((
            head_copy(2, i, p.at[xn * 2 + which, lower], r2p.at[i, half:], nxt),
            head_copy(3, i, p.at[xp * 2 + which, upper], r2m.at[i, :half], prv),
        ))
        second.append((
            head_copy(4, i, t2p.at[i], r2p.at[i, :half], nxt),
            head_copy(5, i, t2m.at[i], r2m.at[i, half:], prv),
        ))

    def pass_on(i):
        which, c = items[i]
        upper, lower = rows[c]
        first[i][0].wait_recv()
        t2p[i] = p[xn * 2 + which, upper] + r1p[i]
        second[i][0].start()
        first[i][1].wait_recv()
        t2m[i] = p[xp * 2 + which, lower] + r1m[i]
        second[i][1].start()

    def collect(i):
        which, c = items[i]
        for copy in direct[i] + second[i]:
            copy.wait_recv()
        return (
            p[x * 2 + which, c * part : (c + 1) * part].astype(jnp.float32)
            + r2p[i].astype(jnp.float32)
            + r2m[i].astype(jnp.float32)
        )

    def begin(copies):
        for copy in copies:
            copy.start()

    other = 1 - side
    for c in range(PARTS):
        span = (c * part, (c + 1) * part)
        last_part(*span)
        project(xo * 2 + other, *span)
        begin(first[c])
        if c > 0:
            pass_on(c - 1)
        project(xn * 2 + other, *span)
        project(xp * 2 + other, *span)
        begin(direct[c])
    project(x * 2 + other)
    project(xo * 2 + side)
    for i in range(PARTS, 2 * PARTS):
        begin(first[i])
    pass_on(PARTS - 1)
    ty[0] = collect(0).astype(BF)
    cross(0).start()
    project(xn * 2 + side)
    project(xp * 2 + side)
    for i in range(PARTS, 2 * PARTS):
        begin(direct[i])
    for c in range(1, PARTS):
        ty[c] = collect(c).astype(BF)
        cross(c).start()
    project(x * 2 + side)
    for i in range(PARTS, 2 * PARTS):
        pass_on(i)
    for kind in range(2):
        for off in range(-far, near + 1):
            share(kind, off).wait_send()
    for g in groups:
        swap(g).wait_send()
        for j in range(far):
            p_copy(j, g).wait_send()
            around(j, g).wait_send()
        for j in range(near):
            s_copy(j, g).wait_send()
            back(j, g).wait_send()
        for d in range(1, NY):
            y_copy(d, g).wait_send()
    for j in range(far):
        fixed_around(j).wait_send()
    for j in range(near):
        fixed_back(j).wait_send()
    for hk in range(HK):
        for copy in halo_sends(hk) + forwards(hk):
            copy.wait_send()

    @pl.when(py == 0)
    def _():
        for d in range(1, NY):
            y_fixed(d).wait_send()

    @pl.when(source)
    def _():
        for q in range(1, NZ):
            fixed_copy(q).wait_send()
    for c in range(PARTS):
        total = collect(PARTS + c)
        cross(c).wait_recv()
        out[c * part : (c + 1) * part, :] = (total + ry[c].astype(jnp.float32)).astype(BF)

    for i in range(2 * PARTS):
        for copy in first[i] + direct[i] + second[i]:
            copy.wait_send()
    for c in range(PARTS):
        cross(c).wait_send()


def layer(owners, pattern, q, k, v, w):
    dma = pltpu.SemaphoreType.DMA
    width = LH * HD
    whole = pltpu.VMEM((HK, REF, HD), BF)
    hop = pltpu.VMEM((NZ // 2, GROUPS, PER, PIECE, HD), BF)
    part = TOK // PARTS
    halves = pltpu.VMEM((2 * PARTS, part // 2, width), BF)
    fulls = pltpu.VMEM((2 * PARTS, part, width), BF)
    pairs = pltpu.VMEM((PARTS, part, width), BF)
    column = pltpu.VMEM((LH, TOK, 1), jnp.float32)
    hbm = pl.BlockSpec(memory_space=pl.ANY)
    return pl.pallas_call(
        layer_kernel,
        out_shape=jax.ShapeDtypeStruct((TOK, width), BF),
        in_specs=[SMEM, SMEM, hbm, hbm, hbm, hbm],
        out_specs=VMEM,
        scratch_shapes=[
            pltpu.VMEM((HK, PAD, HD), BF), pltpu.VMEM((TOK, width), BF),
            pltpu.VMEM((LH, TOK, 2 * HD), BF),
            pltpu.VMEM((2 * NX, width, width), BF),
            whole, whole, whole, hop, hop, hop, hop,
            pltpu.VMEM((HK, PIECE, HD), BF), pltpu.VMEM((NY - 1, GROUPS, PER, PIECE, HD), BF),
            pltpu.VMEM((TOK, PAD - OWN), jnp.float32), pltpu.VMEM((TOK, width), BF),
            pltpu.VMEM((LH, TOK, HD), jnp.float32), column, column,
            pltpu.VMEM((2 * NX, TOK, width), BF),
            halves, halves, halves, halves, fulls, fulls, pairs, pairs,
            dma((6, HK)), dma((6, HK)), dma((2, GROUPS)), dma((2, NZ // 2, GROUPS)), dma((2, NZ // 2, GROUPS)),
            dma((2, NZ)), dma((2, NY, GROUPS)), dma((2, NY)),
            dma((2, NZ // 2, GROUPS)), dma((2, NZ // 2, GROUPS)), dma((2, NZ // 2)), dma((2, NZ // 2)), dma((2, 2, NZ)),
            dma((HK,)), dma((2 * NX,)), dma, dma((6, 2 * PARTS)), dma((6, 2 * PARTS)), dma((2, PARTS)),
        ],
        compiler_params=pltpu.CompilerParams(
            collective_id=0, has_side_effects=True, vmem_limit_bytes=56 << 20
        ),
        name="layer",
    )(owners, pattern, q, k, v, w)


def body(query_rows, key_rows, value_rows, pattern, owners, out_weight):
    return layer(owners, pattern, query_rows, key_rows, value_rows, out_weight)


def solution(mesh):
    return jax.shard_map(
        body,
        mesh=mesh,
        in_specs=(
            P("seq", "head"),
            P("seq", "head"),
            P("seq", "head"),
            P("seq", None),
            P(),
            P("head", None),
        ),
        out_specs=P("seq", "head"),
        check_vma=False,
    )
```

```python
import math

import jax
import jax.numpy as jnp
from jax import lax
from jax.experimental import pallas as pl
from jax.experimental.pallas import tpu as pltpu
from jax.sharding import PartitionSpec as P

MESH = pl.DeviceIdType.MESH
HD = 128
LH = 3
TOK = 320
REF = 256
REACH = 3
NZ = 8
NY = 4
NX = 4
HK = 2 * LH
PIECE = REF // NZ
OWN = 4 * REF
HALO = OWN + TOK
KEYS = HALO + 2 * REACH * TOK
PAD = -(-KEYS // 256) * 256
NEG = -1e30
TILE = 256
GROUPS = 1
PER = HK // GROUPS
PARTS = 2
PACE = (
    (("own", 2), ("spread",)),
    (("own", 3),),
    (("own", 4),),
    (("own", 5), ("here",), ("fixed", 0), ("on", 0)),
    (("on", 1), ("on", 2), ("on", 3), ("fixed", 1), ("query",), ("near", 0)),
    (("fixed", 2), ("on", 4)),
    (("on", 5), ("fixed", 3)),
    (("near", 1),),
    (("near", 2),),
    (("fixed_part",),),
)
VMEM = pl.BlockSpec(memory_space=pltpu.VMEM)
SMEM = pl.BlockSpec(memory_space=pltpu.SMEM)
BF = jnp.bfloat16


def layer_kernel(
    owners_ref, pattern_ref, q_hbm, k_hbm, v_hbm, w_hbm, out,
    kv, qb, q2, wb, mine, msend, mrecv, ps, pr, ss, sr, ysend, yr,
    scores, att, acc1, top1, total1, p, r1p, r1m, t2p, t2m, r2p, r2m, ty, ry,
    hs_sem, hr_sem, m_sem, p_sem, s_sem, x_sem, y_sem, ys_sem, a_sem, b_sem, fa_sem, fb_sem, f_sem,
    in_sem, w_sem, q_sem, mix_s, mix_r, c_sem,
):
    s = lax.axis_index("seq")
    head = lax.axis_index("head")
    x = head // 2
    side = lax.rem(head, 2)
    xn = lax.rem(x + 1, NX)
    xp = lax.rem(x + NX - 1, NX)
    xo = lax.rem(x + 2, NX)
    nxt = xn * 2 + side
    prv = xp * 2 + side
    pair = x * 2 + 1 - side
    width = LH * HD
    n = 2 * NZ * NY
    core = lax.rem(s, 2)
    z = lax.rem(s // 2, NZ)
    y = s // (2 * NZ)
    step = 1 - 2 * core
    pz = jnp.where(core == 0, z, NZ - 1 - z)
    py = jnp.where(core == 0, y, NY - 1 - y)
    right = lax.rem(s + 2, n)
    left = lax.rem(s - 2 + n, n)
    partner = s + step
    extra = lax.rem(s - step + n, n)

    def at(yy, zz):
        zz = lax.rem(zz + NZ, NZ)
        yy = lax.rem(yy + NY, NY)
        zz = jnp.where(core == 0, zz, NZ - 1 - zz)
        yy = jnp.where(core == 0, yy, NY - 1 - yy)
        return (yy * NZ + zz) * 2 + core

    far, near = NZ // 2, NZ // 2 - 1
    ahead = at(py, pz + 1)
    behind = at(py, pz - 1)

    loads = []
    for h in range(LH):
        for i, ref in enumerate((k_hbm, v_hbm)):
            loads.append(pltpu.make_async_copy(
                ref.at[:, h * HD : (h + 1) * HD], kv.at[2 * h + i, OWN:HALO], in_sem.at[2 * h + i]
            ))
            loads[-1].start()

    barrier = pltpu.get_barrier_semaphore()
    peers = [partner, right, left, extra]
    peers += [at(py, pz + d) for d in range(1, NZ)]
    peers += [at(py + d, pz) for d in range(1, NY)]
    for peer in peers:
        pl.semaphore_signal(barrier, inc=1, device_id={"seq": peer}, device_id_type=MESH)
    for peer in (nxt, prv, pair):
        pl.semaphore_signal(barrier, inc=1, device_id={"head": peer}, device_id_type=MESH)

    query_load = pltpu.make_async_copy(q_hbm, qb, q_sem)
    weight_loads = [
        pltpu.make_async_copy(w_hbm.at[:, b * width : (b + 1) * width], wb.at[b], w_sem.at[b])
        for b in range(2 * NX)
    ]
    if PAD > KEYS:
        kv[:, KEYS:PAD, :] = jnp.zeros((HK, PAD - KEYS, HD), BF)

    low = jnp.int32(n)
    high = jnp.int32(-1)
    for i in range(4):
        o = owners_ref[i]
        low = jnp.minimum(low, jnp.where(o == 0, n, o))
        high = jnp.maximum(high, jnp.where(o == n - 1, -1, o))
    wanted = jnp.where(core == 0, low, high)
    given = jnp.where(core == 0, high, low)
    keep = jnp.where(wanted == s, 1.0, 0.0).astype(BF)
    give = jnp.where(given == s, 1.0, 0.0).astype(BF)
    for hk in range(HK):
        loads[hk].wait()
        block = kv[hk, OWN : OWN + REF, :]
        mine[hk] = block * keep
        msend[hk] = block * give

    pl.semaphore_wait(barrier, len(peers) + 3)

    def remote(src, dst, send, recv, peer):
        return pltpu.make_async_remote_copy(
            src_ref=src, dst_ref=dst, send_sem=send, recv_sem=recv,
            device_id={"seq": peer}, device_id_type=MESH,
        )

    def planes(ref, g):
        return ref.at[PER * g : PER * g + PER]

    def swap(g):
        return remote(planes(msend, g), planes(mrecv, g), m_sem.at[0, g], m_sem.at[1, g], partner)

    def p_copy(j, g):
        return remote(ps.at[j, g], pr.at[j, g], p_sem.at[0, j, g], p_sem.at[1, j, g], ahead)

    def s_copy(j, g):
        return remote(ss.at[j, g], sr.at[j, g], s_sem.at[0, j, g], s_sem.at[1, j, g], behind)

    base = core * REF

    def piece(g, q):
        start = base + lax.rem(q + NZ, NZ) * PIECE
        return kv.at[PER * g : PER * g + PER, pl.ds(pl.multiple_of(start, PIECE), PIECE)]

    def mine_rows(g, q):
        start = lax.rem(q + NZ, NZ) * PIECE
        return mine[PER * g : PER * g + PER, pl.ds(pl.multiple_of(start, PIECE), PIECE), :]

    def fixed_rows(q):
        start = 2 * REF + base + lax.rem(q + NZ, NZ) * PIECE
        return kv.at[:, pl.ds(pl.multiple_of(start, PIECE), PIECE)]

    def fixed_copy(q):
        return remote(
            kv.at[:, OWN + q * PIECE : OWN + (q + 1) * PIECE], fixed_rows(q),
            x_sem.at[0, q], x_sem.at[1, 0], at(0, q),
        )

    def y_copy(d, g):
        return remote(planes(ysend, g), yr.at[d - 1, g], y_sem.at[0, d, g], y_sem.at[1, d, g], at(py + d, pz))

    def y_fixed(d):
        return remote(fixed_rows(pz), fixed_rows(pz), ys_sem.at[0, d], ys_sem.at[1, 0], at(py + d, pz))

    def around(j, g):
        part = piece(g, pz - j)
        return remote(part, part, a_sem.at[0, j, g], a_sem.at[1, j, g], ahead)

    def around_arrived(j, g):
        part = piece(g, pz - j - 1)
        remote(part, part, a_sem.at[0, j, g], a_sem.at[1, j, g], ahead).wait_recv()

    def back(j, g):
        part = piece(g, pz + j)
        return remote(part, part, b_sem.at[0, j, g], b_sem.at[1, j, g], behind)

    def back_arrived(j, g):
        part = piece(g, pz + j + 1)
        remote(part, part, b_sem.at[0, j, g], b_sem.at[1, j, g], behind).wait_recv()

    def fixed_around(j):
        part = fixed_rows(pz - j)
        return remote(part, part, fa_sem.at[0, j], fa_sem.at[1, j], ahead)

    def fixed_back(j):
        part = fixed_rows(pz + j)
        return remote(part, part, fb_sem.at[0, j], fb_sem.at[1, j], behind)

    def fixed_start(j):
        if j > 0:
            part = fixed_rows(pz - j)
            remote(part, part, fa_sem.at[0, j - 1], fa_sem.at[1, j - 1], ahead).wait_recv()
        fixed_around(j).start()
        share(1, -j).start()
        if j <= near and j > 0:
            part = fixed_rows(pz + j)
            remote(part, part, fb_sem.at[0, j - 1], fb_sem.at[1, j - 1], behind).wait_recv()
            share(1, j).start()
        if j < near:
            fixed_back(j).start()

    def fixed_finish():
        part = fixed_rows(pz - far)
        remote(part, part, fa_sem.at[0, far - 1], fa_sem.at[1, far - 1], ahead).wait_recv()
        share(1, -far).start()

    def fixed_spread():
        @pl.when(py == 0)
        def _():
            @pl.when(pz > 0)
            def _():
                part = fixed_rows(pz)
                remote(part, part, x_sem.at[0, 0], x_sem.at[1, 0], ahead).wait_recv()

            for d in range(1, NY):
                y_fixed(d).start()

    def fixed_here():
        @pl.when(py > 0)
        def _():
            part = fixed_rows(pz)
            remote(part, part, ys_sem.at[0, 0], ys_sem.at[1, 0], ahead).wait_recv()

    def share(kind, off):
        start = (2 * kind + core) * REF + lax.rem(pz + off + NZ, NZ) * PIECE
        part = kv.at[:, pl.ds(pl.multiple_of(start, PIECE), PIECE)]
        return remote(part, part, f_sem.at[0, kind, off + far], f_sem.at[1, kind, off + far], partner)

    def shared(kind):
        for off in range(-far, near + 1):
            start = (2 * kind + 1 - core) * REF + lax.rem(2 * NZ - 1 - pz + off, NZ) * PIECE
            part = kv.at[:, pl.ds(pl.multiple_of(start, PIECE), PIECE)]
            remote(
                part, part, f_sem.at[0, kind, off + far], f_sem.at[1, kind, off + far], partner
            ).wait_recv()

    def halo_rows(hk, col):
        return kv.at[hk, pl.ds(pl.multiple_of(HALO + col * TOK, 16), TOK)]

    def halo_copy(kind, src, hk, col, peer):
        return remote(src, halo_rows(hk, col), hs_sem.at[kind, hk], hr_sem.at[col, hk], peer)

    def own_rows(hk):
        return kv.at[hk, OWN:HALO]

    def halo_sends(hk):
        return (
            halo_copy(0, own_rows(hk), hk, 1, right),
            halo_copy(1, own_rows(hk), hk, 4, left),
            halo_copy(2, own_rows(hk), hk, 2 + core, partner),
        )

    def forwards(hk):
        return (
            halo_copy(5, halo_rows(hk, 4 - 3 * core), hk, 5 - 5 * core, extra),
            halo_copy(3, halo_rows(hk, 1), hk, 2 * core, partner),
            halo_copy(4, halo_rows(hk, 4), hk, 3 + 2 * core, partner),
        )

    def halo_wait(hk, col):
        halo_copy(0, own_rows(hk), hk, col, right).wait_recv()

    def halo_start(hk):
        for copy in halo_sends(hk):
            copy.start()

    def halo_forward(hk):
        halo_wait(hk, 1)
        halo_wait(hk, 4)
        for copy in forwards(hk):
            copy.start()

    position = lax.broadcasted_iota(jnp.int32, (1, PAD - OWN), 1) + OWN
    bias = jnp.where(position >= KEYS, NEG, 0.0)
    for col in range(2 * REACH):
        edge = HALO + col * TOK
        closed = jnp.where(pattern_ref[0, col] != 0, 0.0, NEG)
        bias = bias + jnp.where((position >= edge) & (position < edge + TOK), closed, 0.0)
    scale = HD ** -0.5 * math.log2(math.e)

    def segment(h, first, last, low=0, high=TOK):
        q = q2[h, low:high]
        peak = jnp.full((high - low, HD), NEG, jnp.float32)
        tiles = range(first, last, TILE)
        for row in tiles:
            keys = kv[2 * h, row : row + TILE, :]
            sc = lax.dot_general(
                q, jnp.concatenate([keys, keys], axis=1), (((1,), (1,)), ((), ())),
                preferred_element_type=jnp.float32,
            )
            if row + TILE > HALO:
                sc = sc + bias[:, row - OWN : row - OWN + TILE]
            scores[low:high, row - first : row - first + TILE] = sc
            peak = jnp.maximum(peak, jnp.maximum(sc[:, :HD], sc[:, HD:]))
        top = jnp.max(peak, axis=1, keepdims=True)
        total = jnp.zeros((high - low, HD), jnp.float32)
        acc = jnp.zeros((high - low, HD), jnp.float32)
        for row in tiles:
            w = jnp.exp2(scores[low:high, row - first : row - first + TILE] - top)
            total = total + (w[:, :HD] + w[:, HD:])
            acc = acc + jnp.dot(
                w.astype(BF), kv[2 * h + 1, row : row + TILE, :], preferred_element_type=jnp.float32
            )
        return top, jnp.sum(total, axis=1, keepdims=True), acc

    def scale_queries():
        query_load.wait()
        for h in range(LH):
            exact = qb[:, h * HD : (h + 1) * HD].astype(jnp.float32) * scale
            upper = exact.astype(BF)
            q2[h, :, :HD] = upper
            q2[h, :, HD:] = (exact - upper.astype(jnp.float32)).astype(BF)

    def near_part(h):
        for col in range(2 * REACH):
            if col not in (1, 4):
                halo_wait(2 * h, col)
                halo_wait(2 * h + 1, col)
        top, total, acc = segment(h, OWN, PAD)
        top1[h] = top
        total1[h] = total
        acc1[h] = acc

    def joined(h, first, last, low=0, high=TOK):
        top, total, acc = segment(h, first, last, low, high)
        before = top1[h, low:high]
        best = jnp.maximum(top, before)
        new = jnp.exp2(top - best)
        old = jnp.exp2(before - best)
        return best, total * new + total1[h, low:high] * old, acc * new + acc1[h, low:high] * old

    def fixed_part():
        fixed_finish()
        shared(1)
        for h in range(LH):
            best, total, acc = joined(h, 2 * REF, OWN)
            top1[h] = best
            total1[h] = total
            acc1[h] = acc

    def last_part(low, high):
        for h in range(LH):
            best, total, acc = joined(h, 0, 2 * REF, low, high)
            att[low:high, h * HD : (h + 1) * HD] = (acc / total).astype(BF)

    source = (pz == 0) & (py == 0)
    heads = range(LH)
    groups = range(GROUPS)
    step_actions = {
        "own": halo_start, "on": halo_forward, "near": near_part, "spread": fixed_spread,
        "here": fixed_here, "fixed": fixed_start, "fixed_part": fixed_part, "query": scale_queries,
    }
    for g in groups:
        swap(g).start()

    @pl.when(source)
    def _():
        for q in range(1, NZ):
            fixed_copy(q).start()
        fixed_rows(0)[...] = kv[:, OWN : OWN + PIECE, :]

    halo_start(0)
    halo_start(1)
    query_load.start()
    for load in weight_loads:
        load.start()
    for j in range(far):
        for g in groups:
            if j == 0:
                swap(g).wait_recv()
                mine[PER * g : PER * g + PER] = mine[PER * g : PER * g + PER] + mrecv[PER * g : PER * g + PER]
                ps[0, g] = mine_rows(g, pz + far)
                p_copy(0, g).start()
                if near > 0:
                    ss[0, g] = mine_rows(g, pz - near)
                    s_copy(0, g).start()
            else:
                p_copy(j - 1, g).wait_recv()
                ps[j, g] = mine_rows(g, pz + far - j) + pr[j - 1, g]
                p_copy(j, g).start()
                if j < near:
                    s_copy(j - 1, g).wait_recv()
                    ss[j, g] = mine_rows(g, pz - near + j) + sr[j - 1, g]
                    s_copy(j, g).start()
        for action in PACE[j]:
            step_actions[action[0]](*action[1:])
    for g in groups:
        total = mine_rows(g, pz)
        if near > 0:
            s_copy(near - 1, g).wait_recv()
            total = total + sr[near - 1, g]
        p_copy(far - 1, g).wait_recv()
        ysend[PER * g : PER * g + PER] = total + pr[far - 1, g]
        for d in range(1, NY):
            y_copy(d, g).start()
    for action in PACE[far]:
        step_actions[action[0]](*action[1:])
    for g in groups:
        total = ysend[PER * g : PER * g + PER]
        for d in range(1, NY):
            y_copy(d, g).wait_recv()
            total = total + yr[d - 1, g]
        piece(g, pz)[...] = total
        around(0, g).start()
        if near > 0:
            back(0, g).start()
        share(0, 0).start()
    for action in PACE[far + 1]:
        step_actions[action[0]](*action[1:])
    for j in range(1, far):
        for g in groups:
            around_arrived(j - 1, g)
            around(j, g).start()
            share(0, -j).start()
            if j <= near:
                back_arrived(j - 1, g)
                share(0, j).start()
            if j < near:
                back(j, g).start()
        for action in PACE[far + 1 + j]:
            step_actions[action[0]](*action[1:])
    for g in groups:
        around_arrived(far - 1, g)
        share(0, -far).start()
    for action in PACE[2 * far + 1]:
        step_actions[action[0]](*action[1:])
    shared(0)
    for load in weight_loads:
        load.wait()

    def project(b, low=0, high=TOK):
        p[b, low:high] = jnp.dot(
            att[low:high], wb[b], preferred_element_type=jnp.float32
        ).astype(BF)

    def head_copy(kind, i, src, dst, peer):
        return pltpu.make_async_remote_copy(
            src_ref=src, dst_ref=dst, send_sem=mix_s.at[kind, i], recv_sem=mix_r.at[kind, i],
            device_id={"head": peer}, device_id_type=MESH,
        )

    def cross(c):
        return pltpu.make_async_remote_copy(
            src_ref=ty.at[c], dst_ref=ry.at[c], send_sem=c_sem.at[0, c], recv_sem=c_sem.at[1, c],
            device_id={"head": pair}, device_id_type=MESH,
        )

    part = TOK // PARTS
    half = part // 2
    items = [(which, c) for which in (1 - side, side) for c in range(PARTS)]
    rows = [(slice(c * part, c * part + half), slice(c * part + half, (c + 1) * part)) for c in range(PARTS)]
    first, direct, second = [], [], []
    for i, (which, c) in enumerate(items):
        upper, lower = rows[c]
        first.append((
            head_copy(0, i, p.at[xo * 2 + which, upper], r1p.at[i], nxt),
            head_copy(1, i, p.at[xo * 2 + which, lower], r1m.at[i], prv),
        ))
        direct.append((
            head_copy(2, i, p.at[xn * 2 + which, lower], r2p.at[i, half:], nxt),
            head_copy(3, i, p.at[xp * 2 + which, upper], r2m.at[i, :half], prv),
        ))
        second.append((
            head_copy(4, i, t2p.at[i], r2p.at[i, :half], nxt),
            head_copy(5, i, t2m.at[i], r2m.at[i, half:], prv),
        ))

    def pass_on(i):
        which, c = items[i]
        upper, lower = rows[c]
        first[i][0].wait_recv()
        t2p[i] = p[xn * 2 + which, upper] + r1p[i]
        second[i][0].start()
        first[i][1].wait_recv()
        t2m[i] = p[xp * 2 + which, lower] + r1m[i]
        second[i][1].start()

    def collect(i):
        which, c = items[i]
        for copy in direct[i] + second[i]:
            copy.wait_recv()
        return (
            p[x * 2 + which, c * part : (c + 1) * part].astype(jnp.float32)
            + r2p[i].astype(jnp.float32)
            + r2m[i].astype(jnp.float32)
        )

    def begin(copies):
        for copy in copies:
            copy.start()

    other = 1 - side
    for c in range(PARTS):
        span = (c * part, (c + 1) * part)
        last_part(*span)
        project(xo * 2 + other, *span)
        begin(first[c])
        if c > 0:
            pass_on(c - 1)
        project(xn * 2 + other, *span)
        project(xp * 2 + other, *span)
        begin(direct[c])
    project(x * 2 + other)
    project(xo * 2 + side)
    for i in range(PARTS, 2 * PARTS):
        begin(first[i])
    pass_on(PARTS - 1)
    ty[0] = collect(0).astype(BF)
    cross(0).start()
    project(xn * 2 + side)
    project(xp * 2 + side)
    for i in range(PARTS, 2 * PARTS):
        begin(direct[i])
    for c in range(1, PARTS):
        ty[c] = collect(c).astype(BF)
        cross(c).start()
    project(x * 2 + side)
    for i in range(PARTS, 2 * PARTS):
        pass_on(i)
    for kind in range(2):
        for off in range(-far, near + 1):
            share(kind, off).wait_send()
    for g in groups:
        swap(g).wait_send()
        for j in range(far):
            p_copy(j, g).wait_send()
            around(j, g).wait_send()
        for j in range(near):
            s_copy(j, g).wait_send()
            back(j, g).wait_send()
        for d in range(1, NY):
            y_copy(d, g).wait_send()
    for j in range(far):
        fixed_around(j).wait_send()
    for j in range(near):
        fixed_back(j).wait_send()
    for hk in range(HK):
        for copy in halo_sends(hk) + forwards(hk):
            copy.wait_send()

    @pl.when(py == 0)
    def _():
        for d in range(1, NY):
            y_fixed(d).wait_send()

    @pl.when(source)
    def _():
        for q in range(1, NZ):
            fixed_copy(q).wait_send()
    for c in range(PARTS):
        total = collect(PARTS + c)
        cross(c).wait_recv()
        out[c * part : (c + 1) * part, :] = (total + ry[c].astype(jnp.float32)).astype(BF)

    for i in range(2 * PARTS):
        for copy in first[i] + direct[i] + second[i]:
            copy.wait_send()
    for c in range(PARTS):
        cross(c).wait_send()


def layer(owners, pattern, q, k, v, w):
    dma = pltpu.SemaphoreType.DMA
    width = LH * HD
    whole = pltpu.VMEM((HK, REF, HD), BF)
    hop = pltpu.VMEM((NZ // 2, GROUPS, PER, PIECE, HD), BF)
    part = TOK // PARTS
    halves = pltpu.VMEM((2 * PARTS, part // 2, width), BF)
    fulls = pltpu.VMEM((2 * PARTS, part, width), BF)
    pairs = pltpu.VMEM((PARTS, part, width), BF)
    column = pltpu.VMEM((LH, TOK, 1), jnp.float32)
    hbm = pl.BlockSpec(memory_space=pl.ANY)
    return pl.pallas_call(
        layer_kernel,
        out_shape=jax.ShapeDtypeStruct((TOK, width), BF),
        in_specs=[SMEM, SMEM, hbm, hbm, hbm, hbm],
        out_specs=VMEM,
        scratch_shapes=[
            pltpu.VMEM((HK, PAD, HD), BF), pltpu.VMEM((TOK, width), BF),
            pltpu.VMEM((LH, TOK, 2 * HD), BF),
            pltpu.VMEM((2 * NX, width, width), BF),
            whole, whole, whole, hop, hop, hop, hop,
            pltpu.VMEM((HK, PIECE, HD), BF), pltpu.VMEM((NY - 1, GROUPS, PER, PIECE, HD), BF),
            pltpu.VMEM((TOK, PAD - OWN), jnp.float32), pltpu.VMEM((TOK, width), BF),
            pltpu.VMEM((LH, TOK, HD), jnp.float32), column, column,
            pltpu.VMEM((2 * NX, TOK, width), BF),
            halves, halves, halves, halves, fulls, fulls, pairs, pairs,
            dma((6, HK)), dma((6, HK)), dma((2, GROUPS)), dma((2, NZ // 2, GROUPS)), dma((2, NZ // 2, GROUPS)),
            dma((2, NZ)), dma((2, NY, GROUPS)), dma((2, NY)),
            dma((2, NZ // 2, GROUPS)), dma((2, NZ // 2, GROUPS)), dma((2, NZ // 2)), dma((2, NZ // 2)), dma((2, 2, NZ)),
            dma((HK,)), dma((2 * NX,)), dma, dma((6, 2 * PARTS)), dma((6, 2 * PARTS)), dma((2, PARTS)),
        ],
        compiler_params=pltpu.CompilerParams(
            collective_id=0, has_side_effects=True, vmem_limit_bytes=56 << 20
        ),
        name="layer",
    )(owners, pattern, q, k, v, w)


def body(query_rows, key_rows, value_rows, pattern, owners, out_weight):
    return layer(owners, pattern, query_rows, key_rows, value_rows, out_weight)


def solution(mesh):
    return jax.shard_map(
        body,
        mesh=mesh,
        in_specs=(
            P("seq", "head"),
            P("seq", "head"),
            P("seq", "head"),
            P("seq", None),
            P(),
            P("head", None),
        ),
        out_specs=P("seq", "head"),
        check_vma=False,
    )
```

```python
import math

import jax
import jax.numpy as jnp
from jax import lax
from jax.experimental import pallas as pl
from jax.experimental.pallas import tpu as pltpu
from jax.sharding import PartitionSpec as P

MESH = pl.DeviceIdType.MESH
HD = 128
LH = 3
TOK = 320
REF = 256
REACH = 3
NZ = 8
NY = 4
NX = 4
HK = 2 * LH
PIECE = REF // NZ
OWN = 4 * REF
HALO = OWN + TOK
KEYS = HALO + 2 * REACH * TOK
PAD = -(-KEYS // 256) * 256
NEG = -1e30
TILE = 256
GROUPS = 1
PER = HK // GROUPS
PARTS = 2
PACE = (
    (("own", 2), ("spread",)),
    (("own", 3),),
    (("own", 4), ("here",), ("fixed", 0)),
    (("own", 5), ("fixed", 1), ("on", 0), ("on", 1)),
    (("fixed", 2), ("on", 2), ("on", 3), ("query",), ("near", 0)),
    (("fixed", 3), ("on", 4)),
    (("on", 5), ("near", 1)),
    (("near", 2), ("fixed_part",)),
    (),
    (),
)
VMEM = pl.BlockSpec(memory_space=pltpu.VMEM)
SMEM = pl.BlockSpec(memory_space=pltpu.SMEM)
BF = jnp.bfloat16


def layer_kernel(
    owners_ref, pattern_ref, q_hbm, k_hbm, v_hbm, w_hbm, out,
    kv, qb, q2, wb, mine, msend, mrecv, ps, pr, ss, sr, ysend, yr,
    scores, att, acc1, top1, total1, p, r1p, r1m, t2p, t2m, r2p, r2m, ty, ry,
    hs_sem, hr_sem, m_sem, p_sem, s_sem, x_sem, y_sem, ys_sem, a_sem, b_sem, fa_sem, fb_sem, f_sem,
    in_sem, w_sem, q_sem, mix_s, mix_r, c_sem,
):
    s = lax.axis_index("seq")
    head = lax.axis_index("head")
    x = head // 2
    side = lax.rem(head, 2)
    xn = lax.rem(x + 1, NX)
    xp = lax.rem(x + NX - 1, NX)
    xo = lax.rem(x + 2, NX)
    nxt = xn * 2 + side
    prv = xp * 2 + side
    pair = x * 2 + 1 - side
    width = LH * HD
    n = 2 * NZ * NY
    core = lax.rem(s, 2)
    z = lax.rem(s // 2, NZ)
    y = s // (2 * NZ)
    step = 1 - 2 * core
    pz = jnp.where(core == 0, z, NZ - 1 - z)
    py = jnp.where(core == 0, y, NY - 1 - y)
    right = lax.rem(s + 2, n)
    left = lax.rem(s - 2 + n, n)
    partner = s + step
    extra = lax.rem(s - step + n, n)

    def at(yy, zz):
        zz = lax.rem(zz + NZ, NZ)
        yy = lax.rem(yy + NY, NY)
        zz = jnp.where(core == 0, zz, NZ - 1 - zz)
        yy = jnp.where(core == 0, yy, NY - 1 - yy)
        return (yy * NZ + zz) * 2 + core

    far, near = NZ // 2, NZ // 2 - 1
    ahead = at(py, pz + 1)
    behind = at(py, pz - 1)

    loads = []
    for h in range(LH):
        for i, ref in enumerate((k_hbm, v_hbm)):
            loads.append(pltpu.make_async_copy(
                ref.at[:, h * HD : (h + 1) * HD], kv.at[2 * h + i, OWN:HALO], in_sem.at[2 * h + i]
            ))
            loads[-1].start()

    barrier = pltpu.get_barrier_semaphore()
    peers = [partner, right, left, extra]
    peers += [at(py, pz + d) for d in range(1, NZ)]
    peers += [at(py + d, pz) for d in range(1, NY)]
    for peer in peers:
        pl.semaphore_signal(barrier, inc=1, device_id={"seq": peer}, device_id_type=MESH)
    for peer in (nxt, prv, pair):
        pl.semaphore_signal(barrier, inc=1, device_id={"head": peer}, device_id_type=MESH)

    query_load = pltpu.make_async_copy(q_hbm, qb, q_sem)
    weight_loads = [
        pltpu.make_async_copy(w_hbm.at[:, b * width : (b + 1) * width], wb.at[b], w_sem.at[b])
        for b in range(2 * NX)
    ]
    if PAD > KEYS:
        kv[:, KEYS:PAD, :] = jnp.zeros((HK, PAD - KEYS, HD), BF)

    low = jnp.int32(n)
    high = jnp.int32(-1)
    for i in range(4):
        o = owners_ref[i]
        low = jnp.minimum(low, jnp.where(o == 0, n, o))
        high = jnp.maximum(high, jnp.where(o == n - 1, -1, o))
    wanted = jnp.where(core == 0, low, high)
    given = jnp.where(core == 0, high, low)
    keep = jnp.where(wanted == s, 1.0, 0.0).astype(BF)
    give = jnp.where(given == s, 1.0, 0.0).astype(BF)
    for hk in range(HK):
        loads[hk].wait()
        block = kv[hk, OWN : OWN + REF, :]
        mine[hk] = block * keep
        msend[hk] = block * give

    pl.semaphore_wait(barrier, len(peers) + 3)

    def remote(src, dst, send, recv, peer):
        return pltpu.make_async_remote_copy(
            src_ref=src, dst_ref=dst, send_sem=send, recv_sem=recv,
            device_id={"seq": peer}, device_id_type=MESH,
        )

    def planes(ref, g):
        return ref.at[PER * g : PER * g + PER]

    def swap(g):
        return remote(planes(msend, g), planes(mrecv, g), m_sem.at[0, g], m_sem.at[1, g], partner)

    def p_copy(j, g):
        return remote(ps.at[j, g], pr.at[j, g], p_sem.at[0, j, g], p_sem.at[1, j, g], ahead)

    def s_copy(j, g):
        return remote(ss.at[j, g], sr.at[j, g], s_sem.at[0, j, g], s_sem.at[1, j, g], behind)

    base = core * REF

    def piece(g, q):
        start = base + lax.rem(q + NZ, NZ) * PIECE
        return kv.at[PER * g : PER * g + PER, pl.ds(pl.multiple_of(start, PIECE), PIECE)]

    def mine_rows(g, q):
        start = lax.rem(q + NZ, NZ) * PIECE
        return mine[PER * g : PER * g + PER, pl.ds(pl.multiple_of(start, PIECE), PIECE), :]

    def fixed_rows(q):
        start = 2 * REF + base + lax.rem(q + NZ, NZ) * PIECE
        return kv.at[:, pl.ds(pl.multiple_of(start, PIECE), PIECE)]

    def fixed_copy(q):
        return remote(
            kv.at[:, OWN + q * PIECE : OWN + (q + 1) * PIECE], fixed_rows(q),
            x_sem.at[0, q], x_sem.at[1, 0], at(0, q),
        )

    def y_copy(d, g):
        return remote(planes(ysend, g), yr.at[d - 1, g], y_sem.at[0, d, g], y_sem.at[1, d, g], at(py + d, pz))

    def y_fixed(d):
        return remote(fixed_rows(pz), fixed_rows(pz), ys_sem.at[0, d], ys_sem.at[1, 0], at(py + d, pz))

    def around(j, g):
        part = piece(g, pz - j)
        return remote(part, part, a_sem.at[0, j, g], a_sem.at[1, j, g], ahead)

    def around_arrived(j, g):
        part = piece(g, pz - j - 1)
        remote(part, part, a_sem.at[0, j, g], a_sem.at[1, j, g], ahead).wait_recv()

    def back(j, g):
        part = piece(g, pz + j)
        return remote(part, part, b_sem.at[0, j, g], b_sem.at[1, j, g], behind)

    def back_arrived(j, g):
        part = piece(g, pz + j + 1)
        remote(part, part, b_sem.at[0, j, g], b_sem.at[1, j, g], behind).wait_recv()

    def fixed_around(j):
        part = fixed_rows(pz - j)
        return remote(part, part, fa_sem.at[0, j], fa_sem.at[1, j], ahead)

    def fixed_back(j):
        part = fixed_rows(pz + j)
        return remote(part, part, fb_sem.at[0, j], fb_sem.at[1, j], behind)

    def fixed_start(j):
        if j > 0:
            part = fixed_rows(pz - j)
            remote(part, part, fa_sem.at[0, j - 1], fa_sem.at[1, j - 1], ahead).wait_recv()
        fixed_around(j).start()
        share(1, -j).start()
        if j <= near and j > 0:
            part = fixed_rows(pz + j)
            remote(part, part, fb_sem.at[0, j - 1], fb_sem.at[1, j - 1], behind).wait_recv()
            share(1, j).start()
        if j < near:
            fixed_back(j).start()

    def fixed_finish():
        part = fixed_rows(pz - far)
        remote(part, part, fa_sem.at[0, far - 1], fa_sem.at[1, far - 1], ahead).wait_recv()
        share(1, -far).start()

    def fixed_spread():
        @pl.when(py == 0)
        def _():
            @pl.when(pz > 0)
            def _():
                part = fixed_rows(pz)
                remote(part, part, x_sem.at[0, 0], x_sem.at[1, 0], ahead).wait_recv()

            for d in range(1, NY):
                y_fixed(d).start()

    def fixed_here():
        @pl.when(py > 0)
        def _():
            part = fixed_rows(pz)
            remote(part, part, ys_sem.at[0, 0], ys_sem.at[1, 0], ahead).wait_recv()

    def share(kind, off):
        start = (2 * kind + core) * REF + lax.rem(pz + off + NZ, NZ) * PIECE
        part = kv.at[:, pl.ds(pl.multiple_of(start, PIECE), PIECE)]
        return remote(part, part, f_sem.at[0, kind, off + far], f_sem.at[1, kind, off + far], partner)

    def shared(kind):
        for off in range(-far, near + 1):
            start = (2 * kind + 1 - core) * REF + lax.rem(2 * NZ - 1 - pz + off, NZ) * PIECE
            part = kv.at[:, pl.ds(pl.multiple_of(start, PIECE), PIECE)]
            remote(
                part, part, f_sem.at[0, kind, off + far], f_sem.at[1, kind, off + far], partner
            ).wait_recv()

    def halo_rows(hk, col):
        return kv.at[hk, pl.ds(pl.multiple_of(HALO + col * TOK, 16), TOK)]

    def halo_copy(kind, src, hk, col, peer):
        return remote(src, halo_rows(hk, col), hs_sem.at[kind, hk], hr_sem.at[col, hk], peer)

    def own_rows(hk):
        return kv.at[hk, OWN:HALO]

    def halo_sends(hk):
        return (
            halo_copy(0, own_rows(hk), hk, 1, right),
            halo_copy(1, own_rows(hk), hk, 4, left),
            halo_copy(2, own_rows(hk), hk, 2 + core, partner),
        )

    def forwards(hk):
        return (
            halo_copy(5, halo_rows(hk, 4 - 3 * core), hk, 5 - 5 * core, extra),
            halo_copy(3, halo_rows(hk, 1), hk, 2 * core, partner),
            halo_copy(4, halo_rows(hk, 4), hk, 3 + 2 * core, partner),
        )

    def halo_wait(hk, col):
        halo_copy(0, own_rows(hk), hk, col, right).wait_recv()

    def halo_start(hk):
        for copy in halo_sends(hk):
            copy.start()

    def halo_forward(hk):
        halo_wait(hk, 1)
        halo_wait(hk, 4)
        for copy in forwards(hk):
            copy.start()

    position = lax.broadcasted_iota(jnp.int32, (1, PAD - OWN), 1) + OWN
    bias = jnp.where(position >= KEYS, NEG, 0.0)
    for col in range(2 * REACH):
        edge = HALO + col * TOK
        closed = jnp.where(pattern_ref[0, col] != 0, 0.0, NEG)
        bias = bias + jnp.where((position >= edge) & (position < edge + TOK), closed, 0.0)
    scale = HD ** -0.5 * math.log2(math.e)

    def segment(h, first, last, low=0, high=TOK):
        q = q2[h, low:high]
        peak = jnp.full((high - low, HD), NEG, jnp.float32)
        tiles = range(first, last, TILE)
        for row in tiles:
            keys = kv[2 * h, row : row + TILE, :]
            sc = lax.dot_general(
                q, jnp.concatenate([keys, keys], axis=1), (((1,), (1,)), ((), ())),
                preferred_element_type=jnp.float32,
            )
            if row + TILE > HALO:
                sc = sc + bias[:, row - OWN : row - OWN + TILE]
            scores[low:high, row - first : row - first + TILE] = sc
            peak = jnp.maximum(peak, jnp.maximum(sc[:, :HD], sc[:, HD:]))
        top = jnp.max(peak, axis=1, keepdims=True)
        total = jnp.zeros((high - low, HD), jnp.float32)
        acc = jnp.zeros((high - low, HD), jnp.float32)
        for row in tiles:
            w = jnp.exp2(scores[low:high, row - first : row - first + TILE] - top)
            total = total + (w[:, :HD] + w[:, HD:])
            acc = acc + jnp.dot(
                w.astype(BF), kv[2 * h + 1, row : row + TILE, :], preferred_element_type=jnp.float32
            )
        return top, jnp.sum(total, axis=1, keepdims=True), acc

    def scale_queries():
        query_load.wait()
        for h in range(LH):
            exact = qb[:, h * HD : (h + 1) * HD].astype(jnp.float32) * scale
            upper = exact.astype(BF)
            q2[h, :, :HD] = upper
            q2[h, :, HD:] = (exact - upper.astype(jnp.float32)).astype(BF)

    def near_part(h):
        for col in range(2 * REACH):
            if col not in (1, 4):
                halo_wait(2 * h, col)
                halo_wait(2 * h + 1, col)
        top, total, acc = segment(h, OWN, PAD)
        top1[h] = top
        total1[h] = total
        acc1[h] = acc

    def joined(h, first, last, low=0, high=TOK):
        top, total, acc = segment(h, first, last, low, high)
        before = top1[h, low:high]
        best = jnp.maximum(top, before)
        new = jnp.exp2(top - best)
        old = jnp.exp2(before - best)
        return best, total * new + total1[h, low:high] * old, acc * new + acc1[h, low:high] * old

    def fixed_part():
        fixed_finish()
        shared(1)
        for h in range(LH):
            best, total, acc = joined(h, 2 * REF, OWN)
            top1[h] = best
            total1[h] = total
            acc1[h] = acc

    def last_part(low, high):
        for h in range(LH):
            best, total, acc = joined(h, 0, 2 * REF, low, high)
            att[low:high, h * HD : (h + 1) * HD] = (acc / total).astype(BF)

    source = (pz == 0) & (py == 0)
    heads = range(LH)
    groups = range(GROUPS)
    step_actions = {
        "own": halo_start, "on": halo_forward, "near": near_part, "spread": fixed_spread,
        "here": fixed_here, "fixed": fixed_start, "fixed_part": fixed_part, "query": scale_queries,
    }
    for g in groups:
        swap(g).start()

    @pl.when(source)
    def _():
        for q in range(1, NZ):
            fixed_copy(q).start()
        fixed_rows(0)[...] = kv[:, OWN : OWN + PIECE, :]

    halo_start(0)
    halo_start(1)
    query_load.start()
    for load in weight_loads:
        load.start()
    for j in range(far):
        for g in groups:
            if j == 0:
                swap(g).wait_recv()
                mine[PER * g : PER * g + PER] = mine[PER * g : PER * g + PER] + mrecv[PER * g : PER * g + PER]
                ps[0, g] = mine_rows(g, pz + far)
                p_copy(0, g).start()
                if near > 0:
                    ss[0, g] = mine_rows(g, pz - near)
                    s_copy(0, g).start()
            else:
                p_copy(j - 1, g).wait_recv()
                ps[j, g] = mine_rows(g, pz + far - j) + pr[j - 1, g]
                p_copy(j, g).start()
                if j < near:
                    s_copy(j - 1, g).wait_recv()
                    ss[j, g] = mine_rows(g, pz - near + j) + sr[j - 1, g]
                    s_copy(j, g).start()
        for action in PACE[j]:
            step_actions[action[0]](*action[1:])
    for g in groups:
        total = mine_rows(g, pz)
        if near > 0:
            s_copy(near - 1, g).wait_recv()
            total = total + sr[near - 1, g]
        p_copy(far - 1, g).wait_recv()
        ysend[PER * g : PER * g + PER] = total + pr[far - 1, g]
        for d in range(1, NY):
            y_copy(d, g).start()
    for action in PACE[far]:
        step_actions[action[0]](*action[1:])
    for g in groups:
        total = ysend[PER * g : PER * g + PER]
        for d in range(1, NY):
            y_copy(d, g).wait_recv()
            total = total + yr[d - 1, g]
        piece(g, pz)[...] = total
        around(0, g).start()
        if near > 0:
            back(0, g).start()
        share(0, 0).start()
    for action in PACE[far + 1]:
        step_actions[action[0]](*action[1:])
    for j in range(1, far):
        for g in groups:
            around_arrived(j - 1, g)
            around(j, g).start()
            share(0, -j).start()
            if j <= near:
                back_arrived(j - 1, g)
                share(0, j).start()
            if j < near:
                back(j, g).start()
        for action in PACE[far + 1 + j]:
            step_actions[action[0]](*action[1:])
    for g in groups:
        around_arrived(far - 1, g)
        share(0, -far).start()
    for action in PACE[2 * far + 1]:
        step_actions[action[0]](*action[1:])
    shared(0)
    for load in weight_loads:
        load.wait()

    def project(b, low=0, high=TOK):
        p[b, low:high] = jnp.dot(
            att[low:high], wb[b], preferred_element_type=jnp.float32
        ).astype(BF)

    def head_copy(kind, i, src, dst, peer):
        return pltpu.make_async_remote_copy(
            src_ref=src, dst_ref=dst, send_sem=mix_s.at[kind, i], recv_sem=mix_r.at[kind, i],
            device_id={"head": peer}, device_id_type=MESH,
        )

    def cross(c):
        return pltpu.make_async_remote_copy(
            src_ref=ty.at[c], dst_ref=ry.at[c], send_sem=c_sem.at[0, c], recv_sem=c_sem.at[1, c],
            device_id={"head": pair}, device_id_type=MESH,
        )

    part = TOK // PARTS
    half = part // 2
    items = [(which, c) for which in (1 - side, side) for c in range(PARTS)]
    rows = [(slice(c * part, c * part + half), slice(c * part + half, (c + 1) * part)) for c in range(PARTS)]
    first, direct, second = [], [], []
    for i, (which, c) in enumerate(items):
        upper, lower = rows[c]
        first.append((
            head_copy(0, i, p.at[xo * 2 + which, upper], r1p.at[i], nxt),
            head_copy(1, i, p.at[xo * 2 + which, lower], r1m.at[i], prv),
        ))
        direct.append((
            head_copy(2, i, p.at[xn * 2 + which, lower], r2p.at[i, half:], nxt),
            head_copy(3, i, p.at[xp * 2 + which, upper], r2m.at[i, :half], prv),
        ))
        second.append((
            head_copy(4, i, t2p.at[i], r2p.at[i, :half], nxt),
            head_copy(5, i, t2m.at[i], r2m.at[i, half:], prv),
        ))

    def pass_on(i):
        which, c = items[i]
        upper, lower = rows[c]
        first[i][0].wait_recv()
        t2p[i] = p[xn * 2 + which, upper] + r1p[i]
        second[i][0].start()
        first[i][1].wait_recv()
        t2m[i] = p[xp * 2 + which, lower] + r1m[i]
        second[i][1].start()

    def collect(i):
        which, c = items[i]
        for copy in direct[i] + second[i]:
            copy.wait_recv()
        return (
            p[x * 2 + which, c * part : (c + 1) * part].astype(jnp.float32)
            + r2p[i].astype(jnp.float32)
            + r2m[i].astype(jnp.float32)
        )

    def begin(copies):
        for copy in copies:
            copy.start()

    other = 1 - side
    for c in range(PARTS):
        span = (c * part, (c + 1) * part)
        last_part(*span)
        project(xo * 2 + other, *span)
        begin(first[c])
        if c > 0:
            pass_on(c - 1)
        project(xn * 2 + other, *span)
        project(xp * 2 + other, *span)
        begin(direct[c])
    project(x * 2 + other)
    project(xo * 2 + side)
    for i in range(PARTS, 2 * PARTS):
        begin(first[i])
    pass_on(PARTS - 1)
    ty[0] = collect(0).astype(BF)
    cross(0).start()
    project(xn * 2 + side)
    project(xp * 2 + side)
    for i in range(PARTS, 2 * PARTS):
        begin(direct[i])
    for c in range(1, PARTS):
        ty[c] = collect(c).astype(BF)
        cross(c).start()
    project(x * 2 + side)
    for i in range(PARTS, 2 * PARTS):
        pass_on(i)
    for kind in range(2):
        for off in range(-far, near + 1):
            share(kind, off).wait_send()
    for g in groups:
        swap(g).wait_send()
        for j in range(far):
            p_copy(j, g).wait_send()
            around(j, g).wait_send()
        for j in range(near):
            s_copy(j, g).wait_send()
            back(j, g).wait_send()
        for d in range(1, NY):
            y_copy(d, g).wait_send()
    for j in range(far):
        fixed_around(j).wait_send()
    for j in range(near):
        fixed_back(j).wait_send()
    for hk in range(HK):
        for copy in halo_sends(hk) + forwards(hk):
            copy.wait_send()

    @pl.when(py == 0)
    def _():
        for d in range(1, NY):
            y_fixed(d).wait_send()

    @pl.when(source)
    def _():
        for q in range(1, NZ):
            fixed_copy(q).wait_send()
    for c in range(PARTS):
        total = collect(PARTS + c)
        cross(c).wait_recv()
        out[c * part : (c + 1) * part, :] = (total + ry[c].astype(jnp.float32)).astype(BF)

    for i in range(2 * PARTS):
        for copy in first[i] + direct[i] + second[i]:
            copy.wait_send()
    for c in range(PARTS):
        cross(c).wait_send()


def layer(owners, pattern, q, k, v, w):
    dma = pltpu.SemaphoreType.DMA
    width = LH * HD
    whole = pltpu.VMEM((HK, REF, HD), BF)
    hop = pltpu.VMEM((NZ // 2, GROUPS, PER, PIECE, HD), BF)
    part = TOK // PARTS
    halves = pltpu.VMEM((2 * PARTS, part // 2, width), BF)
    fulls = pltpu.VMEM((2 * PARTS, part, width), BF)
    pairs = pltpu.VMEM((PARTS, part, width), BF)
    column = pltpu.VMEM((LH, TOK, 1), jnp.float32)
    hbm = pl.BlockSpec(memory_space=pl.ANY)
    return pl.pallas_call(
        layer_kernel,
        out_shape=jax.ShapeDtypeStruct((TOK, width), BF),
        in_specs=[SMEM, SMEM, hbm, hbm, hbm, hbm],
        out_specs=VMEM,
        scratch_shapes=[
            pltpu.VMEM((HK, PAD, HD), BF), pltpu.VMEM((TOK, width), BF),
            pltpu.VMEM((LH, TOK, 2 * HD), BF),
            pltpu.VMEM((2 * NX, width, width), BF),
            whole, whole, whole, hop, hop, hop, hop,
            pltpu.VMEM((HK, PIECE, HD), BF), pltpu.VMEM((NY - 1, GROUPS, PER, PIECE, HD), BF),
            pltpu.VMEM((TOK, PAD - OWN), jnp.float32), pltpu.VMEM((TOK, width), BF),
            pltpu.VMEM((LH, TOK, HD), jnp.float32), column, column,
            pltpu.VMEM((2 * NX, TOK, width), BF),
            halves, halves, halves, halves, fulls, fulls, pairs, pairs,
            dma((6, HK)), dma((6, HK)), dma((2, GROUPS)), dma((2, NZ // 2, GROUPS)), dma((2, NZ // 2, GROUPS)),
            dma((2, NZ)), dma((2, NY, GROUPS)), dma((2, NY)),
            dma((2, NZ // 2, GROUPS)), dma((2, NZ // 2, GROUPS)), dma((2, NZ // 2)), dma((2, NZ // 2)), dma((2, 2, NZ)),
            dma((HK,)), dma((2 * NX,)), dma, dma((6, 2 * PARTS)), dma((6, 2 * PARTS)), dma((2, PARTS)),
        ],
        compiler_params=pltpu.CompilerParams(
            collective_id=0, has_side_effects=True, vmem_limit_bytes=56 << 20
        ),
        name="layer",
    )(owners, pattern, q, k, v, w)


def body(query_rows, key_rows, value_rows, pattern, owners, out_weight):
    return layer(owners, pattern, query_rows, key_rows, value_rows, out_weight)


def solution(mesh):
    return jax.shard_map(
        body,
        mesh=mesh,
        in_specs=(
            P("seq", "head"),
            P("seq", "head"),
            P("seq", "head"),
            P("seq", None),
            P(),
            P("head", None),
        ),
        out_specs=P("seq", "head"),
        check_vma=False,
    )
```
